32 devices in a mesh: dp: 8 (over y, x, core), seq: 4 (over z).
Axes of the slice: x: 2, y: 2, z: 4, core: 2. Of those that a mesh axis runs over, the one named last changes fastest.
Arguments:
- patches: bfloat16 [16, 1024, 1152], P('dp', 'seq'), may hold values from -6 to 6
- picture_ids: int32 [16, 1024], P('dp'), may hold values from 0 to 11, as said below
- valid_mask: int32 [16, 1024], P('dp'), may hold values from 0 to 1, as said below
- ln1_gain: bfloat16 [1152], P('dp'), may hold values from 0.5 to 1.5
- ln1_bias: bfloat16 [1152], P('dp'), may hold values from -1.1953125 to 1.1953125
- w_qkv: bfloat16 [1152, 3456], P('dp'), may hold values from -0.1875 to 0.1875
- bias_qv: bfloat16 [2, 1152], P(None, 'dp'), may hold values from -1.1953125 to 1.1953125
- w_out: bfloat16 [1152, 1152], P('dp'), may hold values from -0.75 to 0.75
- b_out: bfloat16 [1152], P('dp'), may hold values from -1.1953125 to 1.1953125
- ln2_gain: bfloat16 [1152], P('dp'), may hold values from 0.5 to 1.5
- ln2_bias: bfloat16 [1152], P('dp'), may hold values from -1.1953125 to 1.1953125
- w_fc1: bfloat16 [1152, 4304], P('dp'), may hold values from -0.1875 to 0.1875
- b_fc1: bfloat16 [4304], P('dp'), may hold values from -1.1953125 to 1.1953125
- w_fc2: bfloat16 [4304, 1152], P(None, 'dp'), may hold values from -0.09375 to 0.09375
- b_fc2: bfloat16 [1152], P('dp'), may hold values from -1.1953125 to 1.1953125
- cotangent: bfloat16 [16, 1024, 1152], P('dp', 'seq'), may hold values from -6 to 6
Outputs:
- layer_out: bfloat16 [16, 1024, 1152], P('dp', 'seq')
- grad_patches: bfloat16 [16, 1024, 1152], P('dp', 'seq')
- grad_ln1_gain: float32 [1152], P('dp')
- grad_ln1_bias: float32 [1152], P('dp')
- grad_w_qkv: float32 [1152, 3456], P('dp')
- grad_bias_qv: float32 [2, 1152], P(None, 'dp')
- grad_w_out: float32 [1152, 1152], P('dp')
- grad_b_out: float32 [1152], P('dp')
- grad_ln2_gain: float32 [1152], P('dp')
- grad_ln2_bias: float32 [1152], P('dp')
- grad_w_fc1: float32 [1152, 4304], P('dp')
- grad_b_fc1: float32 [4304], P('dp')
- grad_w_fc2: float32 [4304, 1152], P(None, 'dp')
- grad_b_fc2: float32 [1152], P('dp')
The draws below stay inside these ranges and needn't reach their ends.
Inputs may be any that keep to these rules, and one draw needn't show every extreme that they name: `picture_ids`: in each row the valid tokens form consecutive pictures of 100 to 512 tokens with ids 0, 1, 2 and so on in order; every row holds one picture of exactly 512 tokens; padding tokens follow the last picture and carry id 11. `valid_mask`: 1 on the tokens of pictures, 0 on the padding that ends a row.
All inputs are finite; a program needn't handle non-finite values.
Results may differ from the reference program's by a relative error of at most 0.017.
Values may be sent and summed in bfloat16 or wider, within the bound.
A program may use at most 256 MiB of HBM per device.

```python
import jax
import jax.numpy as jnp
from jax import lax

D = 1152
HEADS = 16
HD = 72
FF = 4304
ROW_LEN = 1024
PMIN = 100
PMAX = 512
ROWS = 16


def picture_layout(key):
    folded = jax.random.fold_in(key, 11)
    count = ROW_LEN // PMIN + 1
    first_key, second_key = jax.random.split(folded)
    lengths = jax.random.randint(first_key, (ROWS, count), PMIN, PMAX + 1)
    picked = jax.random.randint(second_key, (ROWS, 1), 0, 2)
    slots = jnp.arange(count)[None, :]
    lengths = jnp.where(slots == picked, PMAX, lengths)
    ends = jnp.cumsum(lengths, axis=1)
    filled = jnp.max(jnp.where(ends <= ROW_LEN, ends, 0), axis=1)
    positions = jnp.arange(ROW_LEN)
    ident = jnp.sum((ends[:, None, :] <= positions[None, :, None]).astype(jnp.int32), axis=2)
    living = (positions[None, :] < filled[:, None]).astype(jnp.int32)
    ident = jnp.where(living == 1, ident, count)
    return (ident.astype(jnp.int32), living.astype(jnp.int32))


def draw_picture_ids(key, part):
    return picture_layout(key)[0]


def draw_valid_mask(key, part):
    return picture_layout(key)[1]


def steps_of(rng, shape, cuts, low, top_value):
    factor_of = 1.0
    for dim, parts in cuts:
        heights = jax.random.uniform(jax.random.fold_in(jax.random.fold_in(rng, 6), dim), (parts,), jnp.float32, low / len(cuts), top_value / len(cuts))
        factor_of = factor_of * jnp.repeat(jnp.exp(heights), shape[dim] // parts).reshape((-1,) + (1,) * (len(shape) - 1 - dim))
    return factor_of


def scatter_about(key, extent, width, bound, cuts=(), kind=jnp.bfloat16):
    result = jax.random.normal(key, extent, jnp.float32) * width
    if len(cuts) > 0:
        result = steps_of(key, extent, cuts, -0.22, 0.18) * result
    return jnp.clip(result, min=-bound, max=bound).astype(kind)


def setup_inputs(seed: int = 0) -> dict:
    keys = jax.random.split(jax.random.key(seed), 17)
    patches = scatter_about(keys[0], (ROWS, ROW_LEN, D), 1.0, 6.0, ((0, 8), (1, 4)))
    picture_ids = draw_picture_ids(jax.random.fold_in(keys[16], 71), 0)
    valid_mask = draw_valid_mask(jax.random.fold_in(keys[16], 71), 0)
    ln1_gain = jnp.clip(1.0 + 0.1 * jax.random.normal(keys[3], (D,), jnp.float32), 0.5, 1.5).astype(jnp.bfloat16)
    ln1_bias = scatter_about(keys[4], (D,), 0.2, 1.1953125, ((0, 8),))
    w_qkv = scatter_about(keys[5], (D, 3 * D), D ** -0.5, 0.1875, ((0, 8),))
    bias_qv = scatter_about(keys[6], (2, D), 0.2, 1.1953125, ((1, 8),))
    w_out = scatter_about(keys[7], (D, D), (D // 16) ** -0.5, 0.75, ((0, 8),))
    b_out = scatter_about(keys[8], (D,), 0.2, 1.1953125, ((0, 8),))
    ln2_gain = jnp.clip(1.0 + 0.1 * jax.random.normal(keys[9], (D,), jnp.float32), 0.5, 1.5).astype(jnp.bfloat16)
    ln2_bias = scatter_about(keys[10], (D,), 0.2, 1.1953125, ((0, 8),))
    w_fc1 = scatter_about(keys[11], (D, FF), D ** -0.5, 0.1875, ((0, 8),))
    b_fc1 = scatter_about(keys[12], (FF,), 0.2, 1.1953125, ((0, 8),))
    w_fc2 = scatter_about(keys[13], (FF, D), FF ** -0.5, 0.09375, ((1, 8),))
    b_fc2 = scatter_about(keys[14], (D,), 0.2, 1.1953125, ((0, 8),))
    cotangent = scatter_about(keys[15], (ROWS, ROW_LEN, D), 1.0, 6.0, ((0, 8), (1, 4)))
    return {"patches": patches, "picture_ids": picture_ids, "valid_mask": valid_mask, "ln1_gain": ln1_gain, "ln1_bias": ln1_bias, "w_qkv": w_qkv, "bias_qv": bias_qv, "w_out": w_out, "b_out": b_out, "ln2_gain": ln2_gain, "ln2_bias": ln2_bias, "w_fc1": w_fc1, "b_fc1": b_fc1, "w_fc2": w_fc2, "b_fc2": b_fc2, "cotangent": cotangent}


@jax.custom_vjp
def low(v):
    return lax.optimization_barrier(v.astype(jnp.bfloat16)).astype(jnp.float32)

@jax.custom_vjp
def low_back(v):
    return v

def low_keep(v):
    return (low(v), None)

def low_pass(kept, grad):
    return (grad,)

def back_keep(v):
    return (v, None)

def back_low(kept, grad):
    return (low(grad),)
low.defvjp(low_keep, low_pass)
low_back.defvjp(back_keep, back_low)
epsilon = 1e-06
big_negative = -1e+30
highest = lax.Precision.HIGHEST

def layer_norm(values, scales, offset):
    center = values - lax.optimization_barrier(jnp.mean(values, axis=-1, keepdims=True))
    spread = lax.optimization_barrier(jnp.mean(center * center, axis=-1, keepdims=True))
    return center * lax.rsqrt(spread + epsilon) * scales + offset

def gelu_tanh(values):
    return 0.5 * values * (1.0 + jnp.tanh(0.7978845608028654 * (values + 0.044715 * values * values * values)))

def attend_group(projected, allowed):
    heads_first = jnp.transpose(projected, (3, 2, 0, 1, 4))
    scaling = HD ** (-0.5)

    def one_head(triple):
        scores = jnp.einsum('gqe,gke->gqk', triple[0], triple[1], precision=highest) * scaling
        scores = low_back(scores)
        scores = jnp.where(allowed, scores, big_negative)
        row_max = lax.optimization_barrier(jnp.max(scores, axis=-1, keepdims=True))
        exp_terms = jnp.exp(scores - row_max)
        attn_probs = low(exp_terms / lax.optimization_barrier(jnp.sum(exp_terms, axis=-1, keepdims=True)))
        return jnp.einsum('gqk,gke->gqe', attn_probs, triple[2], precision=highest)
    mixing = lax.map(jax.checkpoint(one_head), heads_first)
    return jnp.transpose(mixing, (1, 2, 0, 3))

def group_forward(group_x, group_ids, group_valid, params):
    ln1_gain, ln1_bias, w_qkv, bias_qv, w_out, b_out, ln2_gain, ln2_bias, w_fc1, b_fc1, w_fc2, b_fc2 = params
    group_count = group_x.shape[0]
    length = group_x.shape[1]
    normed = low(layer_norm(group_x, ln1_gain, ln1_bias))
    projected = jnp.einsum('gld,de->gle', normed, w_qkv, precision=highest)
    bias_full = jnp.concatenate([bias_qv[0], jnp.zeros_like(bias_qv[0]), bias_qv[1]])
    projected = low(low_back(projected + bias_full))
    projected = projected.reshape(group_count, length, 3, HEADS, HD)
    positions = jnp.arange(length)
    same_picture = (group_ids[:, :, None] == group_ids[:, None, :]) & (group_valid[:, None, :] == 1)
    allowed = same_picture | (positions[:, None] == positions[None, :])[None]
    attended = attend_group(projected, allowed).reshape(group_count, length, HEADS * HD)
    attended = low(low_back(attended))
    branch = low_back(jnp.einsum('gld,de->gle', attended, w_out, precision=highest) + b_out)
    middle = group_x + branch
    normed_two = low(layer_norm(middle, ln2_gain, ln2_bias))
    hidden = low_back(jnp.einsum('gld,df->glf', normed_two, w_fc1, precision=highest) + b_fc1)
    active = low(gelu_tanh(hidden))
    second = low_back(jnp.einsum('glf,fd->gld', active, w_fc2, precision=highest) + b_fc2)
    return middle + second

def forward(inputs, params, picture_ids, valid_mask):
    row_count, row_length, model_width = inputs.shape
    grouped = inputs.reshape(row_count // 2, 2, row_length, model_width)
    ids_grouped = picture_ids.reshape(row_count // 2, 2, row_length)
    valid_grouped = valid_mask.reshape(row_count // 2, 2, row_length)

    def run_group(pieces):
        return group_forward(pieces[0], pieces[1], pieces[2], params)
    outputs = lax.map(jax.checkpoint(run_group), (grouped, ids_grouped, valid_grouped))
    return outputs.reshape(row_count, row_length, model_width)

def reference(patches, picture_ids, valid_mask, ln1_gain, ln1_bias, w_qkv, bias_qv, w_out, b_out, ln2_gain, ln2_bias, w_fc1, b_fc1, w_fc2, b_fc2, cotangent):
    params = (ln1_gain.astype(jnp.float32), ln1_bias.astype(jnp.float32), w_qkv.astype(jnp.float32), bias_qv.astype(jnp.float32), w_out.astype(jnp.float32), b_out.astype(jnp.float32), ln2_gain.astype(jnp.float32), ln2_bias.astype(jnp.float32), w_fc1.astype(jnp.float32), b_fc1.astype(jnp.float32), w_fc2.astype(jnp.float32), b_fc2.astype(jnp.float32))

    def run_layer(inputs, weights):
        return forward(inputs, weights, picture_ids, valid_mask)
    layer_out, pullback = jax.vjp(run_layer, patches.astype(jnp.float32), params)
    grad_patches, grads = pullback(cotangent.astype(jnp.float32))
    grad_ln1_gain, grad_ln1_bias, grad_w_qkv, grad_bias_qv, grad_w_out, grad_b_out, grad_ln2_gain, grad_ln2_bias, grad_w_fc1, grad_b_fc1, grad_w_fc2, grad_b_fc2 = grads
    return (layer_out.astype(jnp.bfloat16), grad_patches.astype(jnp.bfloat16), grad_ln1_gain, grad_ln1_bias, grad_w_qkv, grad_bias_qv, grad_w_out, grad_b_out, grad_ln2_gain, grad_ln2_bias, grad_w_fc1, grad_b_fc1, grad_w_fc2, grad_b_fc2)
```

```python
import functools

import jax
import jax.numpy as jnp
from jax import lax
from jax.experimental import pallas as pl
from jax.experimental.pallas import tpu as pltpu
from jax.sharding import PartitionSpec as P

HEADS = 16
HD = 72


epsilon = 1e-06
big_negative = -1e30


def layer_norm(values, scales, offset):
    center = values - jnp.mean(values, axis=-1, keepdims=True)
    spread = jnp.mean(center * center, axis=-1, keepdims=True)
    return center * lax.rsqrt(spread + epsilon) * scales + offset


def gelu_tanh(values):
    return (
        0.5
        * values
        * (1.0 + jnp.tanh(0.7978845608028654 * (values + 0.044715 * values * values * values)))
    )


def contract_rows(left, right):
    return lax.dot_general(
        left, right, (((0,), (0,)), ((), ())), preferred_element_type=jnp.float32
    )


def contract_cols(left, right):
    return lax.dot_general(
        left, right, (((1,), (1,)), ((), ())), preferred_element_type=jnp.float32
    )


def gather_weights(
    ln1_gain, ln1_bias, w_qkv, bias_qv, w_out, b_out, ln2_gain, ln2_bias, w_fc1, b_fc1, w_fc2, b_fc2
):
    return (
        lax.all_gather(ln1_gain, "dp", axis=0, tiled=True),
        lax.all_gather(ln1_bias, "dp", axis=0, tiled=True),
        lax.all_gather(w_qkv, "dp", axis=0, tiled=True),
        lax.all_gather(bias_qv, "dp", axis=1, tiled=True),
        lax.all_gather(w_out, "dp", axis=0, tiled=True),
        lax.all_gather(b_out, "dp", axis=0, tiled=True),
        lax.all_gather(ln2_gain, "dp", axis=0, tiled=True),
        lax.all_gather(ln2_bias, "dp", axis=0, tiled=True),
        lax.all_gather(w_fc1, "dp", axis=0, tiled=True),
        lax.all_gather(b_fc1, "dp", axis=0, tiled=True),
        lax.all_gather(w_fc2, "dp", axis=1, tiled=True),
        lax.all_gather(b_fc2, "dp", axis=0, tiled=True),
    )


def block_scores(queries, key_vectors, picture_ids, valid_mask, first_row, block_rows):
    length = picture_ids.shape[1]
    query_block = lax.dynamic_slice_in_dim(queries, first_row, block_rows, 1)
    ids_block = lax.dynamic_slice_in_dim(picture_ids, first_row, block_rows, 1)
    same_picture = (ids_block[:, :, None] == picture_ids[:, None, :]) & (
        valid_mask[:, None, :] == 1
    )
    diagonal = (first_row + jnp.arange(block_rows))[:, None] == jnp.arange(length)[None, :]
    allowed = (same_picture | diagonal[None])[:, None]
    scaling = queries.shape[-1] ** (-0.5)
    scores = (
        jnp.einsum("rqhe,rkhe->rhqk", query_block, key_vectors, preferred_element_type=jnp.float32)
        * scaling
    )
    return (query_block, jnp.where(allowed, scores, big_negative))


def attention_forward(queries, key_vectors, value_vectors, picture_ids, valid_mask):
    row_count, length, head_count, head_size = queries.shape
    block_rows = min(512, length)

    def one_block(block_index):
        query_block, scores = block_scores(
            queries, key_vectors, picture_ids, valid_mask, block_index * block_rows, block_rows
        )
        row_max = jnp.max(scores, axis=-1, keepdims=True)
        exp_terms = jnp.exp(scores - row_max)
        totals = jnp.sum(exp_terms, axis=-1, keepdims=True)
        probs_low = (exp_terms / totals).astype(jnp.bfloat16)
        mixing = jnp.einsum(
            "rhqk,rkhe->rqhe", probs_low, value_vectors, preferred_element_type=jnp.float32
        )
        return (mixing.astype(jnp.bfloat16), (row_max + jnp.log(totals))[..., 0])

    outputs, log_sums = lax.map(one_block, jnp.arange(length // block_rows))
    outputs = jnp.moveaxis(outputs, 0, 1).reshape(row_count, length, head_count, head_size)
    log_sums = jnp.moveaxis(log_sums, 0, 2).reshape(row_count, head_count, length)
    return (outputs, log_sums)


def attention_backward(
    queries, key_vectors, value_vectors, log_sums, grad_heads, picture_ids, valid_mask
):
    row_count, length, head_count, head_size = queries.shape
    block_rows = min(512, length)
    scaling = head_size ** (-0.5)

    def one_block(running, block_index):
        grad_keys, grad_values = running
        first_row = block_index * block_rows
        query_block, scores = block_scores(
            queries, key_vectors, picture_ids, valid_mask, first_row, block_rows
        )
        lse_block = lax.dynamic_slice_in_dim(log_sums, first_row, block_rows, 2)
        attn_probs = jnp.exp(scores - lse_block[..., None])
        grad_block = lax.dynamic_slice_in_dim(grad_heads, first_row, block_rows, 1)
        grad_values = grad_values + jnp.einsum(
            "rhqk,rqhe->rkhe",
            attn_probs.astype(jnp.bfloat16),
            grad_block,
            preferred_element_type=jnp.float32,
        )
        grad_probs = jnp.einsum(
            "rqhe,rkhe->rhqk", grad_block, value_vectors, preferred_element_type=jnp.float32
        )
        inner = jnp.sum(attn_probs * grad_probs, axis=-1, keepdims=True)
        grad_scores = (attn_probs * (grad_probs - inner)).astype(jnp.bfloat16)
        grad_query = (
            jnp.einsum(
                "rhqk,rkhe->rqhe", grad_scores, key_vectors, preferred_element_type=jnp.float32
            )
            * scaling
        )
        grad_keys = (
            grad_keys
            + jnp.einsum(
                "rhqk,rqhe->rkhe", grad_scores, query_block, preferred_element_type=jnp.float32
            )
            * scaling
        )
        return ((grad_keys, grad_values), grad_query)

    zeros_start = jnp.zeros(queries.shape, jnp.float32)
    (grad_keys, grad_values), grad_queries = lax.scan(
        one_block, (zeros_start, zeros_start), jnp.arange(length // block_rows)
    )
    grad_queries = jnp.moveaxis(grad_queries, 0, 1).reshape(
        row_count, length, head_count, head_size
    )
    return (grad_queries, grad_keys, grad_values)


def forward_pass(patches, picture_ids, valid_mask, gathered):
    (
        ln1_gain,
        ln1_bias,
        w_qkv,
        bias_qv,
        w_out,
        b_out,
        ln2_gain,
        ln2_bias,
        w_fc1,
        b_fc1,
        w_fc2,
        b_fc2,
    ) = gathered
    row_count, local_len, model_width = patches.shape
    inputs = patches.astype(jnp.float32).reshape(row_count * local_len, model_width)
    normed = layer_norm(inputs, ln1_gain.astype(jnp.float32), ln1_bias.astype(jnp.float32)).astype(
        jnp.bfloat16
    )
    projected = jnp.dot(normed, w_qkv, preferred_element_type=jnp.float32)
    bias_full = jnp.concatenate([bias_qv[0], jnp.zeros_like(bias_qv[0]), bias_qv[1]]).astype(
        jnp.float32
    )
    projected = (
        (projected + bias_full).astype(jnp.bfloat16).reshape(row_count, local_len, 3, HEADS, HD)
    )
    by_heads = lax.all_to_all(projected, "seq", split_axis=3, concat_axis=1, tiled=True)
    queries = by_heads[:, :, 0]
    key_vectors = by_heads[:, :, 1]
    value_vectors = by_heads[:, :, 2]
    mixing, log_sums = attention_forward(
        queries, key_vectors, value_vectors, picture_ids, valid_mask
    )
    token_mixing = lax.all_to_all(mixing, "seq", split_axis=1, concat_axis=2, tiled=True)
    attended = token_mixing.reshape(row_count * local_len, model_width)
    middle = (
        inputs
        + jnp.dot(attended, w_out, preferred_element_type=jnp.float32)
        + b_out.astype(jnp.float32)
    )
    normed_two = layer_norm(
        middle, ln2_gain.astype(jnp.float32), ln2_bias.astype(jnp.float32)
    ).astype(jnp.bfloat16)
    hidden = jnp.dot(normed_two, w_fc1, preferred_element_type=jnp.float32) + b_fc1.astype(
        jnp.float32
    )
    active = gelu_tanh(hidden).astype(jnp.bfloat16)
    outputs = (
        middle
        + jnp.dot(active, w_fc2, preferred_element_type=jnp.float32)
        + b_fc2.astype(jnp.float32)
    )
    layer_out = outputs.astype(jnp.bfloat16).reshape(row_count, local_len, model_width)
    kept_values = (
        inputs,
        normed,
        queries,
        key_vectors,
        value_vectors,
        log_sums,
        attended,
        middle,
        normed_two,
        hidden,
        active,
    )
    return (layer_out, kept_values)


def backward_pass(cotangent, picture_ids, valid_mask, gathered, kept_values):
    (
        ln1_gain,
        ln1_bias,
        w_qkv,
        bias_qv,
        w_out,
        b_out,
        ln2_gain,
        ln2_bias,
        w_fc1,
        b_fc1,
        w_fc2,
        b_fc2,
    ) = gathered
    (
        inputs,
        normed,
        queries,
        key_vectors,
        value_vectors,
        log_sums,
        attended,
        middle,
        normed_two,
        hidden,
        active,
    ) = kept_values
    row_count, local_len, model_width = cotangent.shape
    grad_z = cotangent.reshape(row_count * local_len, model_width)
    grad_w_fc2 = contract_rows(active, grad_z)
    grad_b_fc2 = jnp.sum(grad_z.astype(jnp.float32), axis=0)
    grad_active = contract_cols(grad_z, w_fc2)
    grad_hidden = jax.vjp(gelu_tanh, hidden)[1](grad_active)[0].astype(jnp.bfloat16)
    grad_w_fc1 = contract_rows(normed_two, grad_hidden)
    grad_b_fc1 = jnp.sum(grad_hidden.astype(jnp.float32), axis=0)
    grad_normed_two = contract_cols(grad_hidden, w_fc1)
    norm_pull = jax.vjp(
        layer_norm, middle, ln2_gain.astype(jnp.float32), ln2_bias.astype(jnp.float32)
    )[1]
    grad_middle, grad_ln2_gain, grad_ln2_bias = norm_pull(grad_normed_two)
    grad_middle = grad_middle + grad_z.astype(jnp.float32)
    grad_branch = grad_middle.astype(jnp.bfloat16)
    grad_w_out = contract_rows(attended, grad_branch)
    grad_b_out = jnp.sum(grad_branch.astype(jnp.float32), axis=0)
    grad_attended = (
        contract_cols(grad_branch, w_out)
        .astype(jnp.bfloat16)
        .reshape(row_count, local_len, HEADS, HD)
    )
    grad_heads = lax.all_to_all(grad_attended, "seq", split_axis=2, concat_axis=1, tiled=True)
    grad_queries, grad_keys, grad_values = attention_backward(
        queries, key_vectors, value_vectors, log_sums, grad_heads, picture_ids, valid_mask
    )
    grad_proj = jnp.stack([grad_queries, grad_keys, grad_values], axis=2).astype(jnp.bfloat16)
    grad_tokens = lax.all_to_all(grad_proj, "seq", split_axis=1, concat_axis=3, tiled=True).reshape(
        row_count * local_len, 3 * model_width
    )
    grad_w_qkv = contract_rows(normed, grad_tokens)
    column_sums = jnp.sum(grad_tokens.astype(jnp.float32), axis=0)
    grad_bias_qv = jnp.stack([column_sums[:model_width], column_sums[2 * model_width :]])
    grad_normed = contract_cols(grad_tokens, w_qkv)
    first_pull = jax.vjp(
        layer_norm, inputs, ln1_gain.astype(jnp.float32), ln1_bias.astype(jnp.float32)
    )[1]
    grad_inputs, grad_ln1_gain, grad_ln1_bias = first_pull(grad_normed)
    grad_patches = (
        (grad_middle + grad_inputs).astype(jnp.bfloat16).reshape(row_count, local_len, model_width)
    )
    grads = (
        grad_ln1_gain,
        grad_ln1_bias,
        grad_w_qkv,
        grad_bias_qv,
        grad_w_out,
        grad_b_out,
        grad_ln2_gain,
        grad_ln2_bias,
        grad_w_fc1,
        grad_b_fc1,
        grad_w_fc2,
        grad_b_fc2,
    )
    return (grad_patches, grads)


def per_device(
    patches,
    picture_ids,
    valid_mask,
    ln1_gain,
    ln1_bias,
    w_qkv,
    bias_qv,
    w_out,
    b_out,
    ln2_gain,
    ln2_bias,
    w_fc1,
    b_fc1,
    w_fc2,
    b_fc2,
    cotangent,
):
    gathered = gather_weights(
        ln1_gain,
        ln1_bias,
        w_qkv,
        bias_qv,
        w_out,
        b_out,
        ln2_gain,
        ln2_bias,
        w_fc1,
        b_fc1,
        w_fc2,
        b_fc2,
    )
    layer_out, kept_values = forward_pass(patches, picture_ids, valid_mask, gathered)
    grad_patches, grads = backward_pass(cotangent, picture_ids, valid_mask, gathered, kept_values)
    (
        grad_ln1_gain,
        grad_ln1_bias,
        grad_w_qkv,
        grad_bias_qv,
        grad_w_out,
        grad_b_out,
        grad_ln2_gain,
        grad_ln2_bias,
        grad_w_fc1,
        grad_b_fc1,
        grad_w_fc2,
        grad_b_fc2,
    ) = grads
    owned = (
        lax.psum_scatter(
            grad_ln1_gain.astype(jnp.bfloat16), "dp", scatter_dimension=0, tiled=True
        ).astype(jnp.float32),
        lax.psum_scatter(
            grad_ln1_bias.astype(jnp.bfloat16), "dp", scatter_dimension=0, tiled=True
        ).astype(jnp.float32),
        lax.psum_scatter(
            grad_w_qkv.astype(jnp.bfloat16), "dp", scatter_dimension=0, tiled=True
        ).astype(jnp.float32),
        lax.psum_scatter(
            grad_bias_qv.astype(jnp.bfloat16), "dp", scatter_dimension=1, tiled=True
        ).astype(jnp.float32),
        lax.psum_scatter(
            grad_w_out.astype(jnp.bfloat16), "dp", scatter_dimension=0, tiled=True
        ).astype(jnp.float32),
        lax.psum_scatter(
            grad_b_out.astype(jnp.bfloat16), "dp", scatter_dimension=0, tiled=True
        ).astype(jnp.float32),
        lax.psum_scatter(
            grad_ln2_gain.astype(jnp.bfloat16), "dp", scatter_dimension=0, tiled=True
        ).astype(jnp.float32),
        lax.psum_scatter(
            grad_ln2_bias.astype(jnp.bfloat16), "dp", scatter_dimension=0, tiled=True
        ).astype(jnp.float32),
        lax.psum_scatter(
            grad_w_fc1.astype(jnp.bfloat16), "dp", scatter_dimension=0, tiled=True
        ).astype(jnp.float32),
        lax.psum_scatter(
            grad_b_fc1.astype(jnp.bfloat16), "dp", scatter_dimension=0, tiled=True
        ).astype(jnp.float32),
        lax.psum_scatter(
            grad_w_fc2.astype(jnp.bfloat16), "dp", scatter_dimension=1, tiled=True
        ).astype(jnp.float32),
        lax.psum_scatter(
            grad_b_fc2.astype(jnp.bfloat16), "dp", scatter_dimension=0, tiled=True
        ).astype(jnp.float32),
    )
    (
        part_ln1_gain,
        part_ln1_bias,
        part_w_qkv,
        part_bias_qv,
        part_w_out,
        part_b_out,
        part_ln2_gain,
        part_ln2_bias,
        part_w_fc1,
        part_b_fc1,
        part_w_fc2,
        part_b_fc2,
    ) = owned
    summed = (
        lax.psum(part_ln1_gain.astype(jnp.bfloat16), "seq").astype(jnp.float32),
        lax.psum(part_ln1_bias.astype(jnp.bfloat16), "seq").astype(jnp.float32),
        lax.psum(part_w_qkv.astype(jnp.bfloat16), "seq").astype(jnp.float32),
        lax.psum(part_bias_qv.astype(jnp.bfloat16), "seq").astype(jnp.float32),
        lax.psum(part_w_out.astype(jnp.bfloat16), "seq").astype(jnp.float32),
        lax.psum(part_b_out.astype(jnp.bfloat16), "seq").astype(jnp.float32),
        lax.psum(part_ln2_gain.astype(jnp.bfloat16), "seq").astype(jnp.float32),
        lax.psum(part_ln2_bias.astype(jnp.bfloat16), "seq").astype(jnp.float32),
        lax.psum(part_w_fc1.astype(jnp.bfloat16), "seq").astype(jnp.float32),
        lax.psum(part_b_fc1.astype(jnp.bfloat16), "seq").astype(jnp.float32),
        lax.psum(part_w_fc2.astype(jnp.bfloat16), "seq").astype(jnp.float32),
        lax.psum(part_b_fc2.astype(jnp.bfloat16), "seq").astype(jnp.float32),
    )
    (
        final_ln1_gain,
        final_ln1_bias,
        final_w_qkv,
        final_bias_qv,
        final_w_out,
        final_b_out,
        final_ln2_gain,
        final_ln2_bias,
        final_w_fc1,
        final_b_fc1,
        final_w_fc2,
        final_b_fc2,
    ) = summed
    return (
        layer_out,
        grad_patches,
        final_ln1_gain,
        final_ln1_bias,
        final_w_qkv,
        final_bias_qv,
        final_w_out,
        final_b_out,
        final_ln2_gain,
        final_ln2_bias,
        final_w_fc1,
        final_b_fc1,
        final_w_fc2,
        final_b_fc2,
    )


WIN = 256
ROWBLK = 64
LOG2E = 1.4426950408889634
ORDER = (0, 2, 4, 6, 1, 3, 5, 7)
bf16 = jnp.bfloat16
f32 = jnp.float32


def nn(a, b):
    return lax.dot_general(a, b, (((1,), (0,)), ((), ())), preferred_element_type=f32)


def nt(a, b):
    return lax.dot_general(a, b, (((1,), (1,)), ((), ())), preferred_element_type=f32)


def tn(a, b):
    return lax.dot_general(a, b, (((0,), (0,)), ((), ())), preferred_element_type=f32)


VM = pl.BlockSpec(memory_space=pltpu.VMEM)
ANY = pl.BlockSpec(memory_space=pl.ANY)


def sds(shape, dtype):
    return jax.ShapeDtypeStruct(shape, dtype)


def row_loop(total, body):
    @pl.loop(0, total // ROWBLK)
    def _(r):
        body(pl.ds(pl.multiple_of(r * ROWBLK, ROWBLK), ROWBLK))


def unit_copies(pieces, half, cols, dst, sem):
    d = lax.axis_index("dp")
    own, c0, xr, cx, yr, cy, da, db, cda, cdb = pieces
    six, seven = (da, cda) if half == 0 else (db, cdb)
    rows = own.shape[1]
    sources = (own, c0, xr, cx, yr, cy)
    copies = []
    for m in range(8):
        if m < 6:
            src = sources[m].at[half, :, cols]
        else:
            src = (six if m == 6 else seven).at[:, cols]
        where = pl.ds(pl.multiple_of(jnp.bitwise_xor(d, m) * rows, rows), rows)
        copies.append(pltpu.make_async_copy(src, dst.at[where, :], sem.at[m]))
    return copies


def norm_rows(v, gain, offset):
    center = v - jnp.mean(v, axis=-1, keepdims=True)
    spread = jnp.mean(center * center, axis=-1, keepdims=True)
    return center * lax.rsqrt(spread + epsilon) * gain + offset


def transpose_ordered(src, flipped, dst):
    d = lax.axis_index("dp")
    width = src.shape[1]
    part = width // 8

    @pl.loop(0, width // 128)
    def _(j):
        cols = pl.ds(pl.multiple_of(j * 128, 128), 128)
        flipped[cols, :] = src[:, cols].T

    for i, m in enumerate(ORDER):
        where = pl.ds(pl.multiple_of(jnp.bitwise_xor(d, m) * part, part), part)
        dst[i * part : (i + 1) * part, :] = flipped[where, :]


def kv_kernel(x_ref, vec_ref, *rest):
    pieces, (n_ref, kv_ref, w, sem) = rest[:10], rest[10:]
    width = x_ref.shape[1]
    copies = unit_copies(pieces, 1, pl.ds(0, 2 * width), w, sem)
    for c in copies:
        c.start()

    def body(rows):
        v = x_ref[rows, :].astype(f32)
        n_ref[rows, :] = norm_rows(v, vec_ref[0:1, 0:width], vec_ref[1:2, 0:width]).astype(bf16)

    row_loop(x_ref.shape[0], body)
    for c in copies:
        c.wait()

    @pl.loop(0, 2 * width // 256)
    def _(t):
        cols = pl.ds(pl.multiple_of(t * 256, 256), 256)
        kv_ref[:, cols] = (nn(n_ref[...], w[:, cols]) + vec_ref[8:9, cols]).astype(bf16)


def column_tiles(width, body):
    full = width // 256

    @pl.loop(0, full)
    def _(t):
        body(pl.ds(pl.multiple_of(t * 256, 256), 256))

    if width % 256:
        body(pl.ds(full * 256, width % 256))


def q_kernel(n_ref, vec_ref, *rest):
    pieces, (q_ref, nt_ref, w, flipped, sem) = rest[:10], rest[10:]
    width = n_ref.shape[1]
    copies = unit_copies(pieces, 0, pl.ds(0, width), w, sem)
    for c in copies:
        c.start()
    transpose_ordered(n_ref, flipped, nt_ref)
    for c in copies:
        c.wait()

    def body(cols):
        q_ref[:, cols] = (nn(n_ref[...], w[:, cols]) + vec_ref[2:3, cols]).astype(bf16)

    column_tiles(width, body)


def head_window(h, width):
    w0 = pl.multiple_of(jnp.minimum((h * HD) // 128, (width - WIN) // 128) * 128, 128)
    lane = lax.broadcasted_iota(jnp.int32, (1, WIN), 1)
    off = h * HD - w0
    return w0, (lane >= off) & (lane < off + HD)


def attention_forward_kernel(q_ref, ko_ref, kx_ref, qid_ref, kid_ref, att_ref, lse_ref, bias, acc, lse_cols):
    tokens, width = q_ref.shape
    scale = HD**-0.5 * LOG2E
    block = 256

    @pl.loop(0, tokens // ROWBLK)
    def _(r):
        rows = pl.ds(pl.multiple_of(r * ROWBLK, ROWBLK), ROWBLK)
        same = qid_ref[rows, 0:1] == kid_ref[0:1, :]
        col = lax.broadcasted_iota(jnp.int32, (ROWBLK, 2 * tokens), 1)
        row = lax.broadcasted_iota(jnp.int32, (ROWBLK, 2 * tokens), 0) + r * ROWBLK
        bias[rows, :] = jnp.where(same | (col == row), 0.0, big_negative)
        acc[rows, :] = jnp.zeros((ROWBLK, width), f32)
        lse_cols[rows, :] = jnp.zeros((ROWBLK, 128), f32)

    @pl.loop(0, HEADS)
    def _(h):
        w0, mask = head_window(h, width)
        win, winv = pl.ds(w0, WIN), pl.ds(w0 + width, WIN)
        zero = jnp.zeros((), bf16)
        ko, kx = jnp.where(mask, ko_ref[:, win], zero), jnp.where(mask, kx_ref[:, win], zero)
        vo, vx = jnp.where(mask, ko_ref[:, winv], zero), jnp.where(mask, kx_ref[:, winv], zero)
        lane = lax.broadcasted_iota(jnp.int32, (1, 128), 1)
        for qb in range(tokens // block):
            rows = pl.ds(qb * block, block)
            qw = q_ref[rows, win]
            so = nt(qw, ko) * scale + bias[rows, 0:tokens]
            sx = nt(qw, kx) * scale + bias[rows, tokens : 2 * tokens]
            m = jnp.maximum(jnp.max(so, axis=1, keepdims=True), jnp.max(sx, axis=1, keepdims=True))
            po, px = jnp.exp2(so - m), jnp.exp2(sx - m)
            total = jnp.sum(po, axis=1, keepdims=True) + jnp.sum(px, axis=1, keepdims=True)
            o = nn(po.astype(bf16), vo) + nn(px.astype(bf16), vx)
            acc[rows, win] += o * (1.0 / total)
            lse_cols[rows, :] = jnp.where(lane == h, m + jnp.log2(total), lse_cols[rows, :])

    def body(rows):
        att_ref[rows, :] = acc[rows, :].astype(bf16)

    row_loop(tokens, body)
    lse_ref[...] = lse_cols[...].T[:HEADS, :]


def attention_backward_kernel(near, q_ref, kv_ref, go_ref, lse_ref, del_ref, kid_ref, qid_ref, dqp_ref, dq_ref, dkv_ref, bias, dqa, dka):
    tokens, width = q_ref.shape
    scale, unit = HD**-0.5 * LOG2E, HD**-0.5

    @pl.loop(0, tokens // ROWBLK)
    def _(r):
        rows = pl.ds(pl.multiple_of(r * ROWBLK, ROWBLK), ROWBLK)
        allowed = kid_ref[rows, 0:1] == qid_ref[0:1, :]
        if near:
            col = lax.broadcasted_iota(jnp.int32, (ROWBLK, tokens), 1)
            row = lax.broadcasted_iota(jnp.int32, (ROWBLK, tokens), 0) + r * ROWBLK
            allowed = allowed | (col == row)
        bias[rows, :] = jnp.where(allowed, 0.0, big_negative)
        dka[rows, :] = jnp.zeros((ROWBLK, 2 * width), f32)
        dqa[rows, :] = dqp_ref[rows, :] if near else jnp.zeros((ROWBLK, width), f32)

    @pl.loop(0, HEADS)
    def _(h):
        w0, mask = head_window(h, width)
        win, winv = pl.ds(w0, WIN), pl.ds(w0 + width, WIN)
        zero = jnp.zeros((), bf16)
        qw = q_ref[:, win]
        qm, gm = jnp.where(mask, qw, zero), jnp.where(mask, go_ref[:, win], zero)
        lse, inner = lse_ref[pl.ds(h, 1), :], del_ref[pl.ds(h, 1), :]
        km, vw = jnp.where(mask, kv_ref[:, win], zero), kv_ref[:, winv]
        pt = jnp.exp2(nt(km, qw) * scale + bias[...] - lse)
        dka[:, winv] += nn(pt.astype(bf16), gm)
        ds = (pt * (nt(vw, gm) - inner)).astype(bf16)
        dka[:, win] += nn(ds, qm)
        dqa[:, win] += tn(ds, km)

    @pl.loop(0, tokens // ROWBLK)
    def _(r):
        rows = pl.ds(pl.multiple_of(r * ROWBLK, ROWBLK), ROWBLK)
        dq_ref[rows, :] = (dqa[rows, :] * unit).astype(bf16) if near else dqa[rows, :]
        dkv_ref[rows, 0:width] = (dka[rows, 0:width] * unit).astype(dkv_ref.dtype)
        dkv_ref[rows, width : 2 * width] = dka[rows, width : 2 * width].astype(dkv_ref.dtype)


def middle_kernel(att_ref, x_ref, cot_ref, vec_ref, *rest):
    pieces, (mid_ref, n2_ref, n2t_ref, cott_ref, attt_ref, w, flipped, sem) = rest[:10], rest[10:]
    tokens, width = x_ref.shape
    copies = unit_copies(pieces, 0, pl.ds(width, width), w, sem)
    for c in copies:
        c.start()
    transpose_ordered(cot_ref, flipped, cott_ref)
    transpose_ordered(att_ref, flipped, attt_ref)
    for c in copies:
        c.wait()

    def body(cols):
        mid_ref[:, cols] = nn(att_ref[...], w[:, cols]) + vec_ref[4:5, cols] + x_ref[:, cols].astype(f32)

    column_tiles(width, body)

    def norm(rows):
        n2_ref[rows, :] = norm_rows(mid_ref[rows, :], vec_ref[5:6, 0:width], vec_ref[6:7, 0:width]).astype(bf16)

    row_loop(tokens, norm)
    transpose_ordered(n2_ref, flipped, n2t_ref)


def mlp_kernel(first, last, n2_ref, cot_ref, n2t_ref, cott_ref, b1_ref, vec_ref, outp_ref, gnp_ref, *rest):
    pieces = rest[:10]
    out_ref, gn_ref, keep_ref, send_ref, gb1_ref, wbuf, acc, gacc, sem = rest[10:]
    t, steps = pl.program_id(0), pl.num_programs(0)
    width = n2_ref.shape[1]
    tile = wbuf.shape[-1]
    half = width // 2

    def copies(step, slot):
        cols = pl.ds(pl.multiple_of(step * tile, tile), tile)
        return unit_copies(pieces, 0, cols, wbuf.at[slot, 0], sem.at[slot, 0]) + unit_copies(
            pieces, 1, cols, wbuf.at[slot, 1], sem.at[slot, 1]
        )

    slot = lax.rem(t, 2)

    @pl.when(t == 0)
    def _():
        for c in copies(0, 0):
            c.start()

        def init(rows):
            acc[rows, :] = outp_ref[rows, :] + vec_ref[7:8, 0:width] if first else outp_ref[rows, :]
            gacc[rows, :] = jnp.zeros((ROWBLK, width), f32) if first else gnp_ref[rows, :]

        row_loop(n2_ref.shape[0], init)

    @pl.when(t + 1 < steps)
    def _():
        for c in copies(t + 1, 1 - slot):
            c.start()

    for c in copies(t, slot):
        c.wait()
    w1, w2 = wbuf[slot, 0], wbuf[slot, 1]
    u = nn(n2_ref[...], w1) + b1_ref[...]
    c0 = 0.7978845608028654
    th = jnp.tanh(c0 * (u + 0.044715 * u * u * u))
    active = (0.5 * u * (1.0 + th)).astype(bf16)
    slope = 0.5 * (1.0 + th) + 0.5 * u * (1.0 - th * th) * (c0 * (1.0 + 3 * 0.044715 * u * u))
    gh = (nn(cot_ref[...], w2) * slope).astype(bf16)
    gb1_ref[...] = jnp.sum(gh.astype(f32), axis=0, keepdims=True)
    acc[...] += nt(active, w2)
    gacc[...] += nt(gh, w1)
    g1 = nn(n2t_ref[...], gh).astype(bf16)
    keep_ref[0], send_ref[0] = g1[:half], g1[half:]
    g2 = nn(cott_ref[...], active).astype(bf16)
    keep_ref[1], send_ref[1] = g2[:half], g2[half:]

    @pl.when(t == steps - 1)
    def _():
        out_ref[...] = acc[...].astype(out_ref.dtype)
        gn_ref[...] = gacc[...]


def mlp_call(first, last, n2, cot, n2t, cott, b1, vec, outp, gnp, pieces):
    tokens, width = n2.shape
    cols, tile = pieces[0].shape[2], 256
    const = lambda a: pl.BlockSpec(a.shape, lambda t: (0,) * a.ndim, pipeline_mode=pl.Buffered(1))
    out_type = bf16 if last else f32
    return pl.pallas_call(
        functools.partial(mlp_kernel, first, last),
        grid=(cols // tile,),
        in_specs=[const(n2), const(cot), const(n2t), const(cott), pl.BlockSpec((1, tile), lambda t: (0, t)), const(vec),
                  const(outp), const(gnp)] + [ANY] * 10,
        out_specs=(
            pl.BlockSpec((tokens, width), lambda t: (0, 0)),
            pl.BlockSpec((tokens, width), lambda t: (0, 0)),
            pl.BlockSpec((2, width // 2, tile), lambda t: (0, 0, t)),
            pl.BlockSpec((2, width // 2, tile), lambda t: (0, 0, t)),
            pl.BlockSpec((1, tile), lambda t: (0, t)),
        ),
        out_shape=(
            sds((tokens, width), out_type),
            sds((tokens, width), f32),
            sds((2, width // 2, cols), bf16),
            sds((2, width // 2, cols), bf16),
            sds((1, cols), f32),
        ),
        scratch_shapes=[
            pltpu.VMEM((2, 2, width, tile), bf16),
            pltpu.VMEM((tokens, width), f32),
            pltpu.VMEM((tokens, width), f32),
            pltpu.SemaphoreType.DMA((2, 2, 8)),
        ],
        cost_estimate=pl.CostEstimate(
            flops=12 * tokens * width * cols, bytes_accessed=8 * width * cols + 12 * tokens * width, transcendentals=tokens * cols
        ),
        name="mlp_first" if first else "mlp_last",
    )(n2, cot, n2t, cott, b1, vec, outp, gnp, *pieces)


def norm_back(v, g, gain):
    center = v - jnp.mean(v, axis=-1, keepdims=True)
    rs = lax.rsqrt(jnp.mean(center * center, axis=-1, keepdims=True) + epsilon)
    n = center * rs
    e = g * gain
    grad = rs * (e - jnp.mean(e, axis=-1, keepdims=True) - n * jnp.mean(e * n, axis=-1, keepdims=True))
    return grad, g * n


def branch_kernel(cot_ref, gn_ref, mid_ref, vec_ref, att_ref, attt_ref, *rest):
    pieces, (gm_ref, ga_ref, keep_ref, send_ref, sums_ref, del_ref, w, gb, sem) = rest[:10], rest[10:]
    tokens, width = cot_ref.shape
    copies = unit_copies(pieces, 0, pl.ds(width, width), w, sem)
    for c in copies:
        c.start()
    sums_ref[...] = jnp.zeros(sums_ref.shape, f32)

    def body(rows):
        cot = cot_ref[rows, :].astype(f32)
        g = gn_ref[rows, :]
        grad, gain_part = norm_back(mid_ref[rows, :], g, vec_ref[5:6, 0:width])
        gm = cot + grad
        gm_ref[rows, :] = gm
        low = gm.astype(bf16)
        gb[rows, :] = low
        sums_ref[0:1, :] += jnp.sum(gain_part, axis=0, keepdims=True)
        sums_ref[1:2, :] += jnp.sum(g, axis=0, keepdims=True)
        sums_ref[2:3, :] += jnp.sum(low.astype(f32), axis=0, keepdims=True)
        sums_ref[3:4, :] += jnp.sum(cot, axis=0, keepdims=True)

    row_loop(tokens, body)
    half, part = width // 2, keep_ref.shape[-1]
    for i in range(2):
        at = i * (width - part)
        g = nn(attt_ref[...], gb[:, at : at + part]).astype(bf16)
        keep_ref[i], send_ref[i] = g[:half], g[half:]
    for c in copies:
        c.wait()
    column = lax.broadcasted_iota(jnp.int32, (HEADS, 128), 1)
    first = lax.broadcasted_iota(jnp.int32, (HEADS, 128), 0) * HD
    del_ref[...] = jnp.zeros(del_ref.shape, f32)

    @pl.loop(0, width // 128)
    def _(j):
        cols = pl.ds(pl.multiple_of(j * 128, 128), 128)
        ga = nt(gb[...], w[cols, :]).astype(bf16)
        ga_ref[:, cols] = ga
        prod = ga.astype(f32) * att_ref[:, cols].astype(f32)
        high = prod.astype(bf16)
        rest_low = (prod - high.astype(f32)).astype(bf16)
        at = column + j * 128
        chosen = jnp.where((at >= first) & (at < first + HD), 1.0, 0.0).astype(bf16)
        del_ref[...] += nt(chosen, high) + nt(chosen, rest_low)


def qkv_grad_kernel(nt_ref, dq_ref, dko_ref, dkr_ref, keep_ref, send_ref, dkv_ref, all_ref):
    tokens, width = dq_ref.shape
    half, part = width // 2, keep_ref.shape[-1]

    def join(rows):
        total = (dko_ref[rows, :] + dkr_ref[rows, :].astype(f32)).astype(bf16)
        dkv_ref[rows, :] = total
        all_ref[rows, 0:width] = dq_ref[rows, :]
        all_ref[rows, width : 3 * width] = total

    row_loop(tokens, join)
    for i in range(2):

        @pl.loop(0, part // 256)
        def _(t):
            cols = pl.ds(pl.multiple_of(t * 256, 256), 256)
            at = pl.ds(pl.multiple_of(t * 256 + i * (3 * width - part), 128), 256)
            g = nn(nt_ref[...], all_ref[:, at]).astype(bf16)
            keep_ref[i, :, cols], send_ref[i, :, cols] = g[:half], g[half:]


def input_grad_kernel(dq_ref, dkv_ref, x_ref, gm_ref, vec_ref, *rest):
    pieces, (gx_ref, sums_ref, wq, wkv, gn, sem) = rest[:10], rest[10:]
    tokens, width = x_ref.shape
    copies = unit_copies(pieces, 0, pl.ds(0, width), wq, sem.at[0]) + unit_copies(
        pieces, 1, pl.ds(0, 2 * width), wkv, sem.at[1]
    )
    for c in copies:
        c.start()
    sums_ref[...] = jnp.zeros(sums_ref.shape, f32)
    for c in copies:
        c.wait()

    @pl.loop(0, width // 128)
    def _(j):
        rows = pl.ds(pl.multiple_of(j * 128, 128), 128)
        gn[:, rows] = nt(dq_ref[...], wq[rows, :]) + nt(dkv_ref[...], wkv[rows, :])

    def body(rows):
        g = gn[rows, :]
        grad, gain_part = norm_back(x_ref[rows, :].astype(f32), g, vec_ref[0:1, 0:width])
        gx_ref[rows, :] = (gm_ref[rows, :] + grad).astype(bf16)
        sums_ref[0:1, :] += jnp.sum(gain_part, axis=0, keepdims=True)
        sums_ref[1:2, :] += jnp.sum(g, axis=0, keepdims=True)
        sums_ref[2:3, :] += jnp.sum(dq_ref[rows, :].astype(f32), axis=0, keepdims=True)
        sums_ref[3:4, :] += jnp.sum(dkv_ref[rows, width : 2 * width].astype(f32), axis=0, keepdims=True)

    row_loop(tokens, body)


def call(body, name, outs, scratch, flops, moved, *args, pieces=()):
    return pl.pallas_call(
        body,
        out_shape=tuple(sds(s, t) for s, t in outs),
        in_specs=[VM] * len(args) + [ANY] * len(pieces),
        out_specs=tuple(VM for _ in outs),
        scratch_shapes=scratch,
        cost_estimate=pl.CostEstimate(flops=flops, bytes_accessed=moved, transcendentals=0),
        name=name,
    )(*args, *pieces)


def swap(v, mask, size):
    return lax.ppermute(v, "dp", [(i, i ^ mask) for i in range(size)])


def after(v, *others):
    return lax.optimization_barrier((v, *others))[0]


def sums_kernel(shape, *refs):
    terms, outs, at = refs[: sum(map(sum, shape))], refs[sum(map(sum, shape)) :], 0
    for out, counts in zip(outs, shape):
        for k, count in enumerate(counts):
            total = terms[at][...].astype(f32)
            for r in terms[at + 1 : at + count]:
                total = total + r[...].astype(f32)
            out[k] = total.astype(bf16)
            at += count


def add_blocks(name, *outs):
    first = outs[0][0][0][0]
    rows, cols = first.shape[-2:]
    tile = max(t for t in range(128, 1025, 128) if cols % t == 0)
    specs, args = [], []
    for out in outs:
        for terms in out:
            for array, index in terms:
                specs.append(pl.BlockSpec((None,) * len(index) + (rows, tile), lambda t, index=index: (*index, 0, t)))
                args.append(array)
    count = sum(len(out) for out in outs)
    return pl.pallas_call(
        functools.partial(sums_kernel, [[len(terms) for terms in out] for out in outs]),
        grid=(cols // tile,),
        in_specs=specs,
        out_specs=tuple(pl.BlockSpec((len(out), rows, tile), lambda t: (0, 0, t)) for out in outs),
        out_shape=tuple(sds((len(out), rows, cols), bf16) for out in outs),
        cost_estimate=pl.CostEstimate(flops=len(args) * rows * cols, bytes_accessed=2 * (len(args) + count) * rows * cols, transcendentals=0),
        name=name,
    )(*args)


def blocks(v):
    return v.reshape(2, 4, v.shape[1] // 4, v.shape[2])


def unit_first(name, keep, got, size):
    k, g = blocks(keep), blocks(got)
    sa, sb = add_blocks(
        name, [[(k, (0, j)), (g, (0, j))] for j in (1, 3)], [[(k, (1, j)), (g, (1, j))] for j in (2, 3)]
    )
    return swap(sa, 2, size), swap(sb, 4, size)


def unit_second(name, keep, got, ax, by, size):
    k, g = blocks(keep), blocks(got)
    ta, tb = add_blocks(name, [[(k, (0, 2)), (g, (0, 2)), (ax, (1,))]], [[(k, (1, 1)), (g, (1, 1)), (by, (1,))]])
    return swap(ta, 4, size), swap(tb, 2, size)


def unit_third(name, keep, got, ax, by, ay, bx):
    k, g = blocks(keep), blocks(got)
    return add_blocks(
        name, [[(k, (0, 0)), (g, (0, 0)), (ax, (0,)), (ay, (0,))], [(k, (1, 0)), (g, (1, 0)), (by, (0,)), (bx, (0,))]]
    )[0]


def fold_in(own):
    return lax.ppermute(own, "seq", [(0, 1), (3, 2)])


def across(inner):
    return lax.ppermute(inner, "seq", [(1, 2), (2, 1)])


def fold_out(total):
    return lax.ppermute(total, "seq", [(1, 0), (2, 3)])


def pair_sum(name, a, b):
    return add_blocks(name, [[(a, (i,)), (b, (i,))] for i in range(a.shape[0])])[0]


def reduce_small(rows, size):
    d = lax.axis_index("dp")
    bit, left = 1, rows
    while bit < size:
        pairs = left.reshape(left.shape[0] // 2, 2, -1)
        up = (d // bit) % 2 == 1
        mine = jnp.where(up, pairs[:, 1], pairs[:, 0])
        other = jnp.where(up, pairs[:, 0], pairs[:, 1])
        left = mine + swap(other.astype(bf16), bit, size).astype(f32)
        bit *= 2
    for mask in (1, 2):
        low = left.astype(bf16)
        left = low.astype(f32) + lax.ppermute(low, "seq", [(i, i ^ mask) for i in range(4)]).astype(f32)
    return left[0]


def gather_small(row, size):
    d = lax.axis_index("dp")
    got, bit = row[None], 1
    while bit < size:
        other = swap(got, bit, size)
        up = (d // bit) % 2 == 1
        got = jnp.concatenate([jnp.where(up, other, got), jnp.where(up, got, other)], axis=0)
        bit *= 2
    return got


def token_routes(size, depth):
    routes = []
    for s in range(2):
        perm = []
        for d in range(size):
            for z in range(depth):
                j = (z & 1) ^ s
                to_d, to_z = (d & ~1) | (z >> 1), 2 * (d & 1) + j
                perm.append((d * depth + z, to_d * depth + to_z))
        routes.append(perm)
    return routes


def to_rows(v, routes):
    odd = lax.axis_index("seq") % 2 == 1
    first = jnp.where(odd, v[1], v[0])
    second = jnp.where(odd, v[0], v[1])
    r0 = lax.ppermute(first, ("dp", "seq"), routes[0])
    r1 = lax.ppermute(second, ("dp", "seq"), routes[1])
    return jnp.concatenate([jnp.where(odd, r1, r0), jnp.where(odd, r0, r1)], axis=0)


def from_rows(v, routes):
    odd = lax.axis_index("seq") % 2 == 1
    half = v.shape[0] // 2
    t0, t1 = v[:half], v[half:]
    back = [[(b, a) for a, b in perm] for perm in routes]
    r0 = lax.ppermute(jnp.where(odd, t1, t0), ("dp", "seq"), back[0])
    r1 = lax.ppermute(jnp.where(odd, t0, t1), ("dp", "seq"), back[1])
    return jnp.stack([jnp.where(odd, r1, r0), jnp.where(odd, r0, r1)])


def by_rows(size, depth):
    def step(patches, picture_ids, valid_mask, ln1_gain, ln1_bias, w_qkv, bias_qv, w_out, b_out, ln2_gain, ln2_bias,
             w_fc1, b_fc1, w_fc2, b_fc2, cotangent):
        width = patches.shape[-1]
        ff = w_fc1.shape[1]
        tokens = patches.shape[0] * patches.shape[1]
        part = width // size
        d, z = lax.axis_index("dp"), lax.axis_index("seq")
        core = d % 2
        routes = token_routes(size, depth)

        unit0 = jnp.stack([jnp.concatenate([w_qkv[:, :width], w_out], axis=1), w_qkv[:, width:]])
        extra = -ff % 256
        w1 = jnp.pad(w_fc1, ((0, 0), (0, extra)))
        w2 = jnp.pad(w_fc2.T, ((0, 0), (0, extra)))
        cut = (ff + extra) // 512 * 256 + ((ff + extra) // 256 % 2) * 256
        unit1 = jnp.stack([w1[:, :cut], w2[:, :cut]])
        unit2 = jnp.stack([w1[:, cut:], w2[:, cut:]])
        x = to_rows(patches, routes)
        x0, y0, c0 = swap(unit0, 2, size), swap(unit0, 4, size), swap(unit0, 1, size)
        da0, db0, cx0, cy0 = swap(y0[0], 2, size), swap(x0[1], 4, size), swap(x0, 1, size), swap(y0, 1, size)
        unit1 = after(unit1, x0, y0)
        x1, y1, c1 = swap(unit1, 2, size), swap(unit1, 4, size), swap(unit1, 1, size)
        p0 = (unit0, c0, x0, cx0, y0, cy0, da0, db0, swap(da0, 1, size), swap(db0, 1, size))
        cot = to_rows(after(cotangent, x), routes)

        small = jnp.concatenate([ln1_gain, ln1_bias, bias_qv[0], bias_qv[1], b_out, ln2_gain, ln2_bias, b_fc2, b_fc1])
        small = gather_small(small, size).astype(f32)
        vec = jnp.moveaxis(small[:, : 8 * part].reshape(size, 8, part), 0, 1).reshape(8, width)
        b1 = jnp.pad(small[:, 8 * part :].reshape(1, ff), ((0, 0), (0, extra)))
        vec = jnp.concatenate([vec, jnp.zeros((8, width), f32)], axis=0)
        kv_bias = jnp.concatenate([jnp.zeros((1, width), f32), vec[3:4]], axis=1)
        vec = jnp.concatenate([jnp.pad(vec[:8], ((0, 0), (0, width))), jnp.pad(kv_bias, ((0, 7), (0, 0)))], axis=0)

        ids = jnp.stack([picture_ids, jnp.where(valid_mask == 1, picture_ids, -1)])
        far_ids = swap(ids, 1, size)
        ids = jnp.where(z // 2 == core, ids, far_ids)
        ids = jnp.where(z % 2 == 1, ids[:, 1], ids[:, 0]).reshape(2, 2, tokens)
        near = jnp.where(core == 1, ids[:, 1], ids[:, 0])
        far = jnp.where(core == 1, ids[:, 0], ids[:, 1])
        keys = jnp.concatenate([near[1], far[1]])
        qid_row, qid_col = jnp.broadcast_to(near[0][None], (8, tokens)), jnp.broadcast_to(near[0][:, None], (tokens, 128))
        kid_row, kid_col = jnp.broadcast_to(keys[None], (8, 2 * tokens)), jnp.broadcast_to(keys[:, None], (2 * tokens, 128))

        act = ((tokens, width), bf16)
        flip = ((width, tokens), bf16)
        vm = pltpu.VMEM
        dma8 = pltpu.SemaphoreType.DMA((8,))
        mm = 2 * tokens * width * width
        n, kv = call(kv_kernel, "kv", [act, ((tokens, 2 * width), bf16)], [vm((width, 2 * width), bf16), dma8],
                     2 * mm, 4 * width * width, x, vec, pieces=p0)
        far_kv = swap(kv, 1, size)
        q, nt_ = call(q_kernel, "q", [act, flip], [vm((width, width), bf16), vm((width, tokens), bf16), dma8],
                      mm, 2 * width * width, n, vec, pieces=p0)
        sc = 2 * tokens * 2 * tokens * WIN * HEADS
        q, x1, y1 = lax.optimization_barrier((q, x1, y1))
        da1, db1, cx1, cy1 = swap(y1[0], 2, size), swap(x1[1], 4, size), swap(x1, 1, size), swap(y1, 1, size)
        unit2 = after(unit2, q, x1, y1)
        x2, y2, c2 = swap(unit2, 2, size), swap(unit2, 4, size), swap(unit2, 1, size)
        att, lse = call(
            attention_forward_kernel, "attention_forward", [act, ((HEADS, tokens), f32)],
            [vm((tokens, 2 * tokens), f32), vm((tokens, width), f32), vm((tokens, 128), f32)],
            3 * sc, 8 * tokens * width, q, kv, far_kv, qid_col, kid_row)
        da1, db1, att = lax.optimization_barrier((da1, db1, att))
        p1 = (unit1, c1, x1, cx1, y1, cy1, da1, db1, swap(da1, 1, size), swap(db1, 1, size))
        mid, n2, n2t, cott, attt = call(
            middle_kernel, "middle", [((tokens, width), f32), act, flip, flip, flip],
            [vm((width, width), bf16), vm((width, tokens), bf16), dma8], mm, 2 * width * width, att, x, cot, vec, pieces=p0)
        n2, x2, y2 = lax.optimization_barrier((n2, x2, y2))
        da2, db2, cx2, cy2 = swap(y2[0], 2, size), swap(x2[1], 4, size), swap(x2, 1, size), swap(y2, 1, size)
        acc, gn, keep1, send1, gb1a = mlp_call(True, False, n2, cot, n2t, cott, b1[:, :cut], vec, mid, mid, p1)
        acc, da2, db2 = lax.optimization_barrier((acc, da2, db2))
        p2 = (unit2, c2, x2, cx2, y2, cy2, da2, db2, swap(da2, 1, size), swap(db2, 1, size))
        got1 = swap(send1.reshape(2, width // 2, -1), 1, size)
        out, gn, keep2, send2, gb1b = mlp_call(False, True, n2, cot, n2t, cott, b1[:, cut:], vec, acc, gn, p2)
        keep1, got1, gn = lax.optimization_barrier((keep1, got1, gn))
        ax1, by1 = unit_first("first1", keep1, got1, size)
        got2 = swap(send2, 1, size)
        layer_out = from_rows(out, routes)

        part_o = (width // 256 + 1) * 128
        stacked = ((2, width // 2, part_o), bf16)
        gm, ga, keepo, sendo, sums2, inner = call(
            branch_kernel, "branch", [((tokens, width), f32), act, stacked, stacked, ((8, width), f32), ((HEADS, tokens), f32)],
            [vm((width, width), bf16), vm((tokens, width), bf16), dma8], 2 * mm, 4 * width * width,
            cot, gn, mid, vec, att, attt, pieces=p0)
        keep2, got2, ga = lax.optimization_barrier((keep2, got2, ga))
        ax2, by2 = unit_first("first2", keep2, got2, size)
        goto = swap(sendo, 1, size)

        def attention_backward(near, kv_half, ids_half, dqp):
            return call(
                functools.partial(attention_backward_kernel, near), "attention_backward_near" if near else "attention_backward_far",
                [((tokens, width), bf16 if near else f32), ((tokens, 2 * width), f32 if near else bf16)],
                [vm((tokens, tokens), f32), vm((tokens, width), f32), vm((tokens, 2 * width), f32)],
                3 * sc, 16 * tokens * width, q, kv_half, ga, lse, inner, ids_half, qid_row, dqp)

        dqp, dkx = attention_backward(False, far_kv, kid_col[tokens:], gm)
        dkr = swap(dkx, 1, size)
        dqp, ax1, by1, goto = lax.optimization_barrier((dqp, ax1, by1, goto))
        ay1, bx1 = unit_second("second1", keep1, got1, ax1, by1, size)
        axo, byo = unit_first("firsto", keepo, goto, size)
        dq, dko = attention_backward(True, kv, kid_col[:tokens], dqp)
        dq, ax2, by2, ay1, bx1 = lax.optimization_barrier((dq, ax2, by2, ay1, bx1))
        ay2, bx2 = unit_second("second2", keep2, got2, ax2, by2, size)
        own1 = unit_third("third1", keep1, got1, ax1, by1, ay1, bx1)
        in1 = fold_in(own1)
        part_q = (3 * width // 256 + 1) * 128
        stacked = ((2, width // 2, part_q), bf16)
        keepq, sendq, dkv = call(
            qkv_grad_kernel, "qkv_grad", [stacked, stacked, ((tokens, 2 * width), bf16)], [vm((tokens, 3 * width), bf16)],
            3 * mm, 8 * width * width, nt_, dq, dko, dkr)
        gotq = swap(sendq, 1, size)
        dkv, axo, byo = lax.optimization_barrier((dkv, axo, byo))
        ayo, bxo = unit_second("secondo", keepo, goto, axo, byo, size)
        gx, sums1 = call(
            input_grad_kernel, "input_grad", [act, ((8, width), f32)],
            [vm((width, width), bf16), vm((width, 2 * width), bf16), vm((tokens, width), f32), pltpu.SemaphoreType.DMA((2, 8))],
            3 * mm, 6 * width * width, dq, dkv, x, gm, vec, pieces=p0)
        keepq, gotq, gx = lax.optimization_barrier((keepq, gotq, gx))
        axq, byq = unit_first("firstq", keepq, gotq, size)
        grad_patches = from_rows(gx, routes)

        gb1 = jnp.concatenate([gb1a, gb1b], axis=1)[:, :ff].reshape(size, ff // size)
        vecs = jnp.concatenate([sums1[:4], sums2[:4]]).reshape(8, size, part)
        small = reduce_small(jnp.concatenate([jnp.moveaxis(vecs, 0, 1).reshape(size, 8 * part), gb1], axis=1), size)
        mine, grad_b_fc1 = small[: 8 * part].reshape(8, part), small[8 * part :]

        own2 = unit_third("third2", keep2, got2, ax2, by2, ay2, bx2)
        owno = unit_third("thirdo", keepo, goto, axo, byo, ayo, bxo)
        in2, ino = fold_in(own2), fold_in(owno)
        mid1 = pair_sum("inner1", own1, in1)
        tot1 = pair_sum("total1", mid1, across(mid1))
        mid2, mido = pair_sum("inner2", own2, in2), pair_sum("innero", owno, ino)
        tot2, toto = pair_sum("total2", mid2, across(mid2)), pair_sum("totalo", mido, across(mido))
        ayq, bxq = unit_second("secondq", keepq, gotq, axq, byq, size)
        ownq = unit_third("thirdq", keepq, gotq, axq, byq, ayq, bxq)
        midq = pair_sum("innerq", ownq, fold_in(ownq))
        totq = pair_sum("totalq", midq, across(midq))
        inside = (z == 1) | (z == 2)
        g1, g2, go, gq = [jnp.where(inside, t, fold_out(t)).astype(f32) for t in (tot1, tot2, toto, totq)]
        n1, nk = cut, ff - cut
        w1g = jnp.concatenate([g1[0], g2[0][:, :nk]], axis=1)
        w2g = jnp.concatenate([g1[1], g2[1][:, :nk]], axis=1).T
        wog = jnp.concatenate([go[0], go[1][:, 2 * part_o - width :]], axis=1)
        wqg = jnp.concatenate([gq[0], gq[1][:, 2 * part_q - 3 * width :]], axis=1)
        return (layer_out, grad_patches, mine[0], mine[1], wqg, mine[2:4], wog, mine[6], mine[4], mine[5], w1g, grad_b_fc1, w2g, mine[7])

    return step


def fits_rows(mesh, patches):
    return mesh.shape["dp"] == 8 and mesh.shape["seq"] == 4


def solution(mesh):
    placed = (
        P("dp", "seq", None),
        P("dp", None),
        P("dp", None),
        P("dp"),
        P("dp"),
        P("dp", None),
        P(None, "dp"),
        P("dp", None),
        P("dp"),
        P("dp"),
        P("dp"),
        P("dp", None),
        P("dp"),
        P(None, "dp"),
        P("dp"),
        P("dp", "seq", None),
    )
    return jax.shard_map(
        by_rows(mesh.shape["dp"], mesh.shape["seq"]) if fits_rows(mesh, None) else per_device,
        mesh=mesh,
        in_specs=placed,
        out_specs=(
            P("dp", "seq", None),
            P("dp", "seq", None),
            P("dp"),
            P("dp"),
            P("dp", None),
            P(None, "dp"),
            P("dp", None),
            P("dp"),
            P("dp"),
            P("dp"),
            P("dp", None),
            P("dp"),
            P(None, "dp"),
            P("dp"),
        ),
        check_vma=False,
    )
```

```python
import functools

import jax
import jax.numpy as jnp
from jax import lax
from jax.experimental import pallas as pl
from jax.experimental.pallas import tpu as pltpu
from jax.sharding import PartitionSpec as P

HEADS = 16
HD = 72


epsilon = 1e-06
big_negative = -1e30


def layer_norm(values, scales, offset):
    center = values - jnp.mean(values, axis=-1, keepdims=True)
    spread = jnp.mean(center * center, axis=-1, keepdims=True)
    return center * lax.rsqrt(spread + epsilon) * scales + offset


def gelu_tanh(values):
    return (
        0.5
        * values
        * (1.0 + jnp.tanh(0.7978845608028654 * (values + 0.044715 * values * values * values)))
    )


def contract_rows(left, right):
    return lax.dot_general(
        left, right, (((0,), (0,)), ((), ())), preferred_element_type=jnp.float32
    )


def contract_cols(left, right):
    return lax.dot_general(
        left, right, (((1,), (1,)), ((), ())), preferred_element_type=jnp.float32
    )


def gather_weights(
    ln1_gain, ln1_bias, w_qkv, bias_qv, w_out, b_out, ln2_gain, ln2_bias, w_fc1, b_fc1, w_fc2, b_fc2
):
    return (
        lax.all_gather(ln1_gain, "dp", axis=0, tiled=True),
        lax.all_gather(ln1_bias, "dp", axis=0, tiled=True),
        lax.all_gather(w_qkv, "dp", axis=0, tiled=True),
        lax.all_gather(bias_qv, "dp", axis=1, tiled=True),
        lax.all_gather(w_out, "dp", axis=0, tiled=True),
        lax.all_gather(b_out, "dp", axis=0, tiled=True),
        lax.all_gather(ln2_gain, "dp", axis=0, tiled=True),
        lax.all_gather(ln2_bias, "dp", axis=0, tiled=True),
        lax.all_gather(w_fc1, "dp", axis=0, tiled=True),
        lax.all_gather(b_fc1, "dp", axis=0, tiled=True),
        lax.all_gather(w_fc2, "dp", axis=1, tiled=True),
        lax.all_gather(b_fc2, "dp", axis=0, tiled=True),
    )


def block_scores(queries, key_vectors, picture_ids, valid_mask, first_row, block_rows):
    length = picture_ids.shape[1]
    query_block = lax.dynamic_slice_in_dim(queries, first_row, block_rows, 1)
    ids_block = lax.dynamic_slice_in_dim(picture_ids, first_row, block_rows, 1)
    same_picture = (ids_block[:, :, None] == picture_ids[:, None, :]) & (
        valid_mask[:, None, :] == 1
    )
    diagonal = (first_row + jnp.arange(block_rows))[:, None] == jnp.arange(length)[None, :]
    allowed = (same_picture | diagonal[None])[:, None]
    scaling = queries.shape[-1] ** (-0.5)
    scores = (
        jnp.einsum("rqhe,rkhe->rhqk", query_block, key_vectors, preferred_element_type=jnp.float32)
        * scaling
    )
    return (query_block, jnp.where(allowed, scores, big_negative))


def attention_forward(queries, key_vectors, value_vectors, picture_ids, valid_mask):
    row_count, length, head_count, head_size = queries.shape
    block_rows = min(512, length)

    def one_block(block_index):
        query_block, scores = block_scores(
            queries, key_vectors, picture_ids, valid_mask, block_index * block_rows, block_rows
        )
        row_max = jnp.max(scores, axis=-1, keepdims=True)
        exp_terms = jnp.exp(scores - row_max)
        totals = jnp.sum(exp_terms, axis=-1, keepdims=True)
        probs_low = (exp_terms / totals).astype(jnp.bfloat16)
        mixing = jnp.einsum(
            "rhqk,rkhe->rqhe", probs_low, value_vectors, preferred_element_type=jnp.float32
        )
        return (mixing.astype(jnp.bfloat16), (row_max + jnp.log(totals))[..., 0])

    outputs, log_sums = lax.map(one_block, jnp.arange(length // block_rows))
    outputs = jnp.moveaxis(outputs, 0, 1).reshape(row_count, length, head_count, head_size)
    log_sums = jnp.moveaxis(log_sums, 0, 2).reshape(row_count, head_count, length)
    return (outputs, log_sums)


def attention_backward(
    queries, key_vectors, value_vectors, log_sums, grad_heads, picture_ids, valid_mask
):
    row_count, length, head_count, head_size = queries.shape
    block_rows = min(512, length)
    scaling = head_size ** (-0.5)

    def one_block(running, block_index):
        grad_keys, grad_values = running
        first_row = block_index * block_rows
        query_block, scores = block_scores(
            queries, key_vectors, picture_ids, valid_mask, first_row, block_rows
        )
        lse_block = lax.dynamic_slice_in_dim(log_sums, first_row, block_rows, 2)
        attn_probs = jnp.exp(scores - lse_block[..., None])
        grad_block = lax.dynamic_slice_in_dim(grad_heads, first_row, block_rows, 1)
        grad_values = grad_values + jnp.einsum(
            "rhqk,rqhe->rkhe",
            attn_probs.astype(jnp.bfloat16),
            grad_block,
            preferred_element_type=jnp.float32,
        )
        grad_probs = jnp.einsum(
            "rqhe,rkhe->rhqk", grad_block, value_vectors, preferred_element_type=jnp.float32
        )
        inner = jnp.sum(attn_probs * grad_probs, axis=-1, keepdims=True)
        grad_scores = (attn_probs * (grad_probs - inner)).astype(jnp.bfloat16)
        grad_query = (
            jnp.einsum(
                "rhqk,rkhe->rqhe", grad_scores, key_vectors, preferred_element_type=jnp.float32
            )
            * scaling
        )
        grad_keys = (
            grad_keys
            + jnp.einsum(
                "rhqk,rqhe->rkhe", grad_scores, query_block, preferred_element_type=jnp.float32
            )
            * scaling
        )
        return ((grad_keys, grad_values), grad_query)

    zeros_start = jnp.zeros(queries.shape, jnp.float32)
    (grad_keys, grad_values), grad_queries = lax.scan(
        one_block, (zeros_start, zeros_start), jnp.arange(length // block_rows)
    )
    grad_queries = jnp.moveaxis(grad_queries, 0, 1).reshape(
        row_count, length, head_count, head_size
    )
    return (grad_queries, grad_keys, grad_values)


def forward_pass(patches, picture_ids, valid_mask, gathered):
    (
        ln1_gain,
        ln1_bias,
        w_qkv,
        bias_qv,
        w_out,
        b_out,
        ln2_gain,
        ln2_bias,
        w_fc1,
        b_fc1,
        w_fc2,
        b_fc2,
    ) = gathered
    row_count, local_len, model_width = patches.shape
    inputs = patches.astype(jnp.float32).reshape(row_count * local_len, model_width)
    normed = layer_norm(inputs, ln1_gain.astype(jnp.float32), ln1_bias.astype(jnp.float32)).astype(
        jnp.bfloat16
    )
    projected = jnp.dot(normed, w_qkv, preferred_element_type=jnp.float32)
    bias_full = jnp.concatenate([bias_qv[0], jnp.zeros_like(bias_qv[0]), bias_qv[1]]).astype(
        jnp.float32
    )
    projected = (
        (projected + bias_full).astype(jnp.bfloat16).reshape(row_count, local_len, 3, HEADS, HD)
    )
    by_heads = lax.all_to_all(projected, "seq", split_axis=3, concat_axis=1, tiled=True)
    queries = by_heads[:, :, 0]
    key_vectors = by_heads[:, :, 1]
    value_vectors = by_heads[:, :, 2]
    mixing, log_sums = attention_forward(
        queries, key_vectors, value_vectors, picture_ids, valid_mask
    )
    token_mixing = lax.all_to_all(mixing, "seq", split_axis=1, concat_axis=2, tiled=True)
    attended = token_mixing.reshape(row_count * local_len, model_width)
    middle = (
        inputs
        + jnp.dot(attended, w_out, preferred_element_type=jnp.float32)
        + b_out.astype(jnp.float32)
    )
    normed_two = layer_norm(
        middle, ln2_gain.astype(jnp.float32), ln2_bias.astype(jnp.float32)
    ).astype(jnp.bfloat16)
    hidden = jnp.dot(normed_two, w_fc1, preferred_element_type=jnp.float32) + b_fc1.astype(
        jnp.float32
    )
    active = gelu_tanh(hidden).astype(jnp.bfloat16)
    outputs = (
        middle
        + jnp.dot(active, w_fc2, preferred_element_type=jnp.float32)
        + b_fc2.astype(jnp.float32)
    )
    layer_out = outputs.astype(jnp.bfloat16).reshape(row_count, local_len, model_width)
    kept_values = (
        inputs,
        normed,
        queries,
        key_vectors,
        value_vectors,
        log_sums,
        attended,
        middle,
        normed_two,
        hidden,
        active,
    )
    return (layer_out, kept_values)


def backward_pass(cotangent, picture_ids, valid_mask, gathered, kept_values):
    (
        ln1_gain,
        ln1_bias,
        w_qkv,
        bias_qv,
        w_out,
        b_out,
        ln2_gain,
        ln2_bias,
        w_fc1,
        b_fc1,
        w_fc2,
        b_fc2,
    ) = gathered
    (
        inputs,
        normed,
        queries,
        key_vectors,
        value_vectors,
        log_sums,
        attended,
        middle,
        normed_two,
        hidden,
        active,
    ) = kept_values
    row_count, local_len, model_width = cotangent.shape
    grad_z = cotangent.reshape(row_count * local_len, model_width)
    grad_w_fc2 = contract_rows(active, grad_z)
    grad_b_fc2 = jnp.sum(grad_z.astype(jnp.float32), axis=0)
    grad_active = contract_cols(grad_z, w_fc2)
    grad_hidden = jax.vjp(gelu_tanh, hidden)[1](grad_active)[0].astype(jnp.bfloat16)
    grad_w_fc1 = contract_rows(normed_two, grad_hidden)
    grad_b_fc1 = jnp.sum(grad_hidden.astype(jnp.float32), axis=0)
    grad_normed_two = contract_cols(grad_hidden, w_fc1)
    norm_pull = jax.vjp(
        layer_norm, middle, ln2_gain.astype(jnp.float32), ln2_bias.astype(jnp.float32)
    )[1]
    grad_middle, grad_ln2_gain, grad_ln2_bias = norm_pull(grad_normed_two)
    grad_middle = grad_middle + grad_z.astype(jnp.float32)
    grad_branch = grad_middle.astype(jnp.bfloat16)
    grad_w_out = contract_rows(attended, grad_branch)
    grad_b_out = jnp.sum(grad_branch.astype(jnp.float32), axis=0)
    grad_attended = (
        contract_cols(grad_branch, w_out)
        .astype(jnp.bfloat16)
        .reshape(row_count, local_len, HEADS, HD)
    )
    grad_heads = lax.all_to_all(grad_attended, "seq", split_axis=2, concat_axis=1, tiled=True)
    grad_queries, grad_keys, grad_values = attention_backward(
        queries, key_vectors, value_vectors, log_sums, grad_heads, picture_ids, valid_mask
    )
    grad_proj = jnp.stack([grad_queries, grad_keys, grad_values], axis=2).astype(jnp.bfloat16)
    grad_tokens = lax.all_to_all(grad_proj, "seq", split_axis=1, concat_axis=3, tiled=True).reshape(
        row_count * local_len, 3 * model_width
    )
    grad_w_qkv = contract_rows(normed, grad_tokens)
    column_sums = jnp.sum(grad_tokens.astype(jnp.float32), axis=0)
    grad_bias_qv = jnp.stack([column_sums[:model_width], column_sums[2 * model_width :]])
    grad_normed = contract_cols(grad_tokens, w_qkv)
    first_pull = jax.vjp(
        layer_norm, inputs, ln1_gain.astype(jnp.float32), ln1_bias.astype(jnp.float32)
    )[1]
    grad_inputs, grad_ln1_gain, grad_ln1_bias = first_pull(grad_normed)
    grad_patches = (
        (grad_middle + grad_inputs).astype(jnp.bfloat16).reshape(row_count, local_len, model_width)
    )
    grads = (
        grad_ln1_gain,
        grad_ln1_bias,
        grad_w_qkv,
        grad_bias_qv,
        grad_w_out,
        grad_b_out,
        grad_ln2_gain,
        grad_ln2_bias,
        grad_w_fc1,
        grad_b_fc1,
        grad_w_fc2,
        grad_b_fc2,
    )
    return (grad_patches, grads)


def per_device(
    patches,
    picture_ids,
    valid_mask,
    ln1_gain,
    ln1_bias,
    w_qkv,
    bias_qv,
    w_out,
    b_out,
    ln2_gain,
    ln2_bias,
    w_fc1,
    b_fc1,
    w_fc2,
    b_fc2,
    cotangent,
):
    gathered = gather_weights(
        ln1_gain,
        ln1_bias,
        w_qkv,
        bias_qv,
        w_out,
        b_out,
        ln2_gain,
        ln2_bias,
        w_fc1,
        b_fc1,
        w_fc2,
        b_fc2,
    )
    layer_out, kept_values = forward_pass(patches, picture_ids, valid_mask, gathered)
    grad_patches, grads = backward_pass(cotangent, picture_ids, valid_mask, gathered, kept_values)
    (
        grad_ln1_gain,
        grad_ln1_bias,
        grad_w_qkv,
        grad_bias_qv,
        grad_w_out,
        grad_b_out,
        grad_ln2_gain,
        grad_ln2_bias,
        grad_w_fc1,
        grad_b_fc1,
        grad_w_fc2,
        grad_b_fc2,
    ) = grads
    owned = (
        lax.psum_scatter(
            grad_ln1_gain.astype(jnp.bfloat16), "dp", scatter_dimension=0, tiled=True
        ).astype(jnp.float32),
        lax.psum_scatter(
            grad_ln1_bias.astype(jnp.bfloat16), "dp", scatter_dimension=0, tiled=True
        ).astype(jnp.float32),
        lax.psum_scatter(
            grad_w_qkv.astype(jnp.bfloat16), "dp", scatter_dimension=0, tiled=True
        ).astype(jnp.float32),
        lax.psum_scatter(
            grad_bias_qv.astype(jnp.bfloat16), "dp", scatter_dimension=1, tiled=True
        ).astype(jnp.float32),
        lax.psum_scatter(
            grad_w_out.astype(jnp.bfloat16), "dp", scatter_dimension=0, tiled=True
        ).astype(jnp.float32),
        lax.psum_scatter(
            grad_b_out.astype(jnp.bfloat16), "dp", scatter_dimension=0, tiled=True
        ).astype(jnp.float32),
        lax.psum_scatter(
            grad_ln2_gain.astype(jnp.bfloat16), "dp", scatter_dimension=0, tiled=True
        ).astype(jnp.float32),
        lax.psum_scatter(
            grad_ln2_bias.astype(jnp.bfloat16), "dp", scatter_dimension=0, tiled=True
        ).astype(jnp.float32),
        lax.psum_scatter(
            grad_w_fc1.astype(jnp.bfloat16), "dp", scatter_dimension=0, tiled=True
        ).astype(jnp.float32),
        lax.psum_scatter(
            grad_b_fc1.astype(jnp.bfloat16), "dp", scatter_dimension=0, tiled=True
        ).astype(jnp.float32),
        lax.psum_scatter(
            grad_w_fc2.astype(jnp.bfloat16), "dp", scatter_dimension=1, tiled=True
        ).astype(jnp.float32),
        lax.psum_scatter(
            grad_b_fc2.astype(jnp.bfloat16), "dp", scatter_dimension=0, tiled=True
        ).astype(jnp.float32),
    )
    (
        part_ln1_gain,
        part_ln1_bias,
        part_w_qkv,
        part_bias_qv,
        part_w_out,
        part_b_out,
        part_ln2_gain,
        part_ln2_bias,
        part_w_fc1,
        part_b_fc1,
        part_w_fc2,
        part_b_fc2,
    ) = owned
    summed = (
        lax.psum(part_ln1_gain.astype(jnp.bfloat16), "seq").astype(jnp.float32),
        lax.psum(part_ln1_bias.astype(jnp.bfloat16), "seq").astype(jnp.float32),
        lax.psum(part_w_qkv.astype(jnp.bfloat16), "seq").astype(jnp.float32),
        lax.psum(part_bias_qv.astype(jnp.bfloat16), "seq").astype(jnp.float32),
        lax.psum(part_w_out.astype(jnp.bfloat16), "seq").astype(jnp.float32),
        lax.psum(part_b_out.astype(jnp.bfloat16), "seq").astype(jnp.float32),
        lax.psum(part_ln2_gain.astype(jnp.bfloat16), "seq").astype(jnp.float32),
        lax.psum(part_ln2_bias.astype(jnp.bfloat16), "seq").astype(jnp.float32),
        lax.psum(part_w_fc1.astype(jnp.bfloat16), "seq").astype(jnp.float32),
        lax.psum(part_b_fc1.astype(jnp.bfloat16), "seq").astype(jnp.float32),
        lax.psum(part_w_fc2.astype(jnp.bfloat16), "seq").astype(jnp.float32),
        lax.psum(part_b_fc2.astype(jnp.bfloat16), "seq").astype(jnp.float32),
    )
    (
        final_ln1_gain,
        final_ln1_bias,
        final_w_qkv,
        final_bias_qv,
        final_w_out,
        final_b_out,
        final_ln2_gain,
        final_ln2_bias,
        final_w_fc1,
        final_b_fc1,
        final_w_fc2,
        final_b_fc2,
    ) = summed
    return (
        layer_out,
        grad_patches,
        final_ln1_gain,
        final_ln1_bias,
        final_w_qkv,
        final_bias_qv,
        final_w_out,
        final_b_out,
        final_ln2_gain,
        final_ln2_bias,
        final_w_fc1,
        final_b_fc1,
        final_w_fc2,
        final_b_fc2,
    )


WIN = 256
ROWBLK = 64
LOG2E = 1.4426950408889634
ORDER = (0, 2, 4, 6, 1, 3, 5, 7)
bf16 = jnp.bfloat16
f32 = jnp.float32


def nn(a, b):
    return lax.dot_general(a, b, (((1,), (0,)), ((), ())), preferred_element_type=f32)


def nt(a, b):
    return lax.dot_general(a, b, (((1,), (1,)), ((), ())), preferred_element_type=f32)


def tn(a, b):
    return lax.dot_general(a, b, (((0,), (0,)), ((), ())), preferred_element_type=f32)


VM = pl.BlockSpec(memory_space=pltpu.VMEM)
ANY = pl.BlockSpec(memory_space=pl.ANY)


def sds(shape, dtype):
    return jax.ShapeDtypeStruct(shape, dtype)


def row_loop(total, body):
    @pl.loop(0, total // ROWBLK)
    def _(r):
        body(pl.ds(pl.multiple_of(r * ROWBLK, ROWBLK), ROWBLK))


MESH = pl.DeviceIdType.MESH


def flipped_index(d, mask):
    for bit in (1, 2, 4):
        if mask & bit:
            d = d + bit - 2 * bit * lax.rem(lax.div(d, bit), 2)
    return d


def sibling():
    return flipped_index(lax.axis_index("dp"), 1), lax.axis_index("seq")


def meet_sibling():
    barrier = pltpu.get_barrier_semaphore()
    pl.semaphore_signal(barrier, inc=1, device_id=sibling(), device_id_type=MESH)
    pl.semaphore_wait(barrier, 1)


def to_sibling(src, dst, sem, i):
    return pltpu.make_async_remote_copy(
        src_ref=src, dst_ref=dst, send_sem=sem.at[1, i], recv_sem=sem.at[2, i], device_id=sibling(), device_id_type=MESH
    )


def unit_copies(pieces, half, rows, cols, place, sem):
    d = lax.axis_index("dp")
    own, xr, yr, da, db = pieces
    copies = []
    for i, piece in enumerate((own, xr, yr, da if half == 0 else db)):
        src = piece.at[half, rows, cols] if i < 3 else piece.at[rows, cols]
        dst = place(flipped_index(d, 2 * i))
        copies.append(pltpu.make_async_copy(src, dst, sem.at[0, i]))
        copies.append(to_sibling(src, dst, sem, i))
    return copies


def shard_rows(ref, count):
    return lambda j: ref.at[pl.ds(pl.multiple_of(j * count, count), count), :]


def start_all(copies):
    for c in copies:
        c.start()


def wait_all(copies):
    for c in copies:
        c.wait()


def norm_rows(v, gain, offset):
    center = v - jnp.mean(v, axis=-1, keepdims=True)
    spread = jnp.mean(center * center, axis=-1, keepdims=True)
    return center * lax.rsqrt(spread + epsilon) * gain + offset


def transpose_ordered(src, flipped, dst):
    d = lax.axis_index("dp")
    width = src.shape[1]
    part = width // 8

    @pl.loop(0, width // 128)
    def _(j):
        cols = pl.ds(pl.multiple_of(j * 128, 128), 128)
        flipped[cols, :] = src[:, cols].T

    for i, m in enumerate(ORDER):
        where = pl.ds(pl.multiple_of(flipped_index(d, m) * part, part), part)
        dst[i * part : (i + 1) * part, :] = flipped[where, :]


def spread(buf, out_ref, part, span):
    inside = (part + 127) // 128 * 128

    @pl.loop(0, 8)
    def _(j):
        at = pl.multiple_of(jnp.minimum(j * part // 128, (out_ref.shape[1] - span) // 128) * 128, 128)
        r = lax.broadcasted_iota(jnp.int32, (inside, span), 0)
        c = lax.broadcasted_iota(jnp.int32, (inside, span), 1)
        place = jnp.where((c == r + (j * part - at)) & (r < part), 1.0, 0.0).astype(bf16)
        out_ref[0:16, pl.ds(at, span)] += nn(buf[j][:, 0:inside], place)


def kv_kernel(ff, x_ref, *rest):
    pieces, (n_ref, kv_ref, vec_ref, b1_ref, wkv_ref, w, buf, sem, out_sem) = rest[:5], rest[5:]
    width = x_ref.shape[1]
    part = width // 8
    every = pl.ds(0, width)
    meet_sibling()
    vectors, weights = [], []
    for half in range(2):
        vectors += unit_copies(pieces, half, pl.ds(part, 16), every, lambda j, half=half: buf.at[half, j], sem.at[2 + half])
    for half in range(2):
        weights += unit_copies(pieces, half, pl.ds(0, part), every, shard_rows(w.at[half], part), sem.at[half])
    start_all(vectors + weights)
    vec_ref[...] = jnp.zeros(vec_ref.shape, f32)
    b1_ref[...] = jnp.zeros(b1_ref.shape, f32)
    wait_all(vectors)
    spread(buf.at[0], vec_ref, part, 512)

    def body(rows):
        v = x_ref[rows, :].astype(f32)
        n_ref[rows, :] = norm_rows(v, vec_ref[0:1, :], vec_ref[1:2, :]).astype(bf16)

    row_loop(x_ref.shape[0], body)
    wait_all(weights)
    store = pltpu.make_async_copy(w, wkv_ref, out_sem)
    store.start()

    def keys(cols):
        kv_ref[:, cols] = nn(n_ref[...], w[0, :, cols]).astype(bf16)

    column_tiles(width, keys)

    def values(cols):
        total = nn(n_ref[...], w[1, :, cols]) + vec_ref[3:4, cols]
        kv_ref[:, pl.ds(pl.multiple_of(cols.start + width, 128), cols.size)] = total.astype(bf16)

    column_tiles(width, values)
    spread(buf.at[1], b1_ref, ff // 8, 768)
    store.wait()


def column_tiles(width, body):
    full = width // 256

    @pl.loop(0, full)
    def _(t):
        body(pl.ds(pl.multiple_of(t * 256, 256), 256))

    if width % 256:
        body(pl.ds(full * 256, width % 256))


def q_kernel(n_ref, vec_ref, *rest):
    pieces, (q_ref, nt_ref, wq_ref, wo_ref, w, flipped, sem, out_sem) = rest[:5], rest[5:]
    width = n_ref.shape[1]
    part = width // 8
    meet_sibling()
    halves = [
        unit_copies(pieces, half, pl.ds(0, part), pl.ds(0, width), shard_rows(w.at[half], part), sem.at[half]) for half in range(2)
    ]
    start_all(halves[0] + halves[1])
    transpose_ordered(n_ref, flipped, nt_ref)
    wait_all(halves[0])

    def body(cols):
        q_ref[:, cols] = (nn(n_ref[...], w[0, :, cols]) + vec_ref[2:3, cols]).astype(bf16)

    column_tiles(width, body)
    wait_all(halves[1])
    stores = [pltpu.make_async_copy(w.at[i], out, out_sem.at[i]) for i, out in ((0, wq_ref), (1, wo_ref))]
    start_all(stores)
    wait_all(stores)


def head_window(h, width):
    w0 = pl.multiple_of(jnp.minimum((h * HD) // 128, (width - WIN) // 128) * 128, 128)
    lane = lax.broadcasted_iota(jnp.int32, (1, WIN), 1)
    off = h * HD - w0
    return w0, (lane >= off) & (lane < off + HD)


def attention_forward_kernel(q_ref, ko_ref, kx_ref, qid_ref, kid_ref, att_ref, lse_ref, bias, acc, lse_cols):
    tokens, width = q_ref.shape
    scale = HD**-0.5 * LOG2E
    block = 256

    @pl.loop(0, tokens // ROWBLK)
    def _(r):
        rows = pl.ds(pl.multiple_of(r * ROWBLK, ROWBLK), ROWBLK)
        same = qid_ref[rows, 0:1] == kid_ref[0:1, :]
        col = lax.broadcasted_iota(jnp.int32, (ROWBLK, 2 * tokens), 1)
        row = lax.broadcasted_iota(jnp.int32, (ROWBLK, 2 * tokens), 0) + r * ROWBLK
        bias[rows, :] = jnp.where(same | (col == row), 0.0, big_negative)
        acc[rows, :] = jnp.zeros((ROWBLK, width), f32)
        lse_cols[rows, :] = jnp.zeros((ROWBLK, 128), f32)

    @pl.loop(0, HEADS)
    def _(h):
        w0, mask = head_window(h, width)
        win, winv = pl.ds(w0, WIN), pl.ds(w0 + width, WIN)
        zero = jnp.zeros((), bf16)
        ko, kx = jnp.where(mask, ko_ref[:, win], zero), jnp.where(mask, kx_ref[:, win], zero)
        vo, vx = jnp.where(mask, ko_ref[:, winv], zero), jnp.where(mask, kx_ref[:, winv], zero)
        lane = lax.broadcasted_iota(jnp.int32, (1, 128), 1)
        for qb in range(tokens // block):
            rows = pl.ds(qb * block, block)
            qw = q_ref[rows, win]
            so = nt(qw, ko) * scale + bias[rows, 0:tokens]
            sx = nt(qw, kx) * scale + bias[rows, tokens : 2 * tokens]
            m = jnp.maximum(jnp.max(so, axis=1, keepdims=True), jnp.max(sx, axis=1, keepdims=True))
            po, px = jnp.exp2(so - m), jnp.exp2(sx - m)
            total = jnp.sum(po, axis=1, keepdims=True) + jnp.sum(px, axis=1, keepdims=True)
            o = nn(po.astype(bf16), vo) + nn(px.astype(bf16), vx)
            acc[rows, win] += o * (1.0 / total)
            lse_cols[rows, :] = jnp.where(lane == h, m + jnp.log2(total), lse_cols[rows, :])

    def body(rows):
        att_ref[rows, :] = acc[rows, :].astype(bf16)

    row_loop(tokens, body)
    lse_ref[...] = lse_cols[...].T[:HEADS, :]


def attention_backward_kernel(
    h0, h1, base, done, q_ref, kn_ref, kf_ref, go_ref, lse_ref, del_ref, kid_ref, qid_ref, cin_ref,
    dq_ref, dkn_ref, dkf_ref, cout_ref, bias, acc
):
    tokens, width = q_ref.shape
    span = acc.shape[2]
    scale, unit = HD**-0.5 * LOG2E, HD**-0.5

    @pl.loop(0, 2 * tokens // ROWBLK)
    def _(r):
        rows = pl.ds(pl.multiple_of(r * ROWBLK, ROWBLK), ROWBLK)
        col = lax.broadcasted_iota(jnp.int32, (ROWBLK, tokens), 1)
        row = lax.broadcasted_iota(jnp.int32, (ROWBLK, tokens), 0) + r * ROWBLK
        allowed = (kid_ref[rows, 0:1] == qid_ref[0:1, :]) | (col == row)
        bias[rows, :] = jnp.where(allowed, 0.0, big_negative)

    @pl.loop(0, tokens // ROWBLK)
    def _(r):
        rows = pl.ds(pl.multiple_of(r * ROWBLK, ROWBLK), ROWBLK)
        for i in range(5):
            if base == 0:
                acc[i, rows, :] = jnp.zeros((ROWBLK, span), f32)
            else:
                acc[i, rows, 0:128] = cin_ref[i, rows, :]
                acc[i, rows, 128:span] = jnp.zeros((ROWBLK, span - 128), f32)

    @pl.loop(h0, h1)
    def _(h):
        w0, mask = head_window(h, width)
        win, winv = pl.ds(w0, WIN), pl.ds(w0 + width, WIN)
        at = pl.ds(pl.multiple_of(w0 - base, 128), WIN)
        zero = jnp.zeros((), bf16)
        qw = q_ref[:, win]
        qm, gm = jnp.where(mask, qw, zero), jnp.where(mask, go_ref[:, win], zero)
        lse, inner = lse_ref[pl.ds(h, 1), :], del_ref[pl.ds(h, 1), :]
        dq = None
        for b, kref in ((0, kn_ref), (1, kf_ref)):
            km, vw = jnp.where(mask, kref[:, win], zero), kref[:, winv]
            pt = jnp.exp2(nt(km, qw) * scale + bias[b * tokens : (b + 1) * tokens, :] - lse)
            acc[2 + 2 * b, :, at] += nn(pt.astype(bf16), gm)
            ds = (pt * (nt(vw, gm) - inner)).astype(bf16)
            acc[1 + 2 * b, :, at] += nn(ds, qm)
            part = tn(ds, km)
            dq = part if dq is None else dq + part
        acc[0, :, at] += dq

    if span == done:
        cout_ref[...] = jnp.zeros(cout_ref.shape, f32)

    @pl.loop(0, tokens // ROWBLK)
    def _(r):
        rows = pl.ds(pl.multiple_of(r * ROWBLK, ROWBLK), ROWBLK)
        dq_ref[rows, :] = (acc[0, rows, 0:done] * unit).astype(bf16)
        for b, out in ((0, dkn_ref), (1, dkf_ref)):
            out[rows, 0:done] = (acc[1 + 2 * b, rows, 0:done] * unit).astype(out.dtype)
            out[rows, done : 2 * done] = acc[2 + 2 * b, rows, 0:done].astype(out.dtype)
        for i in range(5):
            if span > done:
                cout_ref[i, rows, :] = acc[i, rows, done : done + 128]


def middle_kernel(att_ref, x_ref, cot_ref, vec_ref, w, mid_ref, n2_ref, n2t_ref, cott_ref, attt_ref, flipped):
    tokens, width = x_ref.shape
    transpose_ordered(cot_ref, flipped, cott_ref)
    transpose_ordered(att_ref, flipped, attt_ref)

    def body(cols):
        mid_ref[:, cols] = nn(att_ref[...], w[:, cols]) + vec_ref[4:5, cols] + x_ref[:, cols].astype(f32)

    column_tiles(width, body)

    def norm(rows):
        n2_ref[rows, :] = norm_rows(mid_ref[rows, :], vec_ref[5:6, 0:width], vec_ref[6:7, 0:width]).astype(bf16)

    row_loop(tokens, norm)
    transpose_ordered(n2_ref, flipped, n2t_ref)


def store_blocks(half, total, part, keep, send, cols):
    kept = (0, 2) if half == 0 else (0, 1)
    sent = (1, 3) if half == 0 else (2, 3)
    for i in range(2):
        keep[i, :, cols] = total[kept[i] * part : (kept[i] + 1) * part]
        send[i, :, cols] = total[sent[i] * part : (sent[i] + 1) * part]


def mlp_kernel(first, last, aliased, n2_ref, cot_ref, n2t_ref, cott_ref, b1_ref, vec_ref, outp_ref, gnp_ref, *rest):
    pieces = rest[:5]
    out_ref, gn_ref, ka_ref, sa_ref, kb_ref, sb_ref, gb1_ref, wbuf, acc, gacc, mine, theirs, came, sem, gsem, credit = (
        rest[9 if aliased else 5 :])
    t, steps = pl.program_id(0), pl.num_programs(0) - 1
    width = n2_ref.shape[1]
    tile, part = wbuf.shape[-1], width // 8
    half = width // 2
    slot = lax.rem(t, 2)
    before = 1 - slot

    def copies(step, to):
        cols = pl.ds(pl.multiple_of(step * tile, tile), tile)
        every = []
        for h in range(2):
            every += unit_copies(pieces, h, pl.ds(0, part), cols, shard_rows(wbuf.at[to, h], part), sem.at[to, h])
        return every

    def exchange(at, h):
        return to_sibling(theirs.at[at, h], came.at[at, h], gsem.at[at], h)

    @pl.when(t == 0)
    def _():
        meet_sibling()
        start_all(copies(0, 0))

        def init(rows):
            acc[rows, :] = outp_ref[rows, :] + vec_ref[7:8, 0:width] if first else outp_ref[rows, :]
            gacc[rows, :] = jnp.zeros((ROWBLK, width), f32) if first else gnp_ref[rows, :]

        row_loop(n2_ref.shape[0], init)

    @pl.when((t > 0) & (t < steps))
    def _():
        pl.semaphore_wait(credit, 1)

    @pl.when(t + 1 < steps)
    def _():
        start_all(copies(t + 1, before))

    @pl.when(t < steps)
    def _():
        wait_all(copies(t, slot))
        w1, w2 = wbuf[slot, 0], wbuf[slot, 1]
        u = nn(n2_ref[...], w1) + b1_ref[0:1, :]
        c0 = 0.7978845608028654
        th = jnp.tanh(c0 * (u + 0.044715 * u * u * u))
        active = (0.5 * u * (1.0 + th)).astype(bf16)
        slope = 0.5 * (1.0 + th) + 0.5 * u * (1.0 - th * th) * (c0 * (1.0 + 3 * 0.044715 * u * u))
        gh = (nn(cot_ref[...], w2) * slope).astype(bf16)
        gb1_ref[...] = jnp.sum(gh.astype(f32), axis=0, keepdims=True)
        g1 = nn(n2t_ref[...], gh).astype(bf16)
        mine[slot, 0], theirs[slot, 0] = g1[:half], g1[half:]
        exchange(slot, 0).start()
        g2 = nn(cott_ref[...], active).astype(bf16)
        mine[slot, 1], theirs[slot, 1] = g2[:half], g2[half:]
        exchange(slot, 1).start()
        acc[...] += nt(active, w2)
        gacc[...] += nt(gh, w1)

    @pl.when(t > 0)
    def _():
        for h, keep, send in ((0, ka_ref, sa_ref), (1, kb_ref, sb_ref)):
            exchange(before, h).wait()
            total = (mine[before, h].astype(f32) + came[before, h].astype(f32)).astype(bf16)
            store_blocks(h, total, part, keep, send, slice(None))

    @pl.when(t < steps - 1)
    def _():
        pl.semaphore_signal(credit, inc=1, device_id=sibling(), device_id_type=MESH)

    @pl.when(t == steps)
    def _():
        out_ref[...] = acc[...].astype(out_ref.dtype)
        gn_ref[...] = gacc[...]


def mlp_call(name, first, last, n2, cot, n2t, cott, b1, vec, outp, gnp, pieces, begin, total, into=None, collective=0):
    tokens, width = n2.shape
    cols, tile = pieces[0].shape[2], 256
    steps = cols // tile
    const = lambda a: pl.BlockSpec(a.shape, lambda t: (0,) * a.ndim, pipeline_mode=pl.Buffered(1))
    skip = 0 if into is None else (total - cols) // tile
    grads = pl.BlockSpec((2, width // 8, tile), lambda t: (0, 0, jnp.maximum(t - 1, 0) + skip))
    hidden = lambda t: jnp.minimum(t, steps - 1)
    args = (n2, cot, n2t, cott, b1, vec, outp, gnp, *pieces)
    grad = sds((2, width // 8, total), bf16)
    return pl.pallas_call(
        functools.partial(mlp_kernel, first, last, into is not None),
        grid=(steps + 1,),
        in_specs=[const(n2), const(cot), const(n2t), const(cott), pl.BlockSpec((8, tile), lambda t: (0, hidden(t) + begin // tile)),
                  const(vec), const(outp), const(gnp)] + [ANY] * (5 if into is None else 9),
        out_specs=(
            pl.BlockSpec((tokens, width), lambda t: (0, 0)),
            pl.BlockSpec((tokens, width), lambda t: (0, 0)),
            grads,
            grads,
            grads,
            grads,
            pl.BlockSpec((1, tile), lambda t: (0, hidden(t))),
        ),
        out_shape=(
            sds((tokens, width), bf16 if last else f32),
            sds((tokens, width), f32),
            grad,
            grad,
            grad,
            grad,
            sds((1, cols), f32),
        ),
        input_output_aliases={} if into is None else {len(args) + i: 2 + i for i in range(4)},
        scratch_shapes=[
            pltpu.VMEM((2, 2, width, tile), bf16),
            pltpu.VMEM((tokens, width), f32),
            pltpu.VMEM((tokens, width), f32),
            pltpu.VMEM((2, 2, width // 2, tile), bf16),
            pltpu.VMEM((2, 2, width // 2, tile), bf16),
            pltpu.VMEM((2, 2, width // 2, tile), bf16),
            pltpu.SemaphoreType.DMA((2, 2, 3, 4)),
            pltpu.SemaphoreType.DMA((2, 3, 2)),
            pltpu.SemaphoreType.REGULAR,
        ],
        compiler_params=pltpu.CompilerParams(collective_id=collective, has_side_effects=True),
        cost_estimate=pl.CostEstimate(
            flops=12 * tokens * width * cols, bytes_accessed=8 * width * cols + 12 * tokens * width, transcendentals=tokens * cols
        ),
        name=name,
    )(*args, *(() if into is None else into))


def norm_back(v, g, gain):
    center = v - jnp.mean(v, axis=-1, keepdims=True)
    rs = lax.rsqrt(jnp.mean(center * center, axis=-1, keepdims=True) + epsilon)
    n = center * rs
    e = g * gain
    grad = rs * (e - jnp.mean(e, axis=-1, keepdims=True) - n * jnp.mean(e * n, axis=-1, keepdims=True))
    return grad, g * n


def branch_kernel(cot_ref, gn_ref, mid_ref, vec_ref, att_ref, attt_ref, w, gm_ref, ga_ref, sums_ref, del_ref,
                  ka_ref, sa_ref, kb_ref, sb_ref, gb, mine, theirs, came, sem):
    tokens, width = cot_ref.shape
    meet_sibling()
    sums_ref[...] = jnp.zeros(sums_ref.shape, f32)

    def body(rows):
        cot = cot_ref[rows, :].astype(f32)
        g = gn_ref[rows, :]
        grad, gain_part = norm_back(mid_ref[rows, :], g, vec_ref[5:6, 0:width])
        gm = cot + grad
        gm_ref[rows, :] = gm
        low = gm.astype(bf16)
        gb[rows, :] = low
        sums_ref[0:1, :] += jnp.sum(gain_part, axis=0, keepdims=True)
        sums_ref[1:2, :] += jnp.sum(g, axis=0, keepdims=True)
        sums_ref[2:3, :] += jnp.sum(low.astype(f32), axis=0, keepdims=True)
        sums_ref[3:4, :] += jnp.sum(cot, axis=0, keepdims=True)

    row_loop(tokens, body)
    half, part = width // 2, mine.shape[-1]
    exchanges = [to_sibling(theirs.at[i], came.at[i], sem, i) for i in range(2)]
    for i in range(2):
        at = i * (width - part)
        g = nn(attt_ref[...], gb[:, at : at + part]).astype(bf16)
        mine[i], theirs[i] = g[:half], g[half:]
        exchanges[i].start()
    column = lax.broadcasted_iota(jnp.int32, (HEADS, 128), 1)
    first = lax.broadcasted_iota(jnp.int32, (HEADS, 128), 0) * HD
    del_ref[...] = jnp.zeros(del_ref.shape, f32)

    @pl.loop(0, width // 128)
    def _(j):
        cols = pl.ds(pl.multiple_of(j * 128, 128), 128)
        ga = nt(gb[...], w[cols, :]).astype(bf16)
        ga_ref[:, cols] = ga
        prod = ga.astype(f32) * att_ref[:, cols].astype(f32)
        high = prod.astype(bf16)
        rest_low = (prod - high.astype(f32)).astype(bf16)
        at = column + j * 128
        chosen = jnp.where((at >= first) & (at < first + HD), 1.0, 0.0).astype(bf16)
        del_ref[...] += nt(chosen, high) + nt(chosen, rest_low)

    for i, keep, send in ((0, ka_ref, sa_ref), (1, kb_ref, sb_ref)):
        exchanges[i].wait()
        store_blocks(i, (mine[i].astype(f32) + came[i].astype(f32)).astype(bf16), width // 8, keep, send, slice(None))


def qkv_grad_kernel(nt_ref, dq_ref, dko_ref, dkr_ref, all_ref, ka_ref, sa_ref, kb_ref, sb_ref, mine, theirs, came, sem):
    tokens, width = dq_ref.shape
    half, part = nt_ref.shape[0] // 2, mine.shape[-1]
    meet_sibling()

    def join(rows):
        all_ref[rows, 0:width] = dq_ref[rows, :]
        all_ref[rows, width : 3 * width] = (dko_ref[rows, :] + dkr_ref[rows, :].astype(f32)).astype(bf16)

    row_loop(tokens, join)
    exchanges = [to_sibling(theirs.at[i], came.at[i], sem, i) for i in range(2)]
    for i in range(2):

        @pl.loop(0, part // 256)
        def _(t):
            cols = pl.ds(pl.multiple_of(t * 256, 256), 256)
            at = pl.ds(pl.multiple_of(t * 256 + i * (3 * width - part), 128), 256)
            g = nn(nt_ref[...], all_ref[:, at]).astype(bf16)
            mine[i, :, cols], theirs[i, :, cols] = g[:half], g[half:]

        exchanges[i].start()

    for i, keep, send in ((0, ka_ref, sa_ref), (1, kb_ref, sb_ref)):
        exchanges[i].wait()

        @pl.loop(0, part // 256)
        def _(t):
            cols = pl.ds(pl.multiple_of(t * 256, 256), 256)
            total = (mine[i, :, cols].astype(f32) + came[i, :, cols].astype(f32)).astype(bf16)
            store_blocks(i, total, half // 4, keep, send, cols)


def normed_grad_kernel(g1_ref, g2_ref, wq_ref, wkv_ref, gn_ref, sums_ref, w, sem):
    tokens, width = gn_ref.shape
    a, b = g1_ref.shape[1] // 3, g2_ref.shape[1] // 3
    copies = [pltpu.make_async_copy(wq_ref, w.at[0], sem.at[0]), pltpu.make_async_copy(wkv_ref, w.at[pl.ds(1, 2)], sem.at[1])]
    start_all(copies)
    sums_ref[...] = jnp.zeros(sums_ref.shape, f32)

    def body(rows):
        for i, j in ((0, 0), (1, 2)):
            sums_ref[i : i + 1, 0:a] += jnp.sum(g1_ref[rows, j * a : (j + 1) * a].astype(f32), axis=0, keepdims=True)
            sums_ref[i : i + 1, a:width] += jnp.sum(g2_ref[rows, j * b : (j + 1) * b].astype(f32), axis=0, keepdims=True)

    row_loop(tokens, body)
    for c in copies:
        c.wait()

    def columns(cols):
        total = None
        for i in range(3):
            for g, lo, hi in ((g1_ref, 0, a), (g2_ref, a, width)):
                term = nt(g[:, i * (hi - lo) : (i + 1) * (hi - lo)], w[i, cols, lo:hi])
                total = term if total is None else total + term
        gn_ref[:, cols] = total

    column_tiles(width, columns)


def input_grad_kernel(gn_ref, x_ref, gm_ref, vec_ref, gx_ref, sums_ref):
    tokens, width = x_ref.shape
    sums_ref[...] = jnp.zeros(sums_ref.shape, f32)

    def body(rows):
        g = gn_ref[rows, :]
        grad, gain_part = norm_back(x_ref[rows, :].astype(f32), g, vec_ref[0:1, 0:width])
        gx_ref[rows, :] = (gm_ref[rows, :] + grad).astype(bf16)
        sums_ref[0:1, :] += jnp.sum(gain_part, axis=0, keepdims=True)
        sums_ref[1:2, :] += jnp.sum(g, axis=0, keepdims=True)

    row_loop(tokens, body)


def call(body, name, outs, scratch, flops, moved, *args, pieces=(), collective=None, far_outs=0):
    params = {} if collective is None else {"collective_id": collective, "has_side_effects": True}
    return pl.pallas_call(
        body,
        out_shape=tuple(sds(s, t) for s, t in outs),
        in_specs=[VM] * len(args) + [ANY] * len(pieces),
        out_specs=(VM,) * (len(outs) - far_outs) + (ANY,) * far_outs,
        compiler_params=pltpu.CompilerParams(**params),
        scratch_shapes=scratch,
        cost_estimate=pl.CostEstimate(flops=flops, bytes_accessed=moved, transcendentals=0),
        name=name,
    )(*args, *pieces)


def swap(v, mask, size):
    return lax.ppermute(v, "dp", [(i, i ^ mask) for i in range(size)])


def after(v, *others):
    return lax.optimization_barrier((v, *others))[0]


def sums_kernel(shape, *refs):
    terms, outs, at = refs[: sum(map(sum, shape))], refs[sum(map(sum, shape)) :], 0
    for out, counts in zip(outs, shape):
        for k, count in enumerate(counts):
            total = terms[at][...].astype(f32)
            for r in terms[at + 1 : at + count]:
                total = total + r[...].astype(f32)
            out[k] = total.astype(bf16)
            at += count


def add_blocks(name, *outs):
    first = outs[0][0][0][0]
    rows, cols = first.shape[-2:]
    tile = max(t for t in range(128, 1025, 128) if cols % t == 0)
    specs, args = [], []
    for out in outs:
        for terms in out:
            for array, index in terms:
                specs.append(pl.BlockSpec((None,) * len(index) + (rows, tile), lambda t, index=index: (*index, 0, t)))
                args.append(array)
    count = sum(len(out) for out in outs)
    return pl.pallas_call(
        functools.partial(sums_kernel, [[len(terms) for terms in out] for out in outs]),
        grid=(cols // tile,),
        in_specs=specs,
        out_specs=tuple(pl.BlockSpec((len(out), rows, tile), lambda t: (0, 0, t)) for out in outs),
        out_shape=tuple(sds((len(out), rows, cols), bf16) for out in outs),
        cost_estimate=pl.CostEstimate(flops=len(args) * rows * cols, bytes_accessed=2 * (len(args) + count) * rows * cols, transcendentals=0),
        name=name,
    )(*args)


def reduce_small(rows, size):
    d = lax.axis_index("dp")
    bit, left = 1, rows
    while bit < size:
        pairs = left.reshape(left.shape[0] // 2, 2, -1)
        up = (d // bit) % 2 == 1
        mine = jnp.where(up, pairs[:, 1], pairs[:, 0])
        other = jnp.where(up, pairs[:, 0], pairs[:, 1])
        left = mine + swap(other.astype(bf16), bit, size).astype(f32)
        bit *= 2
    for mask in (1, 2):
        low = left.astype(bf16)
        left = low.astype(f32) + lax.ppermute(low, "seq", [(i, i ^ mask) for i in range(4)]).astype(f32)
    return left[0]


def token_routes(size, depth):
    routes = []
    for s in range(2):
        perm = []
        for d in range(size):
            for z in range(depth):
                j = (z & 1) ^ s
                to_d, to_z = (d & ~1) | (z >> 1), 2 * (d & 1) + j
                perm.append((d * depth + z, to_d * depth + to_z))
        routes.append(perm)
    return routes


def to_rows(v, routes):
    odd = lax.axis_index("seq") % 2 == 1
    first = jnp.where(odd, v[1], v[0])
    second = jnp.where(odd, v[0], v[1])
    r0 = lax.ppermute(first, ("dp", "seq"), routes[0])
    r1 = lax.ppermute(second, ("dp", "seq"), routes[1])
    return jnp.concatenate([jnp.where(odd, r1, r0), jnp.where(odd, r0, r1)], axis=0)


def from_rows(v, routes):
    odd = lax.axis_index("seq") % 2 == 1
    half = v.shape[0] // 2
    t0, t1 = v[:half], v[half:]
    back = [[(b, a) for a, b in perm] for perm in routes]
    r0 = lax.ppermute(jnp.where(odd, t1, t0), ("dp", "seq"), back[0])
    r1 = lax.ppermute(jnp.where(odd, t0, t1), ("dp", "seq"), back[1])
    return jnp.stack([jnp.where(odd, r1, r0), jnp.where(odd, r0, r1)])


class Order:
    def __init__(self):
        self.tail, self.meetings = None, 0

    def gate(self, v):
        return v if self.tail is None else after(v, self.tail)

    def call(self, body, name, outs, scratch, flops, moved, first, *args, pieces=(), meets=False, far_outs=0):
        self.meetings += meets
        got = call(body, name, outs, scratch, flops, moved, self.gate(first), *args, pieces=pieces,
                   collective=self.meetings if meets else None, far_outs=far_outs)
        self.tail = got[0]
        return got

    def mlp(self, name, first, last, n2, *args, **named):
        self.meetings += 1
        got = mlp_call(name, first, last, self.gate(n2), *args, collective=self.meetings, **named)
        self.tail = got[2]
        return got

    def add(self, name, *outs):
        (array, index), *terms = outs[0][0]
        outs = ([[(self.gate(array), index), *terms], *outs[0][1:]], *outs[1:])
        got = add_blocks(name, *outs)
        self.tail = got[0]
        return got


class Reduction:
    def __init__(self, name, order, size, keep_a, send_a, keep_b, send_b):
        self.name, self.order, self.size = name, order, size
        self.a, self.b = keep_a, keep_b
        self.ax, self.by = swap(send_a, 2, size), swap(send_b, 4, size)

    def second(self):
        ta, tb = self.order.add(
            "second" + self.name, [[(self.a, (1,)), (self.ax, (1,))]], [[(self.b, (1,)), (self.by, (1,))]]
        )
        self.ay, self.bx = swap(ta, 4, self.size), swap(tb, 2, self.size)

    def third(self):
        a = [(self.a, (0,)), (self.ax, (0,)), (self.ay, (0,))]
        b = [(self.b, (0,)), (self.by, (0,)), (self.bx, (0,))]
        self.own = self.order.add("third" + self.name, [a, b])[0]
        self.inner = lax.ppermute(self.own, "seq", [(0, 1), (3, 2)])

    def add_pair(self, name, a, b):
        return self.order.add(name + self.name, [[(a, (i,)), (b, (i,))] for i in range(2)])[0]

    def fourth(self):
        self.half = self.add_pair("inner", self.own, self.inner)
        self.across = lax.ppermute(self.half, "seq", [(1, 2), (2, 1)])

    def fifth(self):
        self.total = self.add_pair("total", self.half, self.across)
        self.outer = lax.ppermute(self.total, "seq", [(1, 0), (2, 3)])

    def result(self):
        z = lax.axis_index("seq")
        return jnp.where((z == 1) | (z == 2), self.total, self.order.gate(self.outer)).astype(f32)


def by_rows(size, depth):
    def step(patches, picture_ids, valid_mask, ln1_gain, ln1_bias, w_qkv, bias_qv, w_out, b_out, ln2_gain, ln2_bias,
             w_fc1, b_fc1, w_fc2, b_fc2, cotangent):
        width = patches.shape[-1]
        ff = w_fc1.shape[1]
        tokens = patches.shape[0] * patches.shape[1]
        part = width // size
        z, core = lax.axis_index("seq"), lax.axis_index("dp") % 2
        routes = token_routes(size, depth)
        order = Order()
        vm = pltpu.VMEM
        act, flip = ((tokens, width), bf16), ((width, tokens), bf16)
        act32 = ((tokens, width), f32)
        mm = 2 * tokens * width * width

        small = jnp.stack([ln1_gain, ln1_bias, bias_qv[0], bias_qv[1], b_out, ln2_gain, ln2_bias, b_fc2])
        small = jnp.pad(small, ((0, 8), (0, width - part)))
        bias = jnp.pad(b_fc1[None], ((0, 15), (0, width - ff // size)))
        unit0 = jnp.stack([
            jnp.concatenate([w_qkv[:, width : 2 * width], small]), jnp.concatenate([w_qkv[:, 2 * width :], bias])])
        unit1 = jnp.stack([w_qkv[:, :width], w_out])
        extra = -ff % 256
        tiles = (ff + extra) // 256
        ends = [0, tiles // 2 * 256, (tiles - tiles // 5) * 256, tiles * 256]
        w1 = jnp.pad(w_fc1, ((0, 0), (0, extra)))
        w2 = jnp.pad(w_fc2.T, ((0, 0), (0, extra)))
        hidden_units = [jnp.stack([w1[:, a:b], w2[:, a:b]]) for a, b in zip(ends, ends[1:])]

        def straight(unit):
            return swap(unit, 2, size), swap(unit, 4, size)

        def corner(x, y):
            return swap(y[0], 2, size), swap(x[1], 4, size)

        x0, y0 = straight(unit0)
        x = to_rows(patches, routes)
        unit1, y0a, x0b = lax.optimization_barrier((unit1, y0[0], x0[1]))
        p0 = (unit0, x0, y0, swap(y0a, 2, size), swap(x0b, 4, size))
        x1, y1 = straight(unit1)

        ids = jnp.stack([picture_ids, jnp.where(valid_mask == 1, picture_ids, -1)])
        far_ids = swap(ids, 1, size)
        ids = jnp.where(z // 2 == core, ids, far_ids)
        ids = jnp.where(z % 2 == 1, ids[:, 1], ids[:, 0]).reshape(2, 2, tokens)
        near = jnp.where(core == 1, ids[:, 1], ids[:, 0])
        far = jnp.where(core == 1, ids[:, 0], ids[:, 1])
        keys = jnp.concatenate([near[1], far[1]])
        qid_row, qid_col = jnp.broadcast_to(near[0][None], (8, tokens)), jnp.broadcast_to(near[0][:, None], (tokens, 128))
        kid_row, kid_col = jnp.broadcast_to(keys[None], (8, 2 * tokens)), jnp.broadcast_to(keys[:, None], (2 * tokens, 128))

        dma = pltpu.SemaphoreType.DMA
        n, kv, vec, b1, w_kv = order.call(
            functools.partial(kv_kernel, ff), "kv",
            [act, ((tokens, 2 * width), bf16), ((16, width), f32), ((16, ff + extra), f32), ((2, width, width), bf16)],
            [vm((2, width, width), bf16), vm((2, 8, 16, width), bf16), dma((4, 3, 4)), dma],
            2 * mm, 4 * width * width, x, pieces=p0, meets=True, far_outs=1)
        far_kv = swap(kv, 1, size)
        x1, y1 = order.gate(x1), order.gate(y1)
        p1 = (unit1, x1, y1, *corner(x1, y1))
        unit2, unit3, unit4 = hidden_units
        unit2 = after(unit2, x1, y1)
        x2, y2 = straight(unit2)
        cot = to_rows(order.gate(cotangent), routes)
        q, nt_, w_q, w_o = order.call(
            q_kernel, "q", [act, flip, ((width, width), bf16), ((width, width), bf16)],
            [vm((2, width, width), bf16), vm((width, tokens), bf16), dma((2, 3, 4)), dma((2,))],
            mm, 2 * width * width, n, vec, pieces=p1, meets=True, far_outs=2)
        sc = 2 * tokens * 2 * tokens * WIN * HEADS
        att, lse = order.call(
            attention_forward_kernel, "attention_forward", [act, ((HEADS, tokens), f32)],
            [vm((tokens, 2 * tokens), f32), vm((tokens, width), f32), vm((tokens, 128), f32)],
            3 * sc, 8 * tokens * width, q, kv, far_kv, qid_col, kid_row)
        x2, y2 = order.gate(x2), order.gate(y2)
        p2 = (unit2, x2, y2, *corner(x2, y2))
        unit3 = after(unit3, x2, y2)
        x3, y3 = straight(unit3)
        mid, n2, n2t, cott, attt = order.call(
            middle_kernel, "middle", [act32, act, flip, flip, flip],
            [vm((width, tokens), bf16)], mm, 2 * width * width, att, x, cot, vec, w_o)

        args = (cot, n2t, cott)
        acc, gn, *grads1, gb1 = order.mlp("mlp0", True, False, n2, *args, b1, vec, mid, mid, p2, 0, ends[1])
        x3, y3 = order.gate(x3), order.gate(y3)
        p3 = (unit3, x3, y3, *corner(x3, y3))
        unit4 = after(unit4, x3, y3)
        x4, y4 = straight(unit4)
        rest_cols = ends[3] - ends[1]
        acc, gn, *grads2, gb2 = order.mlp("mlp1", False, False, n2, *args, b1, vec, acc, gn, p3, ends[1], rest_cols)
        x4, y4 = order.gate(x4), order.gate(y4)
        p4 = (unit4, x4, y4, *corner(x4, y4))
        r1 = Reduction("1", order, size, *grads1)
        out, gn, *grads2, gb3 = order.mlp(
            "mlp2", False, True, n2, *args, b1, vec, acc, gn, p4, ends[2], rest_cols, into=grads2)
        layer_out = from_rows(out, routes)

        part_o = (width // 256 + 1) * 128

        def gradient(columns):
            return [((2, part, columns), bf16)] * 4

        def exchanged(columns):
            return [vm((2, width // 2, columns), bf16)] * 3 + [dma((3, 2))]

        gm, ga, sums2, inner, *gradso = order.call(
            branch_kernel, "branch", [act32, act, ((8, width), f32), ((HEADS, tokens), f32), *gradient(part_o)],
            [vm((tokens, width), bf16), *exchanged(part_o)], 2 * mm, 4 * width * width,
            cot, gn, mid, vec, att, attt, w_o, meets=True)
        cut_head = (HEADS + 2) // 2
        cut_col = cut_head * HD // 128 * 128

        def attention_backward(name, h0, h1, base, done, span, carry):
            share = 3 * sc * (h1 - h0) // HEADS * 2
            return order.call(
                functools.partial(attention_backward_kernel, h0, h1, base, done), name,
                [((tokens, done), bf16), ((tokens, 2 * done), f32), ((tokens, 2 * done), bf16),
                 ((5, tokens if span > done else 8, 128), f32)],
                [vm((2 * tokens, tokens), f32), vm((5, tokens, span), f32)],
                share, 16 * tokens * width, q, kv, far_kv, ga, lse, inner, kid_col, qid_row, carry)

        def qkv_grad(name, dq, dkn, dkr):
            columns = 3 * dq.shape[1]
            share = (columns + 511) // 512 * 256
            got, *grads = order.call(
                qkv_grad_kernel, name, [((tokens, columns), bf16), *gradient(share)], exchanged(share),
                mm * columns // width, 4 * width * columns, nt_, dq, dkn, dkr, meets=True)
            return got, grads

        dqa, dna, dfa, carry = attention_backward("attention_backward_a", 0, cut_head, 0, cut_col, cut_col + 128, inner)
        dra = swap(dfa, 1, size)
        r1.second()
        r2 = Reduction("2", order, size, *grads2)
        gra, gradsa = qkv_grad("qkv_grad_a", dqa, dna, dra)
        dqb, dnb, dfb, _ = attention_backward(
            "attention_backward_b", cut_head, HEADS, cut_col, width - cut_col, width - cut_col, carry)
        drb = swap(dfb, 1, size)
        r1.third()
        r2.second()
        ro = Reduction("o", order, size, *gradso)
        qa = Reduction("qa", order, size, *gradsa)
        grb, gradsb = qkv_grad("qkv_grad_b", dqb, dnb, drb)
        qb = Reduction("qb", order, size, *gradsb)
        gnq, sums0 = order.call(
            normed_grad_kernel, "normed_grad", [act32, ((8, width), f32)],
            [vm((3, width, width), bf16), dma((2,))], 3 * mm, 6 * width * width, gra, grb, pieces=(w_q, w_kv))
        r1.fourth()
        r2.third()
        gx, sums1 = order.call(input_grad_kernel, "input_grad", [act, ((8, width), f32)], [], 10**7, 12 * tokens * width,
                               gnq, x, gm, vec)
        gx_rows = (gx, routes)
        ro.second()
        qa.second()
        r1.fifth()
        r2.fourth()
        qb.second()
        ro.third()
        qa.third()
        grad_patches = from_rows(*gx_rows)
        bias_grads = jnp.concatenate([gb1, gb2, gb3], axis=1)[:, :ff].reshape(size, ff // size)
        vecs = jnp.concatenate([sums1[:2], sums0[:2], sums2[:4]]).reshape(8, size, part)
        tiny = reduce_small(jnp.concatenate([jnp.moveaxis(vecs, 0, 1).reshape(size, 8 * part), bias_grads], axis=1), size)
        mine, grad_b_fc1 = tiny[: 8 * part].reshape(8, part), tiny[8 * part :]
        r2.fifth()
        qb.third()
        ro.fourth()
        qa.fourth()
        ro.fifth()
        qa.fifth()
        qb.fourth()
        qb.fifth()
        g1, g2, go, ga_, gb_ = [r.result() for r in (r1, r2, ro, qa, qb)]
        left = ff - ends[1]
        w1g = jnp.concatenate([g1[0], g2[0][:, :left]], axis=1)
        w2g = jnp.concatenate([g1[1], g2[1][:, :left]], axis=1).T
        wog = jnp.concatenate([go[0], go[1][:, 2 * part_o - width :]], axis=1)

        def joined(g, columns):
            return jnp.concatenate([g[0], g[1][:, 2 * g.shape[2] - columns :]], axis=1).reshape(part, 3, columns // 3)

        wqg = jnp.concatenate([joined(ga_, 3 * cut_col), joined(gb_, 3 * (width - cut_col))], axis=2).reshape(part, 3 * width)
        return (layer_out, grad_patches, mine[0], mine[1], wqg, mine[2:4], wog, mine[6], mine[4], mine[5], w1g, grad_b_fc1, w2g, mine[7])

    return step


def fits_rows(mesh, patches):
    return mesh.shape["dp"] == 8 and mesh.shape["seq"] == 4


def solution(mesh):
    placed = (
        P("dp", "seq", None),
        P("dp", None),
        P("dp", None),
        P("dp"),
        P("dp"),
        P("dp", None),
        P(None, "dp"),
        P("dp", None),
        P("dp"),
        P("dp"),
        P("dp"),
        P("dp", None),
        P("dp"),
        P(None, "dp"),
        P("dp"),
        P("dp", "seq", None),
    )
    return jax.shard_map(
        by_rows(mesh.shape["dp"], mesh.shape["seq"]) if fits_rows(mesh, None) else per_device,
        mesh=mesh,
        in_specs=placed,
        out_specs=(
            P("dp", "seq", None),
            P("dp", "seq", None),
            P("dp"),
            P("dp"),
            P("dp", None),
            P(None, "dp"),
            P("dp", None),
            P("dp"),
            P("dp"),
            P("dp"),
            P("dp", None),
            P("dp"),
            P(None, "dp"),
            P("dp"),
        ),
        check_vma=False,
    )
```

```python
import functools

import jax
import jax.numpy as jnp
from jax import lax
from jax.experimental import pallas as pl
from jax.experimental.pallas import tpu as pltpu
from jax.sharding import PartitionSpec as P

HEADS = 16
HD = 72


epsilon = 1e-06
big_negative = -1e30


def layer_norm(values, scales, offset):
    center = values - jnp.mean(values, axis=-1, keepdims=True)
    spread = jnp.mean(center * center, axis=-1, keepdims=True)
    return center * lax.rsqrt(spread + epsilon) * scales + offset


def gelu_tanh(values):
    return (
        0.5
        * values
        * (1.0 + jnp.tanh(0.7978845608028654 * (values + 0.044715 * values * values * values)))
    )


def contract_rows(left, right):
    return lax.dot_general(
        left, right, (((0,), (0,)), ((), ())), preferred_element_type=jnp.float32
    )


def contract_cols(left, right):
    return lax.dot_general(
        left, right, (((1,), (1,)), ((), ())), preferred_element_type=jnp.float32
    )


def gather_weights(
    ln1_gain, ln1_bias, w_qkv, bias_qv, w_out, b_out, ln2_gain, ln2_bias, w_fc1, b_fc1, w_fc2, b_fc2
):
    return (
        lax.all_gather(ln1_gain, "dp", axis=0, tiled=True),
        lax.all_gather(ln1_bias, "dp", axis=0, tiled=True),
        lax.all_gather(w_qkv, "dp", axis=0, tiled=True),
        lax.all_gather(bias_qv, "dp", axis=1, tiled=True),
        lax.all_gather(w_out, "dp", axis=0, tiled=True),
        lax.all_gather(b_out, "dp", axis=0, tiled=True),
        lax.all_gather(ln2_gain, "dp", axis=0, tiled=True),
        lax.all_gather(ln2_bias, "dp", axis=0, tiled=True),
        lax.all_gather(w_fc1, "dp", axis=0, tiled=True),
        lax.all_gather(b_fc1, "dp", axis=0, tiled=True),
        lax.all_gather(w_fc2, "dp", axis=1, tiled=True),
        lax.all_gather(b_fc2, "dp", axis=0, tiled=True),
    )


def block_scores(queries, key_vectors, picture_ids, valid_mask, first_row, block_rows):
    length = picture_ids.shape[1]
    query_block = lax.dynamic_slice_in_dim(queries, first_row, block_rows, 1)
    ids_block = lax.dynamic_slice_in_dim(picture_ids, first_row, block_rows, 1)
    same_picture = (ids_block[:, :, None] == picture_ids[:, None, :]) & (
        valid_mask[:, None, :] == 1
    )
    diagonal = (first_row + jnp.arange(block_rows))[:, None] == jnp.arange(length)[None, :]
    allowed = (same_picture | diagonal[None])[:, None]
    scaling = queries.shape[-1] ** (-0.5)
    scores = (
        jnp.einsum("rqhe,rkhe->rhqk", query_block, key_vectors, preferred_element_type=jnp.float32)
        * scaling
    )
    return (query_block, jnp.where(allowed, scores, big_negative))


def attention_forward(queries, key_vectors, value_vectors, picture_ids, valid_mask):
    row_count, length, head_count, head_size = queries.shape
    block_rows = min(512, length)

    def one_block(block_index):
        query_block, scores = block_scores(
            queries, key_vectors, picture_ids, valid_mask, block_index * block_rows, block_rows
        )
        row_max = jnp.max(scores, axis=-1, keepdims=True)
        exp_terms = jnp.exp(scores - row_max)
        totals = jnp.sum(exp_terms, axis=-1, keepdims=True)
        probs_low = (exp_terms / totals).astype(jnp.bfloat16)
        mixing = jnp.einsum(
            "rhqk,rkhe->rqhe", probs_low, value_vectors, preferred_element_type=jnp.float32
        )
        return (mixing.astype(jnp.bfloat16), (row_max + jnp.log(totals))[..., 0])

    outputs, log_sums = lax.map(one_block, jnp.arange(length // block_rows))
    outputs = jnp.moveaxis(outputs, 0, 1).reshape(row_count, length, head_count, head_size)
    log_sums = jnp.moveaxis(log_sums, 0, 2).reshape(row_count, head_count, length)
    return (outputs, log_sums)


def attention_backward(
    queries, key_vectors, value_vectors, log_sums, grad_heads, picture_ids, valid_mask
):
    row_count, length, head_count, head_size = queries.shape
    block_rows = min(512, length)
    scaling = head_size ** (-0.5)

    def one_block(running, block_index):
        grad_keys, grad_values = running
        first_row = block_index * block_rows
        query_block, scores = block_scores(
            queries, key_vectors, picture_ids, valid_mask, first_row, block_rows
        )
        lse_block = lax.dynamic_slice_in_dim(log_sums, first_row, block_rows, 2)
        attn_probs = jnp.exp(scores - lse_block[..., None])
        grad_block = lax.dynamic_slice_in_dim(grad_heads, first_row, block_rows, 1)
        grad_values = grad_values + jnp.einsum(
            "rhqk,rqhe->rkhe",
            attn_probs.astype(jnp.bfloat16),
            grad_block,
            preferred_element_type=jnp.float32,
        )
        grad_probs = jnp.einsum(
            "rqhe,rkhe->rhqk", grad_block, value_vectors, preferred_element_type=jnp.float32
        )
        inner = jnp.sum(attn_probs * grad_probs, axis=-1, keepdims=True)
        grad_scores = (attn_probs * (grad_probs - inner)).astype(jnp.bfloat16)
        grad_query = (
            jnp.einsum(
                "rhqk,rkhe->rqhe", grad_scores, key_vectors, preferred_element_type=jnp.float32
            )
            * scaling
        )
        grad_keys = (
            grad_keys
            + jnp.einsum(
                "rhqk,rqhe->rkhe", grad_scores, query_block, preferred_element_type=jnp.float32
            )
            * scaling
        )
        return ((grad_keys, grad_values), grad_query)

    zeros_start = jnp.zeros(queries.shape, jnp.float32)
    (grad_keys, grad_values), grad_queries = lax.scan(
        one_block, (zeros_start, zeros_start), jnp.arange(length // block_rows)
    )
    grad_queries = jnp.moveaxis(grad_queries, 0, 1).reshape(
        row_count, length, head_count, head_size
    )
    return (grad_queries, grad_keys, grad_values)


def forward_pass(patches, picture_ids, valid_mask, gathered):
    (
        ln1_gain,
        ln1_bias,
        w_qkv,
        bias_qv,
        w_out,
        b_out,
        ln2_gain,
        ln2_bias,
        w_fc1,
        b_fc1,
        w_fc2,
        b_fc2,
    ) = gathered
    row_count, local_len, model_width = patches.shape
    inputs = patches.astype(jnp.float32).reshape(row_count * local_len, model_width)
    normed = layer_norm(inputs, ln1_gain.astype(jnp.float32), ln1_bias.astype(jnp.float32)).astype(
        jnp.bfloat16
    )
    projected = jnp.dot(normed, w_qkv, preferred_element_type=jnp.float32)
    bias_full = jnp.concatenate([bias_qv[0], jnp.zeros_like(bias_qv[0]), bias_qv[1]]).astype(
        jnp.float32
    )
    projected = (
        (projected + bias_full).astype(jnp.bfloat16).reshape(row_count, local_len, 3, HEADS, HD)
    )
    by_heads = lax.all_to_all(projected, "seq", split_axis=3, concat_axis=1, tiled=True)
    queries = by_heads[:, :, 0]
    key_vectors = by_heads[:, :, 1]
    value_vectors = by_heads[:, :, 2]
    mixing, log_sums = attention_forward(
        queries, key_vectors, value_vectors, picture_ids, valid_mask
    )
    token_mixing = lax.all_to_all(mixing, "seq", split_axis=1, concat_axis=2, tiled=True)
    attended = token_mixing.reshape(row_count * local_len, model_width)
    middle = (
        inputs
        + jnp.dot(attended, w_out, preferred_element_type=jnp.float32)
        + b_out.astype(jnp.float32)
    )
    normed_two = layer_norm(
        middle, ln2_gain.astype(jnp.float32), ln2_bias.astype(jnp.float32)
    ).astype(jnp.bfloat16)
    hidden = jnp.dot(normed_two, w_fc1, preferred_element_type=jnp.float32) + b_fc1.astype(
        jnp.float32
    )
    active = gelu_tanh(hidden).astype(jnp.bfloat16)
    outputs = (
        middle
        + jnp.dot(active, w_fc2, preferred_element_type=jnp.float32)
        + b_fc2.astype(jnp.float32)
    )
    layer_out = outputs.astype(jnp.bfloat16).reshape(row_count, local_len, model_width)
    kept_values = (
        inputs,
        normed,
        queries,
        key_vectors,
        value_vectors,
        log_sums,
        attended,
        middle,
        normed_two,
        hidden,
        active,
    )
    return (layer_out, kept_values)


def backward_pass(cotangent, picture_ids, valid_mask, gathered, kept_values):
    (
        ln1_gain,
        ln1_bias,
        w_qkv,
        bias_qv,
        w_out,
        b_out,
        ln2_gain,
        ln2_bias,
        w_fc1,
        b_fc1,
        w_fc2,
        b_fc2,
    ) = gathered
    (
        inputs,
        normed,
        queries,
        key_vectors,
        value_vectors,
        log_sums,
        attended,
        middle,
        normed_two,
        hidden,
        active,
    ) = kept_values
    row_count, local_len, model_width = cotangent.shape
    grad_z = cotangent.reshape(row_count * local_len, model_width)
    grad_w_fc2 = contract_rows(active, grad_z)
    grad_b_fc2 = jnp.sum(grad_z.astype(jnp.float32), axis=0)
    grad_active = contract_cols(grad_z, w_fc2)
    grad_hidden = jax.vjp(gelu_tanh, hidden)[1](grad_active)[0].astype(jnp.bfloat16)
    grad_w_fc1 = contract_rows(normed_two, grad_hidden)
    grad_b_fc1 = jnp.sum(grad_hidden.astype(jnp.float32), axis=0)
    grad_normed_two = contract_cols(grad_hidden, w_fc1)
    norm_pull = jax.vjp(
        layer_norm, middle, ln2_gain.astype(jnp.float32), ln2_bias.astype(jnp.float32)
    )[1]
    grad_middle, grad_ln2_gain, grad_ln2_bias = norm_pull(grad_normed_two)
    grad_middle = grad_middle + grad_z.astype(jnp.float32)
    grad_branch = grad_middle.astype(jnp.bfloat16)
    grad_w_out = contract_rows(attended, grad_branch)
    grad_b_out = jnp.sum(grad_branch.astype(jnp.float32), axis=0)
    grad_attended = (
        contract_cols(grad_branch, w_out)
        .astype(jnp.bfloat16)
        .reshape(row_count, local_len, HEADS, HD)
    )
    grad_heads = lax.all_to_all(grad_attended, "seq", split_axis=2, concat_axis=1, tiled=True)
    grad_queries, grad_keys, grad_values = attention_backward(
        queries, key_vectors, value_vectors, log_sums, grad_heads, picture_ids, valid_mask
    )
    grad_proj = jnp.stack([grad_queries, grad_keys, grad_values], axis=2).astype(jnp.bfloat16)
    grad_tokens = lax.all_to_all(grad_proj, "seq", split_axis=1, concat_axis=3, tiled=True).reshape(
        row_count * local_len, 3 * model_width
    )
    grad_w_qkv = contract_rows(normed, grad_tokens)
    column_sums = jnp.sum(grad_tokens.astype(jnp.float32), axis=0)
    grad_bias_qv = jnp.stack([column_sums[:model_width], column_sums[2 * model_width :]])
    grad_normed = contract_cols(grad_tokens, w_qkv)
    first_pull = jax.vjp(
        layer_norm, inputs, ln1_gain.astype(jnp.float32), ln1_bias.astype(jnp.float32)
    )[1]
    grad_inputs, grad_ln1_gain, grad_ln1_bias = first_pull(grad_normed)
    grad_patches = (
        (grad_middle + grad_inputs).astype(jnp.bfloat16).reshape(row_count, local_len, model_width)
    )
    grads = (
        grad_ln1_gain,
        grad_ln1_bias,
        grad_w_qkv,
        grad_bias_qv,
        grad_w_out,
        grad_b_out,
        grad_ln2_gain,
        grad_ln2_bias,
        grad_w_fc1,
        grad_b_fc1,
        grad_w_fc2,
        grad_b_fc2,
    )
    return (grad_patches, grads)


def per_device(
    patches,
    picture_ids,
    valid_mask,
    ln1_gain,
    ln1_bias,
    w_qkv,
    bias_qv,
    w_out,
    b_out,
    ln2_gain,
    ln2_bias,
    w_fc1,
    b_fc1,
    w_fc2,
    b_fc2,
    cotangent,
):
    gathered = gather_weights(
        ln1_gain,
        ln1_bias,
        w_qkv,
        bias_qv,
        w_out,
        b_out,
        ln2_gain,
        ln2_bias,
        w_fc1,
        b_fc1,
        w_fc2,
        b_fc2,
    )
    layer_out, kept_values = forward_pass(patches, picture_ids, valid_mask, gathered)
    grad_patches, grads = backward_pass(cotangent, picture_ids, valid_mask, gathered, kept_values)
    (
        grad_ln1_gain,
        grad_ln1_bias,
        grad_w_qkv,
        grad_bias_qv,
        grad_w_out,
        grad_b_out,
        grad_ln2_gain,
        grad_ln2_bias,
        grad_w_fc1,
        grad_b_fc1,
        grad_w_fc2,
        grad_b_fc2,
    ) = grads
    owned = (
        lax.psum_scatter(
            grad_ln1_gain.astype(jnp.bfloat16), "dp", scatter_dimension=0, tiled=True
        ).astype(jnp.float32),
        lax.psum_scatter(
            grad_ln1_bias.astype(jnp.bfloat16), "dp", scatter_dimension=0, tiled=True
        ).astype(jnp.float32),
        lax.psum_scatter(
            grad_w_qkv.astype(jnp.bfloat16), "dp", scatter_dimension=0, tiled=True
        ).astype(jnp.float32),
        lax.psum_scatter(
            grad_bias_qv.astype(jnp.bfloat16), "dp", scatter_dimension=1, tiled=True
        ).astype(jnp.float32),
        lax.psum_scatter(
            grad_w_out.astype(jnp.bfloat16), "dp", scatter_dimension=0, tiled=True
        ).astype(jnp.float32),
        lax.psum_scatter(
            grad_b_out.astype(jnp.bfloat16), "dp", scatter_dimension=0, tiled=True
        ).astype(jnp.float32),
        lax.psum_scatter(
            grad_ln2_gain.astype(jnp.bfloat16), "dp", scatter_dimension=0, tiled=True
        ).astype(jnp.float32),
        lax.psum_scatter(
            grad_ln2_bias.astype(jnp.bfloat16), "dp", scatter_dimension=0, tiled=True
        ).astype(jnp.float32),
        lax.psum_scatter(
            grad_w_fc1.astype(jnp.bfloat16), "dp", scatter_dimension=0, tiled=True
        ).astype(jnp.float32),
        lax.psum_scatter(
            grad_b_fc1.astype(jnp.bfloat16), "dp", scatter_dimension=0, tiled=True
        ).astype(jnp.float32),
        lax.psum_scatter(
            grad_w_fc2.astype(jnp.bfloat16), "dp", scatter_dimension=1, tiled=True
        ).astype(jnp.float32),
        lax.psum_scatter(
            grad_b_fc2.astype(jnp.bfloat16), "dp", scatter_dimension=0, tiled=True
        ).astype(jnp.float32),
    )
    (
        part_ln1_gain,
        part_ln1_bias,
        part_w_qkv,
        part_bias_qv,
        part_w_out,
        part_b_out,
        part_ln2_gain,
        part_ln2_bias,
        part_w_fc1,
        part_b_fc1,
        part_w_fc2,
        part_b_fc2,
    ) = owned
    summed = (
        lax.psum(part_ln1_gain.astype(jnp.bfloat16), "seq").astype(jnp.float32),
        lax.psum(part_ln1_bias.astype(jnp.bfloat16), "seq").astype(jnp.float32),
        lax.psum(part_w_qkv.astype(jnp.bfloat16), "seq").astype(jnp.float32),
        lax.psum(part_bias_qv.astype(jnp.bfloat16), "seq").astype(jnp.float32),
        lax.psum(part_w_out.astype(jnp.bfloat16), "seq").astype(jnp.float32),
        lax.psum(part_b_out.astype(jnp.bfloat16), "seq").astype(jnp.float32),
        lax.psum(part_ln2_gain.astype(jnp.bfloat16), "seq").astype(jnp.float32),
        lax.psum(part_ln2_bias.astype(jnp.bfloat16), "seq").astype(jnp.float32),
        lax.psum(part_w_fc1.astype(jnp.bfloat16), "seq").astype(jnp.float32),
        lax.psum(part_b_fc1.astype(jnp.bfloat16), "seq").astype(jnp.float32),
        lax.psum(part_w_fc2.astype(jnp.bfloat16), "seq").astype(jnp.float32),
        lax.psum(part_b_fc2.astype(jnp.bfloat16), "seq").astype(jnp.float32),
    )
    (
        final_ln1_gain,
        final_ln1_bias,
        final_w_qkv,
        final_bias_qv,
        final_w_out,
        final_b_out,
        final_ln2_gain,
        final_ln2_bias,
        final_w_fc1,
        final_b_fc1,
        final_w_fc2,
        final_b_fc2,
    ) = summed
    return (
        layer_out,
        grad_patches,
        final_ln1_gain,
        final_ln1_bias,
        final_w_qkv,
        final_bias_qv,
        final_w_out,
        final_b_out,
        final_ln2_gain,
        final_ln2_bias,
        final_w_fc1,
        final_b_fc1,
        final_w_fc2,
        final_b_fc2,
    )


WIN = 256
ROWBLK = 64
LOG2E = 1.4426950408889634
ORDER = (0, 2, 4, 6, 1, 3, 5, 7)
ORDER_SMALL = (0, 4, 2, 6, 1, 5, 3, 7)
bf16 = jnp.bfloat16
f32 = jnp.float32


def nn(a, b):
    return lax.dot_general(a, b, (((1,), (0,)), ((), ())), preferred_element_type=f32)


def nt(a, b):
    return lax.dot_general(a, b, (((1,), (1,)), ((), ())), preferred_element_type=f32)


def tn(a, b):
    return lax.dot_general(a, b, (((0,), (0,)), ((), ())), preferred_element_type=f32)


VM = pl.BlockSpec(memory_space=pltpu.VMEM)
ANY = pl.BlockSpec(memory_space=pl.ANY)


def sds(shape, dtype):
    return jax.ShapeDtypeStruct(shape, dtype)


def row_loop(total, body):
    @pl.loop(0, total // ROWBLK)
    def _(r):
        body(pl.ds(pl.multiple_of(r * ROWBLK, ROWBLK), ROWBLK))


MESH = pl.DeviceIdType.MESH


def flipped_index(d, mask):
    for bit in (1, 2, 4):
        if mask & bit:
            d = d + bit - 2 * bit * lax.rem(lax.div(d, bit), 2)
    return d


def here():
    return lax.axis_index("dp"), lax.axis_index("seq")


def across_links(mask):
    d, z = here()
    return flipped_index(d, mask), z


def row_partner(s):
    d, z = here()
    core, odd = lax.rem(d, 2), lax.rem(z, 2)
    return d - core + lax.div(z, 2), 2 * core + odd + s - 2 * s * odd


def row_stays():
    d, z = here()
    return lax.rem(d, 2) == lax.div(z, 2)


def greet(relations):
    if not relations:
        return
    barrier = pltpu.get_barrier_semaphore()
    d, z = here()

    def signal(device):
        pl.semaphore_signal(barrier, inc=1, device_id=device, device_id_type=MESH)

    count = 0
    for mask in (1, 2, 4):
        if mask in relations:
            signal(across_links(mask))
            count += 1
    conditions = []
    if "z" in relations:
        conditions += [(z > 0, (d, z - 1)), (z < 3, (d, z + 1))]
        count = count + lax.div(z + 2, 3) + lax.div(5 - z, 3)
    if "rows" in relations:
        signal(row_partner(1))
        count += 1
        conditions.append((jnp.logical_not(row_stays()), row_partner(0)))
        away = lax.rem(d, 2) - lax.div(z, 2)
        count = count + away * away
    for condition, device in conditions:
        pl.when(condition)(functools.partial(signal, device))
    pl.semaphore_wait(barrier, count)


def remote(src, dst, sem, device):
    return pltpu.make_async_remote_copy(
        src_ref=src, dst_ref=dst, send_sem=sem.at[0], recv_sem=sem.at[1], device_id=device, device_id_type=MESH
    )


def start_all(copies):
    for c in copies:
        c.start()


def wait_all(copies):
    for c in copies:
        c.wait()


class Hop:
    relations = ()
    ins, outs, scratch = (), (), ()

    def start(self, ins, outs, scratch):
        pass

    def halfway(self, ins, outs, scratch):
        pass

    def finish(self, ins, outs, scratch):
        pass


class Straight(Hop):
    relations = (2, 4)

    def __init__(self, unit):
        self.ins = (unit,)
        self.outs = ((unit.shape, bf16),) * 2
        self.scratch = (pltpu.SemaphoreType.DMA((2, 2)),)

    def copies(self, ins, outs, scratch):
        return [remote(ins[0], outs[i], scratch[0].at[i], across_links(mask)) for i, mask in ((0, 2), (1, 4))]

    def start(self, *refs):
        start_all(self.copies(*refs))

    def finish(self, *refs):
        wait_all(self.copies(*refs))


class Corner(Straight):
    def __init__(self, x, y):
        super().__init__(x)
        self.ins = (x, y)
        self.outs = ((x.shape[1:], bf16),) * 2

    def copies(self, ins, outs, scratch):
        x, y = ins
        return [
            remote(y.at[0], outs[0], scratch[0].at[0], across_links(2)),
            remote(x.at[1], outs[1], scratch[0].at[1], across_links(4)),
        ]


class Chain(Straight):
    def __init__(self, unit, following):
        self.ins = (unit, following)
        self.outs = ((unit.shape, bf16),) * 2 + ((unit.shape[1:], bf16),) * 2 + ((following.shape, bf16),) * 2
        self.scratch = (pltpu.SemaphoreType.DMA((6, 2)),)

    def stages(self, ins, outs, scratch):
        sem = scratch[0]
        x, y, da, db, x2, y2 = outs
        on_x, on_y = across_links(2), across_links(4)
        first = [remote(ins[0], x, sem.at[0], on_x), remote(ins[0], y, sem.at[1], on_y)]
        second = [remote(y.at[0], da, sem.at[2], on_x), remote(x.at[1], db, sem.at[3], on_y),
                  remote(ins[1], x2, sem.at[4], on_x), remote(ins[1], y2, sem.at[5], on_y)]
        return first, second

    def start(self, *refs):
        start_all(self.stages(*refs)[0])

    def halfway(self, *refs):
        first, second = self.stages(*refs)
        wait_all(first)
        start_all(second)

    def finish(self, *refs):
        wait_all(self.stages(*refs)[1])


class Rows(Hop):
    relations = ("rows",)

    def __init__(self, v):
        self.ins = (v,)
        self.outs = ((v.shape, v.dtype),)
        self.scratch = (pltpu.SemaphoreType.DMA((2, 2)), pltpu.SemaphoreType.DMA)

    def each(self, ins, outs, scratch, act):
        odd = lax.rem(lax.axis_index("seq"), 2)
        stays = row_stays()

        @pl.when(stays)
        def _():
            act(pltpu.make_async_copy(ins[0].at[odd], outs[0].at[odd], scratch[1]))

        @pl.when(jnp.logical_not(stays))
        def _():
            act(remote(ins[0].at[odd], outs[0].at[odd], scratch[0].at[0], row_partner(0)))

        act(remote(ins[0].at[1 - odd], outs[0].at[odd], scratch[0].at[1], row_partner(1)))

    def start(self, *refs):
        self.each(*refs, lambda c: c.start())

    def finish(self, *refs):
        self.each(*refs, lambda c: c.wait())


def add_into(total, other):
    @pl.loop(0, total.shape[-1] // 128)
    def _(t):
        cols = pl.ds(pl.multiple_of(t * 128, 128), 128)
        total[..., cols] = (total[..., cols].astype(f32) + other[..., cols].astype(f32)).astype(bf16)


class First(Hop):
    relations = (2, 4)

    def __init__(self, keep_a, send_a, keep_b, send_b):
        self.ins = (keep_a, send_a, keep_b, send_b)
        shape = (2, *keep_a.shape)
        self.outs = ((shape, bf16),)
        self.scratch = (pltpu.VMEM(shape, bf16), pltpu.VMEM(shape, bf16), pltpu.SemaphoreType.DMA((2, 2)),
                        pltpu.SemaphoreType.DMA((3,)))

    def copies(self, ins, outs, scratch):
        kept, got, sem, own = scratch
        return [
            remote(ins[1], got.at[0], sem.at[0], across_links(2)),
            remote(ins[3], got.at[1], sem.at[1], across_links(4)),
            pltpu.make_async_copy(ins[0], kept.at[0], own.at[0]),
            pltpu.make_async_copy(ins[2], kept.at[1], own.at[1]),
        ]

    def start(self, *refs):
        start_all(self.copies(*refs))

    def finish(self, ins, outs, scratch):
        wait_all(self.copies(ins, outs, scratch))
        for i in range(2):
            add_into(scratch[0].at[i], scratch[1].at[i])
        done = pltpu.make_async_copy(scratch[0], outs[0], scratch[3].at[2])
        done.start()
        done.wait()


class Second(Hop):
    relations = (2, 4)

    def __init__(self, sums):
        self.ins = (sums,)
        shape = (2, *sums.shape[2:])
        self.outs = ((shape, bf16),)
        self.scratch = (pltpu.VMEM(shape, bf16), pltpu.VMEM(shape, bf16), pltpu.SemaphoreType.DMA((2, 2)),
                        pltpu.SemaphoreType.DMA((3,)))

    def copies(self, ins, outs, scratch):
        kept, got, sem, own = scratch
        return [
            remote(ins[0].at[0, 1], got.at[0], sem.at[0], across_links(4)),
            remote(ins[0].at[1, 1], got.at[1], sem.at[1], across_links(2)),
            pltpu.make_async_copy(ins[0].at[0, 0], kept.at[0], own.at[0]),
            pltpu.make_async_copy(ins[0].at[1, 0], kept.at[1], own.at[1]),
        ]

    def start(self, *refs):
        start_all(self.copies(*refs))

    def finish(self, ins, outs, scratch):
        wait_all(self.copies(ins, outs, scratch))
        add_into(scratch[0], scratch[1])
        done = pltpu.make_async_copy(scratch[0], outs[0], scratch[3].at[2])
        done.start()
        done.wait()


INWARD, MIDDLE, OUTWARD = range(3)


def seq_step(stage):
    d, z = here()
    inner = (z == 1) | (z == 2)
    outer = jnp.logical_not(inner)
    side = z + 1 - 2 * lax.rem(z, 2)
    if stage == INWARD:
        return outer, inner, (d, side)
    if stage == MIDDLE:
        return inner, inner, (d, 3 - z)
    return inner, outer, (d, side)


class Seq(Hop):
    relations = ("z",)

    def __init__(self, stage, v, half=None):
        self.stage, self.half = stage, half
        self.ins = (v,)
        shape = v.shape if half is None else v.shape[1:]
        self.outs = ((shape, bf16),)
        self.scratch = (pltpu.VMEM(shape, bf16), pltpu.VMEM(shape, bf16), pltpu.SemaphoreType.DMA((2,)),
                        pltpu.SemaphoreType.DMA((2,)))

    def source(self, ins):
        return ins[0] if self.half is None else ins[0].at[self.half]

    def start(self, ins, outs, scratch):
        kept, got, sem, own = scratch
        sends, _, partner = seq_step(self.stage)
        src = self.source(ins)
        pltpu.make_async_copy(src, kept, own.at[0]).start()

        @pl.when(sends)
        def _():
            remote(src, got, sem, partner).start()

    def finish(self, ins, outs, scratch):
        kept, got, sem, own = scratch
        sends, receives, partner = seq_step(self.stage)
        src = self.source(ins)
        pltpu.make_async_copy(src, kept, own.at[0]).wait()

        @pl.when(sends)
        def _():
            remote(src, got, sem, partner).wait_send()

        def store(ref):
            done = pltpu.make_async_copy(ref, outs[0], own.at[1])
            done.start()
            done.wait()

        @pl.when(receives)
        def _():
            remote(src, got, sem, partner).wait_recv()
            if self.stage != OUTWARD:
                add_into(kept, got)
            store(kept if self.stage != OUTWARD else got)

        @pl.when(jnp.logical_not(receives))
        def _():
            store(kept)


def hop_parts(hops):
    relations = set()
    for h in hops:
        relations |= set(h.relations)
    return (
        [a for h in hops for a in h.ins],
        [sds(s, t) for h in hops for s, t in h.outs],
        [s for h in hops for s in h.scratch],
        relations,
    )


def hop_refs(hops, ins, outs, scratch):
    ins, outs, scratch = list(ins), list(outs), list(scratch)
    parts = []
    for h in hops:
        parts.append(tuple([refs.pop(0) for _ in range(n)] for refs, n in (
            (ins, len(h.ins)), (outs, len(h.outs)), (scratch, len(h.scratch)))))
    return parts


def hop_results(hops, results):
    results, parts = list(results), []
    for h in hops:
        got = tuple(results.pop(0) for _ in h.outs)
        parts.append(got if len(got) > 1 else got[0])
    return parts


def to_sibling(src, dst, sem, i):
    return pltpu.make_async_remote_copy(
        src_ref=src, dst_ref=dst, send_sem=sem.at[1, i], recv_sem=sem.at[2, i], device_id=across_links(1), device_id_type=MESH
    )


def unit_copies(pieces, half, rows, cols, place, sem):
    d = lax.axis_index("dp")
    own, xr, yr, da, db = pieces
    copies = []
    for i, piece in enumerate((own, xr, yr, da if half == 0 else db)):
        src = piece.at[half, rows, cols] if i < 3 else piece.at[rows, cols]
        dst = place(flipped_index(d, 2 * i))
        copies.append(pltpu.make_async_copy(src, dst, sem.at[0, i]))
        copies.append(to_sibling(src, dst, sem, i))
    return copies


def shard_rows(ref, count):
    return lambda j: ref.at[pl.ds(pl.multiple_of(j * count, count), count), :]


def norm_rows(v, gain, offset):
    center = v - jnp.mean(v, axis=-1, keepdims=True)
    spread = jnp.mean(center * center, axis=-1, keepdims=True)
    return center * lax.rsqrt(spread + epsilon) * gain + offset


def transpose_ordered(src, flipped, dst):
    d = lax.axis_index("dp")
    width = src.shape[1]
    part = width // 8

    @pl.loop(0, width // 128)
    def _(j):
        cols = pl.ds(pl.multiple_of(j * 128, 128), 128)
        flipped[cols, :] = src[:, cols].T

    for i, m in enumerate(ORDER):
        where = pl.ds(pl.multiple_of(flipped_index(d, m) * part, part), part)
        dst[i * part : (i + 1) * part, :] = flipped[where, :]


def spread(piece, out_ref, part, span):
    inside = (part + 127) // 128 * 128

    @pl.loop(0, 8)
    def _(j):
        at = pl.multiple_of(lax.div(j * ((out_ref.shape[1] - span) // 128), 7) * 128, 128)
        r = lax.broadcasted_iota(jnp.int32, (inside, span), 0)
        c = lax.broadcasted_iota(jnp.int32, (inside, span), 1)
        place = jnp.where((c == r + (j * part - at)) & (r < part), 1.0, 0.0).astype(bf16)
        out_ref[0:16, pl.ds(at, span)] += nn(piece(j)[:, 0:inside], place)


def column_tiles(width, body):
    full = width // 256

    @pl.loop(0, full)
    def _(t):
        body(pl.ds(pl.multiple_of(t * 256, 256), 256))

    if width % 256:
        body(pl.ds(full * 256, width % 256))


class Gather:
    def __init__(self, unit, place, sem, local, halves=2):
        self.unit, self.place, self.sem, self.local, self.halves = unit, place, sem, local, halves
        self.d = lax.axis_index("dp")

    def own(self, kind, mask):
        return [remote(self.unit.at[h], self.place(h, self.d), self.sem.at[kind, h], across_links(mask)) for h in range(self.halves)]

    def forward(self, kind, h, shard_mask, mask):
        ref = self.place(h, flipped_index(self.d, shard_mask))
        return remote(ref, ref, self.sem.at[kind, h], across_links(mask))

    def here(self):
        return [pltpu.make_async_copy(self.unit.at[h], self.place(h, self.d), self.local.at[h]) for h in range(self.halves)]

    def both(self, kind, shard_mask):
        return [self.forward(kind, h, shard_mask, 1) for h in range(self.halves)]

    def corners(self):
        if self.halves == 1:
            return [self.forward(3, 0, 2, 4)]
        return [self.forward(3, 0, 4, 2), self.forward(3, 1, 2, 4)]

    def begin(self):
        start_all(self.own(0, 2) + self.own(1, 4) + self.own(2, 1) + self.here())

    def turn(self):
        for c in self.own(0, 2) + self.own(1, 4):
            c.wait_recv()
        start_all(self.corners() + self.both(4, 2) + self.both(5, 4))

    def last(self):
        for c in self.corners():
            c.wait_recv()
        start_all(self.both(6, 6))

    def arrived(self):
        for c in self.own(2, 1) + self.both(4, 2) + self.both(5, 4) + self.both(6, 6):
            c.wait_recv()
        wait_all(self.here())

    def sent(self):
        for c in (self.own(0, 2) + self.own(1, 4) + self.own(2, 1) + self.corners() + self.both(4, 2) + self.both(5, 4)
                  + self.both(6, 6)):
            c.wait_send()


def entry_kernel(ff, unit0, small, unit1, patches, x_ref, nt_ref, q_ref, kv_ref, vec_ref, b1_ref, far_ref, w_ref,
                 w, buf, xbuf, n, flipped, sem, small_sem, local, rows_sem, rows_local, far_sem, out_sem):
    width = unit0.shape[2]
    part, tokens = width // 8, n.shape[0]

    def matrix_rows(first):
        return lambda h, j: w.at[first + h, pl.ds(pl.multiple_of(j * part, part), part), :]

    vectors = Gather(small, lambda h, j: buf.at[j], small_sem, local.at[2], halves=1)
    keys, queries = Gather(unit0, matrix_rows(0), sem.at[0], local.at[0]), Gather(unit1, matrix_rows(2), sem.at[1], local.at[1])
    rows = Rows(x_ref)
    row_refs = ([patches], [xbuf], [rows_sem, rows_local])
    far = [remote(kv_ref.at[:, pl.ds(i * width, width)], far_ref.at[:, pl.ds(i * width, width)], far_sem.at[i], across_links(1))
           for i in range(2)]
    vectors.begin()
    keys.begin()
    rows.start(*row_refs)
    vec_ref[...] = jnp.zeros(vec_ref.shape, f32)
    b1_ref[...] = jnp.zeros(b1_ref.shape, f32)
    vectors.turn()
    keys.turn()
    vectors.last()
    queries.begin()
    vectors.arrived()
    spread(lambda j: buf[j, 0], vec_ref, part, 512)
    rows.finish(*row_refs)
    half = tokens // 2
    for i in range(2):

        @pl.loop(0, half // ROWBLK)
        def _(r):
            at = pl.ds(pl.multiple_of(r * ROWBLK, ROWBLK), ROWBLK)
            to = pl.ds(pl.multiple_of(r * ROWBLK + i * half, ROWBLK), ROWBLK)
            v = xbuf[i, at, :]
            x_ref[to, :] = v
            n[to, :] = norm_rows(v.astype(f32), vec_ref[0:1, :], vec_ref[1:2, :]).astype(bf16)

    keys.last()
    keys.arrived()

    def project(i, bias, out, offset):
        def body(cols):
            total = nn(n[...], w[i, :, cols])
            if bias is not None:
                total = total + vec_ref[bias : bias + 1, cols]
            out[:, pl.ds(pl.multiple_of(cols.start + offset, 128), cols.size)] = total.astype(bf16)

        column_tiles(width, body)

    project(0, None, kv_ref, 0)
    far[0].start()
    queries.turn()
    project(1, 3, kv_ref, width)
    far[1].start()
    stores = [pltpu.make_async_copy(w.at[pl.ds(2 * i, 2)], w_ref.at[pl.ds(2 * i, 2)], out_sem.at[i]) for i in range(2)]
    stores[0].start()
    transpose_ordered(n, flipped, nt_ref)
    spread(lambda j: buf[j, 1], b1_ref, ff // 8, 768)
    queries.last()
    queries.arrived()
    stores[1].start()
    project(2, 2, q_ref, 0)
    for g in (vectors, keys, queries):
        g.sent()
    wait_all(far + stores)


def head_window(h, width):
    tile = lax.div(h * HD, 128)
    w0 = pl.multiple_of((tile - lax.div(tile, (width - WIN) // 128 + 1)) * 128, 128)
    lane = lax.broadcasted_iota(jnp.int32, (1, WIN), 1)
    off = h * HD - w0
    return w0, (lane >= off) & (lane < off + HD)


def attention_forward_kernel(q_ref, ko_ref, kx_ref, qid_ref, kid_ref, att_ref, lse_ref, bias, acc, lse_cols):
    tokens, width = q_ref.shape
    scale = HD**-0.5 * LOG2E
    block = 256

    @pl.loop(0, tokens // ROWBLK)
    def _(r):
        rows = pl.ds(pl.multiple_of(r * ROWBLK, ROWBLK), ROWBLK)
        same = qid_ref[rows, 0:1] == kid_ref[0:1, :]
        col = lax.broadcasted_iota(jnp.int32, (ROWBLK, 2 * tokens), 1)
        row = lax.broadcasted_iota(jnp.int32, (ROWBLK, 2 * tokens), 0) + r * ROWBLK
        bias[rows, :] = jnp.where(same | (col == row), 0.0, big_negative)
        acc[rows, :] = jnp.zeros((ROWBLK, width), f32)
        lse_cols[rows, :] = jnp.zeros((ROWBLK, 128), f32)

    @pl.loop(0, HEADS)
    def _(h):
        w0, mask = head_window(h, width)
        win, winv = pl.ds(w0, WIN), pl.ds(w0 + width, WIN)
        zero = jnp.zeros((), bf16)
        ko, kx = jnp.where(mask, ko_ref[:, win], zero), jnp.where(mask, kx_ref[:, win], zero)
        vo, vx = jnp.where(mask, ko_ref[:, winv], zero), jnp.where(mask, kx_ref[:, winv], zero)
        lane = lax.broadcasted_iota(jnp.int32, (1, 128), 1)
        for qb in range(tokens // block):
            rows = pl.ds(qb * block, block)
            qw = q_ref[rows, win]
            so = nt(qw, ko) * scale + bias[rows, 0:tokens]
            sx = nt(qw, kx) * scale + bias[rows, tokens : 2 * tokens]
            m = jnp.maximum(jnp.max(so, axis=1, keepdims=True), jnp.max(sx, axis=1, keepdims=True))
            po, px = jnp.exp2(so - m), jnp.exp2(sx - m)
            total = jnp.sum(po, axis=1, keepdims=True) + jnp.sum(px, axis=1, keepdims=True)
            o = nn(po.astype(bf16), vo) + nn(px.astype(bf16), vx)
            acc[rows, win] += o * (1.0 / total)
            lse_cols[rows, :] = jnp.where(lane == h, m + jnp.log2(total), lse_cols[rows, :])

    def body(rows):
        att_ref[rows, :] = acc[rows, :].astype(bf16)

    row_loop(tokens, body)
    lse_ref[...] = lse_cols[...].T[:HEADS, :]


def attention_backward_kernel(
    h0, h1, base, done, q_ref, kn_ref, kf_ref, go_ref, lse_ref, del_ref, kid_ref, qid_ref, cin_ref,
    dq_ref, dkn_ref, cout_ref, dkr_ref, bias, acc, dkf_ref, far_sem
):
    tokens, width = q_ref.shape
    span = acc.shape[2]
    scale, unit = HD**-0.5 * LOG2E, HD**-0.5

    @pl.loop(0, 2 * tokens // ROWBLK)
    def _(r):
        rows = pl.ds(pl.multiple_of(r * ROWBLK, ROWBLK), ROWBLK)
        col = lax.broadcasted_iota(jnp.int32, (ROWBLK, tokens), 1)
        row = lax.broadcasted_iota(jnp.int32, (ROWBLK, tokens), 0) + r * ROWBLK
        allowed = (kid_ref[rows, 0:1] == qid_ref[0:1, :]) | (col == row)
        bias[rows, :] = jnp.where(allowed, 0.0, big_negative)

    @pl.loop(0, tokens // ROWBLK)
    def _(r):
        rows = pl.ds(pl.multiple_of(r * ROWBLK, ROWBLK), ROWBLK)
        for i in range(5):
            if base == 0:
                acc[i, rows, :] = jnp.zeros((ROWBLK, span), f32)
            else:
                acc[i, rows, 0:128] = cin_ref[i, rows, :]
                acc[i, rows, 128:span] = jnp.zeros((ROWBLK, span - 128), f32)

    @pl.loop(h0, h1)
    def _(h):
        w0, mask = head_window(h, width)
        win, winv = pl.ds(w0, WIN), pl.ds(w0 + width, WIN)
        at = pl.ds(pl.multiple_of(w0 - base, 128), WIN)
        zero = jnp.zeros((), bf16)
        qw = q_ref[:, win]
        qm, gm = jnp.where(mask, qw, zero), jnp.where(mask, go_ref[:, win], zero)
        lse, inner = lse_ref[pl.ds(h, 1), :], del_ref[pl.ds(h, 1), :]
        dq = None
        for b, kref in ((0, kn_ref), (1, kf_ref)):
            km, vw = jnp.where(mask, kref[:, win], zero), kref[:, winv]
            pt = jnp.exp2(nt(km, qw) * scale + bias[b * tokens : (b + 1) * tokens, :] - lse)
            acc[2 + 2 * b, :, at] += nn(pt.astype(bf16), gm)
            ds = (pt * (nt(vw, gm) - inner)).astype(bf16)
            acc[1 + 2 * b, :, at] += nn(ds, qm)
            part = tn(ds, km)
            dq = part if dq is None else dq + part
        acc[0, :, at] += dq

    if span == done:
        cout_ref[...] = jnp.zeros(cout_ref.shape, f32)

    @pl.loop(0, tokens // ROWBLK)
    def _(r):
        rows = pl.ds(pl.multiple_of(r * ROWBLK, ROWBLK), ROWBLK)
        dq_ref[rows, :] = (acc[0, rows, 0:done] * unit).astype(bf16)
        for b, out in ((0, dkn_ref), (1, dkf_ref)):
            out[rows, 0:done] = (acc[1 + 2 * b, rows, 0:done] * unit).astype(out.dtype)
            out[rows, done : 2 * done] = acc[2 + 2 * b, rows, 0:done].astype(out.dtype)
        for i in range(5):
            if span > done:
                cout_ref[i, rows, :] = acc[i, rows, done : done + 128]

    far = remote(dkf_ref, dkr_ref, far_sem, across_links(1))
    far.start()
    far.wait()


def middle_kernel(att_ref, x_ref, cot_ref, vec_ref, w_ref, mid_ref, n2_ref, n2t_ref, cott_ref, attt_ref, flipped, w, sem):
    tokens, width = x_ref.shape
    load = pltpu.make_async_copy(w_ref.at[3], w, sem)
    load.start()
    transpose_ordered(cot_ref, flipped, cott_ref)
    transpose_ordered(att_ref, flipped, attt_ref)
    load.wait()

    def body(cols):
        mid_ref[:, cols] = nn(att_ref[...], w[:, cols]) + vec_ref[4:5, cols] + x_ref[:, cols].astype(f32)

    column_tiles(width, body)

    def norm(rows):
        n2_ref[rows, :] = norm_rows(mid_ref[rows, :], vec_ref[5:6, 0:width], vec_ref[6:7, 0:width]).astype(bf16)

    row_loop(tokens, norm)
    transpose_ordered(n2_ref, flipped, n2t_ref)


def store_blocks(half, total, part, keep, send, cols):
    kept = (0, 2) if half == 0 else (0, 1)
    sent = (1, 3) if half == 0 else (2, 3)
    for i in range(2):
        keep[i, :, cols] = total[kept[i] * part : (kept[i] + 1) * part]
        send[i, :, cols] = total[sent[i] * part : (sent[i] + 1) * part]


def mlp_kernel(first, last, hops, n2_ref, cot_ref, n2t_ref, cott_ref, b1_ref, vec_ref, outp_ref, gnp_ref, *rest):
    counts = [sum(len(part) for part in parts) for parts in zip(*((h.ins, h.outs, h.scratch) for h in hops))] or [0, 0, 0]
    pieces, hop_ins, rest = rest[:5], rest[5 : 5 + counts[0]], rest[5 + counts[0] :]
    (out_ref, gn_ref, ka_ref, sa_ref, kb_ref, sb_ref, gb1_ref), hop_outs, rest = rest[:7], rest[7 : 7 + counts[1]], rest[7 + counts[1] :]
    (wbuf, acc, gacc, mine, theirs, came, sem, gsem, credit), hop_scratch = rest[:9], rest[9:]
    carried = list(zip(hops, hop_refs(hops, hop_ins, hop_outs, hop_scratch)))
    t, steps = pl.program_id(0), pl.num_programs(0) - 1
    width = n2_ref.shape[1]
    tile, part = wbuf.shape[-1], width // 8
    half = width // 2
    slot = lax.rem(t, 2)
    before = 1 - slot

    def copies(step, to):
        cols = pl.ds(pl.multiple_of(step * tile, tile), tile)
        every = []
        for h in range(2):
            every += unit_copies(pieces, h, pl.ds(0, part), cols, shard_rows(wbuf.at[to, h], part), sem.at[to, h])
        return every

    def exchange(at, h):
        return to_sibling(theirs.at[at, h], came.at[at, h], gsem.at[at], h)

    @pl.when(t == 0)
    def _():
        greet(hop_parts(hops)[3] | {1})
        for h, refs in carried:
            h.start(*refs)
        start_all(copies(0, 0))

        def init(rows):
            acc[rows, :] = outp_ref[rows, :] + vec_ref[7:8, 0:width] if first else outp_ref[rows, :]
            gacc[rows, :] = jnp.zeros((ROWBLK, width), f32) if first else gnp_ref[rows, :]

        row_loop(n2_ref.shape[0], init)

    @pl.when((t > 0) & (t < steps))
    def _():
        pl.semaphore_wait(credit, 1)

    @pl.when(t + 1 < steps)
    def _():
        start_all(copies(t + 1, before))

    @pl.when(t < steps)
    def _():
        wait_all(copies(t, slot))
        w1, w2 = wbuf[slot, 0], wbuf[slot, 1]
        u = nn(n2_ref[...], w1) + b1_ref[0:1, :]
        c0 = 0.7978845608028654
        th = jnp.tanh(c0 * (u + 0.044715 * u * u * u))
        active = (0.5 * u * (1.0 + th)).astype(bf16)
        slope = 0.5 * (1.0 + th) + 0.5 * u * (1.0 - th * th) * (c0 * (1.0 + 3 * 0.044715 * u * u))
        gh = (nn(cot_ref[...], w2) * slope).astype(bf16)
        gb1_ref[...] = jnp.sum(gh.astype(f32), axis=0, keepdims=True)
        g1 = nn(n2t_ref[...], gh).astype(bf16)
        mine[slot, 0], theirs[slot, 0] = g1[:half], g1[half:]
        exchange(slot, 0).start()
        g2 = nn(cott_ref[...], active).astype(bf16)
        mine[slot, 1], theirs[slot, 1] = g2[:half], g2[half:]
        exchange(slot, 1).start()
        acc[...] += nt(active, w2)
        gacc[...] += nt(gh, w1)

    @pl.when(t > 0)
    def _():
        for h, keep, send in ((0, ka_ref, sa_ref), (1, kb_ref, sb_ref)):
            exchange(before, h).wait()
            total = (mine[before, h].astype(f32) + came[before, h].astype(f32)).astype(bf16)
            store_blocks(h, total, part, keep, send, slice(None))

    @pl.when(t < steps - 1)
    def _():
        pl.semaphore_signal(credit, inc=1, device_id=across_links(1), device_id_type=MESH)

    @pl.when(t == steps)
    def _():
        out_ref[...] = acc[...].astype(out_ref.dtype)
        gn_ref[...] = gacc[...]
        for h, refs in carried:
            h.finish(*refs)

    @pl.when(t == steps * 5 // 8)
    def _():
        for h, refs in carried:
            h.halfway(*refs)


def mlp_call(name, first, last, n2, cot, n2t, cott, b1, vec, outp, gnp, pieces, begin, collective=0, hops=()):
    tokens, width = n2.shape
    cols, tile = pieces[0].shape[2], 256
    steps = cols // tile
    const = lambda a: pl.BlockSpec(a.shape, lambda t: (0,) * a.ndim, pipeline_mode=pl.Buffered(1))
    grads = pl.BlockSpec((2, width // 8, tile), lambda t: (0, 0, jnp.maximum(t - 1, 0)))
    hidden = lambda t: jnp.minimum(t, steps - 1)
    hop_ins, hop_outs, hop_scratch, _ = hop_parts(hops)
    grad = sds((2, width // 8, cols), bf16)
    got = pl.pallas_call(
        functools.partial(mlp_kernel, first, last, hops),
        grid=(steps + 1,),
        in_specs=[const(n2), const(cot), const(n2t), const(cott), pl.BlockSpec((8, tile), lambda t: (0, hidden(t) + begin // tile)),
                  const(vec), const(outp), const(gnp)] + [ANY] * (5 + len(hop_ins)),
        out_specs=(
            pl.BlockSpec((tokens, width), lambda t: (0, 0)),
            pl.BlockSpec((tokens, width), lambda t: (0, 0)),
            grads,
            grads,
            grads,
            grads,
            pl.BlockSpec((1, tile), lambda t: (0, hidden(t))),
            *[ANY] * len(hop_outs),
        ),
        out_shape=(
            sds((tokens, width), bf16 if last else f32),
            sds((tokens, width), f32),
            grad,
            grad,
            grad,
            grad,
            sds((1, cols), f32),
            *hop_outs,
        ),
        scratch_shapes=[
            pltpu.VMEM((2, 2, width, tile), bf16),
            pltpu.VMEM((tokens, width), f32),
            pltpu.VMEM((tokens, width), f32),
            pltpu.VMEM((2, 2, width // 2, tile), bf16),
            pltpu.VMEM((2, 2, width // 2, tile), bf16),
            pltpu.VMEM((2, 2, width // 2, tile), bf16),
            pltpu.SemaphoreType.DMA((2, 2, 3, 4)),
            pltpu.SemaphoreType.DMA((2, 3, 2)),
            pltpu.SemaphoreType.REGULAR,
            *hop_scratch,
        ],
        compiler_params=pltpu.CompilerParams(collective_id=collective, has_side_effects=True),
        cost_estimate=pl.CostEstimate(
            flops=12 * tokens * width * cols, bytes_accessed=8 * width * cols + 12 * tokens * width, transcendentals=tokens * cols
        ),
        name=name,
    )(n2, cot, n2t, cott, b1, vec, outp, gnp, *pieces, *hop_ins)
    return got[:7], hop_results(hops, got[7:])


def norm_back(v, g, gain):
    center = v - jnp.mean(v, axis=-1, keepdims=True)
    rs = lax.rsqrt(jnp.mean(center * center, axis=-1, keepdims=True) + epsilon)
    n = center * rs
    e = g * gain
    grad = rs * (e - jnp.mean(e, axis=-1, keepdims=True) - n * jnp.mean(e * n, axis=-1, keepdims=True))
    return grad, g * n


def branch_kernel(cot_ref, gn_ref, mid_ref, vec_ref, att_ref, attt_ref, w_ref, gm_ref, ga_ref, sums_ref, del_ref,
                  ka_ref, sa_ref, kb_ref, sb_ref, gb, mine, theirs, came, sem, w, load_sem):
    tokens, width = cot_ref.shape
    load = pltpu.make_async_copy(w_ref.at[3], w, load_sem)
    load.start()
    sums_ref[...] = jnp.zeros(sums_ref.shape, f32)

    def body(rows):
        cot = cot_ref[rows, :].astype(f32)
        g = gn_ref[rows, :]
        grad, gain_part = norm_back(mid_ref[rows, :], g, vec_ref[5:6, 0:width])
        gm = cot + grad
        gm_ref[rows, :] = gm
        low = gm.astype(bf16)
        gb[rows, :] = low
        sums_ref[0:1, :] += jnp.sum(gain_part, axis=0, keepdims=True)
        sums_ref[1:2, :] += jnp.sum(g, axis=0, keepdims=True)
        sums_ref[2:3, :] += jnp.sum(low.astype(f32), axis=0, keepdims=True)
        sums_ref[3:4, :] += jnp.sum(cot, axis=0, keepdims=True)

    row_loop(tokens, body)
    half, part = width // 2, mine.shape[-1]
    exchanges = [to_sibling(theirs.at[i], came.at[i], sem, i) for i in range(2)]
    for i in range(2):
        at = i * (width - part)
        g = nn(attt_ref[...], gb[:, at : at + part]).astype(bf16)
        mine[i], theirs[i] = g[:half], g[half:]
        exchanges[i].start()
    load.wait()
    column = lax.broadcasted_iota(jnp.int32, (HEADS, 128), 1)
    first = lax.broadcasted_iota(jnp.int32, (HEADS, 128), 0) * HD
    del_ref[...] = jnp.zeros(del_ref.shape, f32)

    @pl.loop(0, width // 128)
    def _(j):
        cols = pl.ds(pl.multiple_of(j * 128, 128), 128)
        ga = nt(gb[...], w[cols, :]).astype(bf16)
        ga_ref[:, cols] = ga
        prod = ga.astype(f32) * att_ref[:, cols].astype(f32)
        high = prod.astype(bf16)
        rest_low = (prod - high.astype(f32)).astype(bf16)
        at = column + j * 128
        chosen = jnp.where((at >= first) & (at < first + HD), 1.0, 0.0).astype(bf16)
        del_ref[...] += nt(chosen, high) + nt(chosen, rest_low)

    for i, keep, send in ((0, ka_ref, sa_ref), (1, kb_ref, sb_ref)):
        exchanges[i].wait()
        store_blocks(i, (mine[i].astype(f32) + came[i].astype(f32)).astype(bf16), width // 8, keep, send, slice(None))


def qkv_grad_kernel(nt_ref, dq_ref, dko_ref, dkr_ref, all_ref, ka_ref, sa_ref, kb_ref, sb_ref, mine, theirs, came, sem):
    tokens, width = dq_ref.shape
    half, part = nt_ref.shape[0] // 2, mine.shape[-1]

    def join(rows):
        all_ref[rows, 0:width] = dq_ref[rows, :]
        all_ref[rows, width : 3 * width] = (dko_ref[rows, :] + dkr_ref[rows, :].astype(f32)).astype(bf16)

    row_loop(tokens, join)
    exchanges = [to_sibling(theirs.at[i], came.at[i], sem, i) for i in range(2)]
    for i in range(2):

        @pl.loop(0, part // 256)
        def _(t):
            cols = pl.ds(pl.multiple_of(t * 256, 256), 256)
            at = pl.ds(pl.multiple_of(t * 256 + i * (3 * width - part), 128), 256)
            g = nn(nt_ref[...], all_ref[:, at]).astype(bf16)
            mine[i, :, cols], theirs[i, :, cols] = g[:half], g[half:]

        exchanges[i].start()

    for i, keep, send in ((0, ka_ref, sa_ref), (1, kb_ref, sb_ref)):
        exchanges[i].wait()

        @pl.loop(0, part // 256)
        def _(t):
            cols = pl.ds(pl.multiple_of(t * 256, 256), 256)
            total = (mine[i, :, cols].astype(f32) + came[i, :, cols].astype(f32)).astype(bf16)
            store_blocks(i, total, half // 4, keep, send, cols)


def normed_grad_kernel(g1_ref, g2_ref, w_ref, gn_ref, sums_ref, w, sem):
    tokens, width = gn_ref.shape
    a, b = g1_ref.shape[1] // 3, g2_ref.shape[1] // 3
    copies = [pltpu.make_async_copy(w_ref.at[2], w.at[0], sem.at[0]), pltpu.make_async_copy(w_ref.at[pl.ds(0, 2)], w.at[pl.ds(1, 2)], sem.at[1])]
    start_all(copies)
    sums_ref[...] = jnp.zeros(sums_ref.shape, f32)

    def body(rows):
        for i, j in ((0, 0), (1, 2)):
            sums_ref[i : i + 1, 0:a] += jnp.sum(g1_ref[rows, j * a : (j + 1) * a].astype(f32), axis=0, keepdims=True)
            sums_ref[i : i + 1, a:width] += jnp.sum(g2_ref[rows, j * b : (j + 1) * b].astype(f32), axis=0, keepdims=True)

    row_loop(tokens, body)
    for c in copies:
        c.wait()

    def columns(cols):
        total = None
        for i in range(3):
            for g, lo, hi in ((g1_ref, 0, a), (g2_ref, a, width)):
                term = nt(g[:, i * (hi - lo) : (i + 1) * (hi - lo)], w[i, cols, lo:hi])
                total = term if total is None else total + term
        gn_ref[:, cols] = total

    column_tiles(width, columns)


def input_grad_kernel(gn_ref, x_ref, gm_ref, vec_ref, gx_ref, sums_ref):
    tokens, width = x_ref.shape
    sums_ref[...] = jnp.zeros(sums_ref.shape, f32)

    def body(rows):
        g = gn_ref[rows, :]
        grad, gain_part = norm_back(x_ref[rows, :].astype(f32), g, vec_ref[0:1, 0:width])
        gx_ref[rows, :] = (gm_ref[rows, :] + grad).astype(bf16)
        sums_ref[0:1, :] += jnp.sum(gain_part, axis=0, keepdims=True)
        sums_ref[1:2, :] += jnp.sum(g, axis=0, keepdims=True)

    row_loop(tokens, body)


def carrying(body, counts, hops, relations, *refs):
    refs, parts = list(refs), []
    for n in counts:
        parts.append([refs.pop(0) for _ in range(n)])
    ins, hop_ins, outs, hop_outs, scratch, hop_scratch = parts
    carried = list(zip(hops, hop_refs(hops, hop_ins, hop_outs, hop_scratch)))
    greet(relations)
    for h, r in carried:
        h.start(*r)
    body(*ins, *outs, *scratch)
    for h, r in carried:
        h.finish(*r)


def call(body, name, outs, scratch, flops, moved, *args, pieces=(), far_outs=0, hops=(), relations=(), collective=0):
    hop_ins, hop_outs, hop_scratch, hop_relations = hop_parts(hops)
    relations = hop_relations | set(relations)
    counts = (len(args) + len(pieces), len(hop_ins), len(outs), len(hop_outs), len(scratch), len(hop_scratch))
    got = pl.pallas_call(
        functools.partial(carrying, body, counts, hops, relations),
        out_shape=tuple(sds(s, t) for s, t in outs) + tuple(hop_outs),
        in_specs=[VM] * len(args) + [ANY] * (len(pieces) + len(hop_ins)),
        out_specs=(VM,) * (len(outs) - far_outs) + (ANY,) * (far_outs + len(hop_outs)),
        scratch_shapes=list(scratch) + hop_scratch,
        compiler_params=pltpu.CompilerParams(**({"collective_id": collective, "has_side_effects": True} if relations else {})),
        cost_estimate=pl.CostEstimate(flops=flops, bytes_accessed=moved, transcendentals=0),
        name=name,
    )(*args, *pieces, *hop_ins)
    return got[: len(outs)], hop_results(hops, got[len(outs) :])


def swap(v, mask, size):
    return lax.ppermute(v, "dp", [(i, i ^ mask) for i in range(size)])


def after(v, *others):
    return lax.optimization_barrier((v, *others))[0]


class Order:
    def __init__(self):
        self.tail, self.count = None, 0

    def gate(self, v):
        return v if self.tail is None else after(v, self.tail)

    def call(self, body, name, outs, scratch, flops, moved, *args, **named):
        self.count += 1
        if args:
            args = (self.gate(args[0]), *args[1:])
        got, carried = call(body, name, outs, scratch, flops, moved, *args, collective=self.count, **named)
        self.tail = got[0]
        return (*got, *carried)

    def mlp(self, name, first, last, n2, *args, **named):
        self.count += 1
        got, carried = mlp_call(name, first, last, self.gate(n2), *args, collective=self.count, **named)
        self.tail = got[2]
        return (*got, *carried)


def small_kernel(rows_ref, out_ref, held, came, core_sem, x_sem, y_sem, z_sem):
    d, z = here()
    for i, m in enumerate(ORDER_SMALL):
        held[i] = rows_ref[flipped_index(d, m)]
    for sem, mask, count in ((core_sem, 1, 4), (x_sem, 2, 2), (y_sem, 4, 1)):
        hop = remote(held.at[pl.ds(count, count)], came.at[pl.ds(count, count)], sem, across_links(mask))
        hop.start()
        hop.wait()
        held[0:count] = held[0:count] + came[count : 2 * count]
    sends, receives, partner = seq_step(INWARD)
    hop = remote(held.at[0], came.at[0], z_sem, partner)

    @pl.when(sends)
    def _():
        hop.start()
        hop.wait_send()

    out_ref[...] = held[0].astype(bf16)

    @pl.when(receives)
    def _():
        hop.wait_recv()
        out_ref[...] = (held[0] + came[0]).astype(bf16)


def nothing_kernel(first_ref, out_ref):
    out_ref[...] = jnp.zeros(out_ref.shape, f32)


def by_rows(size, depth):
    def step(patches, picture_ids, valid_mask, ln1_gain, ln1_bias, w_qkv, bias_qv, w_out, b_out, ln2_gain, ln2_bias,
             w_fc1, b_fc1, w_fc2, b_fc2, cotangent):
        width = patches.shape[-1]
        ff = w_fc1.shape[1]
        tokens = patches.shape[0] * patches.shape[1]
        part = width // size
        z, core = lax.axis_index("seq"), lax.axis_index("dp") % 2
        order = Order()
        vm = pltpu.VMEM
        act, flip = ((tokens, width), bf16), ((width, tokens), bf16)
        act32 = ((tokens, width), f32)
        mm = 2 * tokens * width * width

        small = jnp.stack([ln1_gain, ln1_bias, bias_qv[0], bias_qv[1], b_out, ln2_gain, ln2_bias, b_fc2])
        small = jnp.pad(small, ((0, 8), (0, width - part)))
        small = jnp.stack([small, jnp.pad(b_fc1[None], ((0, 15), (0, width - ff // size)))])[None]
        unit0 = jnp.stack([w_qkv[:, width : 2 * width], w_qkv[:, 2 * width :]])
        unit1 = jnp.stack([w_qkv[:, :width], w_out])
        extra = -ff % 256
        tiles = (ff + extra) // 256
        ends = [0, tiles // 2 * 256, (tiles - tiles // 5) * 256, tiles * 256]
        w1 = jnp.pad(w_fc1, ((0, 0), (0, extra)))
        w2 = jnp.pad(w_fc2.T, ((0, 0), (0, extra)))
        hidden_units = [jnp.stack([w1[:, a:b], w2[:, a:b]]) for a, b in zip(ends, ends[1:])]

        ids = jnp.stack([picture_ids, jnp.where(valid_mask == 1, picture_ids, -1)])
        far_ids = swap(ids, 1, size)
        ids = jnp.where(z // 2 == core, ids, far_ids)
        ids = jnp.where(z % 2 == 1, ids[:, 1], ids[:, 0]).reshape(2, 2, tokens)
        near = jnp.where(core == 1, ids[:, 1], ids[:, 0])
        far = jnp.where(core == 1, ids[:, 0], ids[:, 1])
        keys = jnp.concatenate([near[1], far[1]])
        qid_row, qid_col = jnp.broadcast_to(near[0][None], (8, tokens)), jnp.broadcast_to(near[0][:, None], (tokens, 128))
        kid_row, kid_col = jnp.broadcast_to(keys[None], (8, 2 * tokens)), jnp.broadcast_to(keys[:, None], (2 * tokens, 128))

        dma = pltpu.SemaphoreType.DMA
        half_rows = (2, tokens // 2, width)
        x, nt_, q, kv, vec, b1, far_kv, w_all = order.call(
            functools.partial(entry_kernel, ff), "entry",
            [act, flip, act, ((tokens, 2 * width), bf16), ((16, width), f32), ((16, ff + extra), f32),
             ((tokens, 2 * width), bf16), ((4, width, width), bf16)],
            [vm((4, width, width), bf16), vm((8, 2, 16, width), bf16), vm(half_rows, bf16), vm((tokens, width), bf16),
             vm((width, tokens), bf16), dma((2, 7, 2, 2)), dma((7, 1, 2)), dma((3, 2)), dma((2, 2)), dma, dma((2, 2)), dma((2,))],
            3 * mm, 8 * width * width, pieces=(unit0, small, unit1, patches), relations=(1, 2, 4, "rows"), far_outs=2)
        unit2, unit3, unit4 = hidden_units
        sc = 2 * tokens * 2 * tokens * WIN * HEADS
        att, lse, (x2, y2), cot = order.call(
            attention_forward_kernel, "attention_forward", [act, ((HEADS, tokens), f32)],
            [vm((tokens, 2 * tokens), f32), vm((tokens, width), f32), vm((tokens, 128), f32)],
            3 * sc, 8 * tokens * width, q, kv, far_kv, qid_col, kid_row, hops=(Straight(unit2), Rows(cotangent)))
        cot = cot.reshape(tokens, width)
        mid, n2, n2t, cott, attt, (da2, db2) = order.call(
            middle_kernel, "middle", [act32, act, flip, flip, flip],
            [vm((width, tokens), bf16), vm((width, width), bf16), dma], mm, 2 * width * width, att, x, cot, vec,
            pieces=(w_all,), hops=(Corner(x2, y2),))

        args = (cot, n2t, cott)
        acc, gn, *grads1, gb1, chain = order.mlp(
            "mlp0", True, False, n2, *args, b1, vec, mid, mid, (unit2, x2, y2, da2, db2), 0, hops=(Chain(unit3, unit4),))
        x3, y3, da3, db3, x4, y4 = chain
        acc, gn, *grads2, gb2, (da4, db4), p1 = order.mlp(
            "mlp1", False, False, n2, *args, b1, vec, acc, gn, (unit3, x3, y3, da3, db3), ends[1],
            hops=(Corner(x4, y4), First(*grads1)))
        out, gn, *grads3, gb3, own1 = order.mlp(
            "mlp2", False, True, n2, *args, b1, vec, acc, gn, (unit4, x4, y4, da4, db4), ends[2], hops=(Second(p1),))

        part_o = (width // 256 + 1) * 128

        def gradient(columns):
            return [((2, part, columns), bf16)] * 4

        def exchanged(columns):
            return [vm((2, width // 2, columns), bf16)] * 3 + [dma((3, 2))]

        gm, ga, sums2, inner, *gradso, p2, layer_out = order.call(
            branch_kernel, "branch", [act32, act, ((8, width), f32), ((HEADS, tokens), f32), *gradient(part_o)],
            [vm((tokens, width), bf16), *exchanged(part_o), vm((width, width), bf16), dma], 2 * mm, 4 * width * width,
            cot, gn, mid, vec, att, attt, pieces=(w_all,), relations=(1,),
            hops=(First(*grads2), Rows(out.reshape(half_rows))))
        cut_head = (HEADS + 2) // 2
        cut_col = cut_head * HD // 128 * 128

        def attention_backward(name, h0, h1, base, done, span, carry, hops):
            share = 3 * sc * (h1 - h0) // HEADS * 2
            return order.call(
                functools.partial(attention_backward_kernel, h0, h1, base, done), name,
                [((tokens, done), bf16), ((tokens, 2 * done), f32), ((5, tokens if span > done else 8, 128), f32),
                 ((tokens, 2 * done), bf16)],
                [vm((2 * tokens, tokens), f32), vm((5, tokens, span), f32), vm((tokens, 2 * done), bf16), dma((2,))],
                share, 16 * tokens * width, q, kv, far_kv, ga, lse, inner, kid_col, qid_row, carry,
                relations=(1,), far_outs=1, hops=hops)

        def qkv_grad(name, dq, dkn, dkr, hops):
            columns = 3 * dq.shape[1]
            share = (columns + 511) // 512 * 256
            got, *rest = order.call(
                qkv_grad_kernel, name, [((tokens, columns), bf16), *gradient(share)], exchanged(share),
                mm * columns // width, 4 * width * columns, nt_, dq, dkn, dkr, relations=(1,), hops=hops)
            return got, rest[:4], *rest[4:]

        dqa, dna, carry, dra, own2, p3, in1 = attention_backward(
            "attention_backward_a", 0, cut_head, 0, cut_col, cut_col + 128, inner, (Second(p2), First(*grads3), Seq(INWARD, own1)))
        gra, gradsa, own3, po, mid1a, in2a = qkv_grad(
            "qkv_grad_a", dqa, dna, dra, (Second(p3), First(*gradso), Seq(MIDDLE, in1, 0), Seq(INWARD, own2, 0)))
        dqb, dnb, _, drb, owno, pa, mid1b, in2b, in3 = attention_backward(
            "attention_backward_b", cut_head, HEADS, cut_col, width - cut_col, width - cut_col, carry,
            (Second(po), First(*gradsa), Seq(MIDDLE, in1, 1), Seq(INWARD, own2, 1), Seq(INWARD, own3)))
        grb, gradsb, owna, mid2a, out1a, ino = qkv_grad(
            "qkv_grad_b", dqb, dnb, drb, (Second(pa), Seq(MIDDLE, in2a), Seq(OUTWARD, mid1a), Seq(INWARD, owno)))
        gnq, sums0, pb, mid2b, out1b, ina = order.call(
            normed_grad_kernel, "normed_grad", [act32, ((8, width), f32)],
            [vm((3, width, width), bf16), dma((2,))], 3 * mm, 6 * width * width, gra, grb, pieces=(w_all,),
            hops=(First(*gradsb), Seq(MIDDLE, in2b), Seq(OUTWARD, mid1b), Seq(INWARD, owna)))
        gx, sums1, ownb, mid3, out2a = order.call(
            input_grad_kernel, "input_grad", [act, ((8, width), f32)], [], 10**7, 12 * tokens * width, gnq, x, gm, vec,
            hops=(Second(pb), Seq(MIDDLE, in3), Seq(OUTWARD, mid2a)))

        bias_grads = jnp.concatenate([gb1, gb2, gb3], axis=1)[:, :ff].reshape(size, ff // size)
        vecs = jnp.concatenate([sums1[:2], sums0[:2], sums2[:4]]).reshape(8, size, part)
        rows = jnp.concatenate([jnp.moveaxis(vecs, 0, 1).reshape(size, 8 * part), bias_grads], axis=1)
        lanes = rows.shape[1]
        rows = jnp.pad(rows, ((0, 0), (0, -lanes % 2048))).reshape(size, -1, 128)
        few = rows.shape[1:]
        tiny, grad_patches, inb, mido, mida, out2b, out3 = order.call(
            small_kernel, "small", [(few, bf16)], [vm((8, *few), f32), vm((8, *few), f32)] + [dma((2,))] * 4, 10**6, 10**6, rows,
            relations=(1, 2, 4, "z"),
            hops=(Rows(gx.reshape(half_rows)), Seq(INWARD, ownb), Seq(MIDDLE, ino), Seq(MIDDLE, ina), Seq(OUTWARD, mid2b), Seq(OUTWARD, mid3)))
        _, tiny, midb, outo, outa = order.call(
            nothing_kernel, "middle_sums", [((8, 128), f32)], [], 10**6, 10**6, tiny,
            hops=(Seq(MIDDLE, tiny), Seq(MIDDLE, inb), Seq(OUTWARD, mido), Seq(OUTWARD, mida)))
        _, tiny, outb = order.call(
            nothing_kernel, "outer_sums", [((8, 128), f32)], [], 10**6, 10**6, _, hops=(Seq(OUTWARD, tiny), Seq(OUTWARD, midb)))
        tiny = tiny.reshape(-1)[:lanes].astype(f32)
        mine, grad_b_fc1 = tiny[: 8 * part].reshape(8, part), tiny[8 * part :]
        left = ff - ends[2]
        w1g = jnp.concatenate([out1a, out2a, out3[0][:, :left]], axis=1).astype(f32)
        w2g = jnp.concatenate([out1b, out2b, out3[1][:, :left]], axis=1).T.astype(f32)
        wog = jnp.concatenate([outo[0], outo[1][:, 2 * part_o - width :]], axis=1).astype(f32)

        def joined(g, columns):
            return jnp.concatenate([g[0], g[1][:, 2 * g.shape[2] - columns :]], axis=1).reshape(part, 3, columns // 3)

        wqg = jnp.concatenate([joined(outa, 3 * cut_col), joined(outb, 3 * (width - cut_col))], axis=2)
        wqg = wqg.reshape(part, 3 * width).astype(f32)
        return (layer_out, grad_patches, mine[0], mine[1], wqg, mine[2:4], wog, mine[6], mine[4], mine[5], w1g, grad_b_fc1, w2g, mine[7])

    return step


def fits_rows(mesh, patches):
    return mesh.shape["dp"] == 8 and mesh.shape["seq"] == 4


def solution(mesh):
    placed = (
        P("dp", "seq", None),
        P("dp", None),
        P("dp", None),
        P("dp"),
        P("dp"),
        P("dp", None),
        P(None, "dp"),
        P("dp", None),
        P("dp"),
        P("dp"),
        P("dp"),
        P("dp", None),
        P("dp"),
        P(None, "dp"),
        P("dp"),
        P("dp", "seq", None),
    )
    return jax.shard_map(
        by_rows(mesh.shape["dp"], mesh.shape["seq"]) if fits_rows(mesh, None) else per_device,
        mesh=mesh,
        in_specs=placed,
        out_specs=(
            P("dp", "seq", None),
            P("dp", "seq", None),
            P("dp"),
            P("dp"),
            P("dp", None),
            P(None, "dp"),
            P("dp", None),
            P("dp"),
            P("dp"),
            P("dp"),
            P("dp", None),
            P("dp"),
            P(None, "dp"),
            P("dp"),
        ),
        check_vma=False,
    )
```
